32 devices in a mesh: ctx: 8 (over z, x), head: 4 (over y, core).
Axes of the slice: x: 2, y: 2, z: 4, core: 2. Of those that a mesh axis runs over, the one named last changes fastest.
Arguments:
- keys: bfloat16 [16384, 5120], P('ctx', 'head'), may hold values from -6 to 6
- values: bfloat16 [16384, 5120], P('ctx', 'head'), may hold values from -6 to 6
- queries: bfloat16 [16384, 5120], P('ctx', 'head'), may hold values from -6 to 6
- rates: float32 [16384, 16], P('ctx', 'head'), may hold values from 9.765625e-05 to 0.0009765625
- w_gate: bfloat16 [320, 16, 320], P('ctx', 'head'), may hold values from -0.3125 to 0.3125
- w_up: bfloat16 [320, 16, 320], P('ctx', 'head'), may hold values from -0.3125 to 0.3125
- w_down: bfloat16 [320, 16, 320], P('ctx', 'head'), may hold values from -0.3125 to 0.3125
- gain: float32 [5120], P('head'), may hold values from 0.5 to 1.5
Outputs:
- output: bfloat16 [16384, 5120], P('ctx', 'head')
- new_gate: bfloat16 [320, 16, 320], P('ctx', 'head')
- new_up: bfloat16 [320, 16, 320], P('ctx', 'head')
- new_down: bfloat16 [320, 16, 320], P('ctx', 'head')
The draws below stay inside these ranges and needn't reach their ends.
All inputs are finite; a program needn't handle non-finite values.
Results may differ from the reference program's by a relative error of at most 0.0092.
Values may be sent and summed in bfloat16 or wider, within the bound.
A program may use at most 128 MiB of HBM per device.

```python
import math
import jax
import jax.numpy as jnp
from jax import lax

HEADS = 16
DH = 320
FF = 320
TOKENS = 16384
WIDTH = 5120


def block_scale(own_key, extent, split, smallest, high):
    level, own = 1.0, jax.random.fold_in(own_key, 6)
    for position, parts in split:
        heights = jnp.exp(jax.random.uniform(jax.random.fold_in(own, position), (parts,), jnp.float32, smallest / len(split), high / len(split)))
        level = level * jnp.repeat(heights, extent[position] // parts).reshape([-1 if axis == position else 1 for axis in range(len(extent))])
    return level


def bell_draw(own_key, shape, spread, most, pieces=(), dtype=jnp.bfloat16):
    drawn = spread * jax.random.normal(own_key, shape, jnp.float32)
    if pieces:
        drawn = drawn * block_scale(own_key, shape, pieces, -0.22, 0.18)
    return jnp.clip(drawn, -most, most).astype(dtype)


def setup_inputs(seed: int = 0) -> dict:
    arg_keys = jax.random.split(jax.random.key(seed), 9)
    return {
        "keys": bell_draw(arg_keys[0], (TOKENS, WIDTH), 1.0, 6.0, ((0, 8), (1, 4))),
        "values": bell_draw(arg_keys[1], (TOKENS, WIDTH), 1.0, 6.0, ((0, 8), (1, 4))),
        "queries": bell_draw(arg_keys[2], (TOKENS, WIDTH), 1.0, 6.0, ((0, 8), (1, 4))),
        "rates": jnp.clip(jnp.exp(math.log(0.0009765625) - 2.3025851 * jax.random.uniform(arg_keys[3], (TOKENS, HEADS), jnp.float32) ** block_scale(arg_keys[3], (TOKENS, HEADS), ((0, 8), (1, 4)), -0.2, 0.2)), 9.765625145519152e-05, 0.0009765625),
        "w_gate": bell_draw(arg_keys[4], (FF, HEADS, DH), DH ** -0.5, 0.3125, ((0, 8), (1, 4))),
        "w_up": bell_draw(arg_keys[5], (FF, HEADS, DH), DH ** -0.5, 0.3125, ((0, 8), (1, 4))),
        "w_down": bell_draw(arg_keys[6], (FF, HEADS, DH), FF ** -0.5, 0.3125, ((0, 8), (1, 4))),
        "gain": jnp.clip(1.0 + 0.1 * jax.random.normal(arg_keys[7], (WIDTH,), jnp.float32), 0.5, 1.5),
    }


EPS = 1e-06

def renorm(weight, grad):
    old = weight.astype(jnp.float32)
    updated = old + grad
    old_sq = lax.optimization_barrier(jnp.sum(old * old, axis=0))
    new_sq = lax.optimization_barrier(jnp.sum(updated * updated, axis=0))
    return (updated * (jnp.sqrt(old_sq) * lax.rsqrt(new_sq + EPS))[None, :]).astype(jnp.bfloat16)

def update_head(operands):
    keyh, valueh, rateh, wgate, wup, wdown = operands
    gpre = jnp.dot(keyh, wgate.T, preferred_element_type=jnp.float32)
    upre = jnp.dot(keyh, wup.T, preferred_element_type=jnp.float32)
    sig = jax.nn.sigmoid(gpre)
    act = gpre * sig
    slope = sig * (1.0 + gpre * (1.0 - sig))
    hidden = (act * upre).astype(jnp.bfloat16)
    scaled = (valueh.astype(jnp.float32) * rateh[:, None]).astype(jnp.bfloat16)
    back = jnp.dot(scaled, wdown.T, preferred_element_type=jnp.float32)
    dgate = (back * upre * slope).astype(jnp.bfloat16)
    dup = (back * act).astype(jnp.bfloat16)
    grad_gate = jnp.dot(dgate.T, keyh, preferred_element_type=jnp.float32)
    grad_up = jnp.dot(dup.T, keyh, preferred_element_type=jnp.float32)
    grad_down = jnp.dot(hidden.T, scaled, preferred_element_type=jnp.float32)
    return (renorm(wgate, grad_gate), renorm(wup, grad_up), renorm(wdown, grad_down))

def apply_head(queryh, wgate, wup, wdown):
    gpre = jnp.dot(queryh, wgate.T, preferred_element_type=jnp.float32)
    upre = jnp.dot(queryh, wup.T, preferred_element_type=jnp.float32)
    mixed = (jax.nn.silu(gpre) * upre).astype(jnp.bfloat16)
    return jnp.dot(mixed, wdown, preferred_element_type=jnp.float32)

def reference(keys, values, queries, rates, w_gate, w_up, w_down, gain):
    rows = keys.shape[0]
    keyh = keys.reshape(rows, HEADS, DH).transpose(1, 0, 2)
    valueh = values.reshape(rows, HEADS, DH).transpose(1, 0, 2)
    queryh = queries.reshape(rows, HEADS, DH).transpose(1, 0, 2)
    rateh = rates.T
    new_gate, new_up, new_down = lax.map(update_head, (keyh, valueh, rateh, w_gate.transpose(1, 0, 2), w_up.transpose(1, 0, 2), w_down.transpose(1, 0, 2)))

    def head_squares(operands):
        outh = apply_head(*operands)
        return lax.optimization_barrier(jnp.sum(outh * outh, axis=1))
    squares = lax.optimization_barrier(jnp.sum(lax.map(head_squares, (queryh, new_gate, new_up, new_down)), axis=0))
    scale = lax.rsqrt(squares / (HEADS * DH) + EPS)
    gainh = gain.reshape(HEADS, DH)

    def head_output(operands):
        queryone, wgate, wup, wdown, gainone = operands
        outh = apply_head(queryone, wgate, wup, wdown)
        return (outh * scale[:, None] * gainone[None, :]).astype(jnp.bfloat16)
    output = lax.map(head_output, (queryh, new_gate, new_up, new_down, gainh))
    output = output.transpose(1, 0, 2).reshape(rows, HEADS * DH)
    return (output, new_gate.transpose(1, 0, 2), new_up.transpose(1, 0, 2), new_down.transpose(1, 0, 2))
```

```python
import functools
import math

import jax
import jax.numpy as jnp
from jax import lax
from jax.experimental import pallas as pl
from jax.experimental.pallas import tpu as pltpu
from jax.sharding import PartitionSpec as P

EPS = 1e-06


def inner_size(n):
    inner = 1
    while inner * inner * 4 <= n and n % (inner * 2) == 0:
        inner *= 2
    return inner if inner > 1 or n % 2 else 2


def place(n, inner):
    me = lax.axis_index("ctx")
    return me, me // inner, lax.rem(me, inner), n // inner


def greet(z, x, outer, inner):
    barrier = pltpu.get_barrier_semaphore()
    for s in range(1, outer):
        pl.semaphore_signal(barrier, inc=1, device_id={"ctx": lax.rem(z + s, outer) * inner + x})
    for t in range(1, inner):
        pl.semaphore_signal(barrier, inc=1, device_id={"ctx": z * inner + lax.rem(x + t, inner)})
    pl.semaphore_wait(barrier, outer + inner - 2)


def spread(z, x, outer, inner, own_ref, out_ref, send_sem, recv_sem):
    me = z * inner + x
    copies = {}

    def send(src, block, device, s, t):
        copy = pltpu.make_async_remote_copy(
            src_ref=src,
            dst_ref=out_ref.at[block],
            send_sem=send_sem.at[s, t],
            recv_sem=recv_sem.at[s, t],
            device_id={"ctx": device},
        )
        copy.start()
        copies[s, t] = copy

    for s in range(1, outer):
        send(own_ref, me, lax.rem(z + s, outer) * inner + x, s, 0)
    for t in range(1, inner):
        send(own_ref, me, z * inner + lax.rem(x + t, inner), 0, t)
    for s in range(1, outer):
        copies[s, 0].wait_recv()
        block = lax.rem(z + outer - s, outer) * inner + x
        for t in range(1, inner):
            send(out_ref.at[block], block, z * inner + lax.rem(x + t, inner), s, t)
    for (s, t), copy in copies.items():
        if t:
            copy.wait_recv()
    for copy in copies.values():
        copy.wait_send()


def gather_kernel(n, inner, own_ref, out_ref, local_sem, send_sem, recv_sem):
    me, z, x, outer = place(n, inner)
    greet(z, x, outer, inner)
    keep = pltpu.make_async_copy(own_ref, out_ref.at[me], local_sem)
    keep.start()
    spread(z, x, outer, inner, own_ref, out_ref, send_sem, recv_sem)
    keep.wait()


def update_kernel(
    n, inner, grad_ref, old_ref, out_ref, near, part, far, fresh,
    local_sem, near_send, near_recv, far_send, far_recv, send_sem, recv_sem,
):
    me, z, x, outer = place(n, inner)
    greet(z, x, outer, inner)
    order = list(range(1, outer)) + [0]
    first = {}
    for s in order:
        row = lax.rem(z + s, outer) * inner
        for t in range(1, inner):
            column = lax.rem(x + t, inner)
            copy = pltpu.make_async_remote_copy(
                src_ref=grad_ref.at[row + column],
                dst_ref=near.at[s, t - 1],
                send_sem=near_send.at[s, t],
                recv_sem=near_recv.at[s, t],
                device_id={"ctx": z * inner + column},
            )
            copy.start()
            first[s, t] = copy
    second = {}
    total = None
    for s in order:
        row = lax.rem(z + s, outer) * inner
        total = grad_ref[row + x].astype(jnp.float32)
        for t in range(1, inner):
            first[s, t].wait_recv()
            total = total + near[s, t - 1].astype(jnp.float32)
        if s:
            part[s] = total.astype(part.dtype)
            copy = pltpu.make_async_remote_copy(
                src_ref=part.at[s],
                dst_ref=far.at[s],
                send_sem=far_send.at[s],
                recv_sem=far_recv.at[s],
                device_id={"ctx": row + x},
            )
            copy.start()
            second[s] = copy
    for s, copy in second.items():
        copy.wait_recv()
        total = total + far[s].astype(jnp.float32)
    old = old_ref[...].astype(jnp.float32)
    updated = old + total
    old_sq = jnp.sum(old * old, axis=1, keepdims=True)
    new_sq = jnp.sum(updated * updated, axis=1, keepdims=True)
    fresh[...] = (updated * (jnp.sqrt(old_sq) * lax.rsqrt(new_sq + EPS))).astype(fresh.dtype)
    keep = pltpu.make_async_copy(fresh, out_ref.at[me], local_sem)
    keep.start()
    keep.wait()
    spread(z, x, outer, inner, out_ref.at[me], out_ref, send_sem, recv_sem)
    for copy in first.values():
        copy.wait_send()
    for copy in second.values():
        copy.wait_send()


def vmem(count):
    return [pl.BlockSpec(memory_space=pltpu.VMEM)] * count


def gather(own, n):
    inner = inner_size(n)
    outer = n // inner
    return pl.pallas_call(
        functools.partial(gather_kernel, n, inner),
        out_shape=jax.ShapeDtypeStruct((n,) + own.shape, own.dtype),
        in_specs=vmem(1),
        out_specs=vmem(1)[0],
        scratch_shapes=[pltpu.SemaphoreType.DMA]
        + [pltpu.SemaphoreType.DMA((outer, inner))] * 2,
        compiler_params=pltpu.CompilerParams(collective_id=0, has_side_effects=True),
        name="gather_weights",
    )(own)


def update(grads, old, n):
    inner = inner_size(n)
    outer = n // inner
    block = grads.shape[1:]
    return pl.pallas_call(
        functools.partial(update_kernel, n, inner),
        out_shape=jax.ShapeDtypeStruct(grads.shape, grads.dtype),
        in_specs=vmem(2),
        out_specs=vmem(1)[0],
        scratch_shapes=[
            pltpu.VMEM((outer, max(inner - 1, 1)) + block, grads.dtype),
            pltpu.VMEM((outer,) + block, grads.dtype),
            pltpu.VMEM((outer,) + block, grads.dtype),
            pltpu.VMEM(block, grads.dtype),
            pltpu.SemaphoreType.DMA,
        ]
        + [pltpu.SemaphoreType.DMA((outer, inner))] * 2
        + [pltpu.SemaphoreType.DMA((outer,))] * 2
        + [pltpu.SemaphoreType.DMA((outer, inner))] * 2,
        compiler_params=pltpu.CompilerParams(collective_id=1, has_side_effects=True),
        name="update_weights",
    )(grads, old)


def dot(a, b, left, right):
    return lax.dot_general(a, b, (((left,), (right,)), ((), ())), preferred_element_type=jnp.float32)


def grads_kernel(key_ref, value_ref, rate_ref, weight_ref, out_ref, acc):
    step = pl.program_id(0)

    @pl.when(step == 0)
    def _():
        acc[...] = jnp.zeros_like(acc)

    heads, width = weight_ref.shape[1:3]
    for h in range(heads):
        columns = slice(h * width, (h + 1) * width)
        key = key_ref[:, columns]
        gpre = dot(key, weight_ref[0, h], 1, 0)
        upre = dot(key, weight_ref[1, h], 1, 0)
        scaled = (value_ref[:, columns].astype(jnp.float32) * rate_ref[:, h : h + 1]).astype(jnp.bfloat16)
        back = dot(scaled, weight_ref[2, h], 1, 0)
        sig = jax.nn.sigmoid(gpre)
        act = gpre * sig
        slope = sig * (1.0 + gpre * (1.0 - sig))
        acc[0, h] += dot(key, (back * upre * slope).astype(jnp.bfloat16), 0, 0)
        acc[1, h] += dot(key, (back * act).astype(jnp.bfloat16), 0, 0)
        acc[2, h] += dot(scaled, (act * upre).astype(jnp.bfloat16), 0, 0)

    @pl.when(step == pl.num_programs(0) - 1)
    def _():
        out_ref[...] = acc[...].astype(out_ref.dtype)


def apply_kernel(query_ref, weight_ref, out_ref, square_ref):
    heads, width = weight_ref.shape[1:3]
    squares = None
    for h in range(heads):
        columns = slice(h * width, (h + 1) * width)
        query = query_ref[:, columns]
        gate = dot(query, weight_ref[0, h], 1, 0)
        up = dot(query, weight_ref[1, h], 1, 0)
        mixed = (jax.nn.silu(gate) * up).astype(jnp.bfloat16)
        out = dot(mixed, weight_ref[2, h], 1, 1)
        part = jnp.sum(out * out, axis=1, keepdims=True)
        squares = part if squares is None else squares + part
        out_ref[:, columns] = out.astype(out_ref.dtype)
    square_ref[...] = squares


def tile(rows, width):
    return pl.BlockSpec((rows, width), lambda i: (i, 0))


def fixed(shape):
    return pl.BlockSpec(shape, lambda i: (0,) * len(shape))


def token_grads(keys, values, rates, weights):
    rows, width = keys.shape
    step = math.gcd(rows, 512)
    return pl.pallas_call(
        grads_kernel,
        grid=(rows // step,),
        out_shape=jax.ShapeDtypeStruct(weights.shape, jnp.bfloat16),
        in_specs=[tile(step, width), tile(step, width), tile(step, rates.shape[1]), fixed(weights.shape)],
        out_specs=fixed(weights.shape),
        scratch_shapes=[pltpu.VMEM(weights.shape, jnp.float32)],
        name="token_grads",
    )(keys, values, rates, weights)


def apply(queries, weights):
    rows, width = queries.shape
    step = math.gcd(rows, 512)
    return pl.pallas_call(
        apply_kernel,
        grid=(rows // step,),
        out_shape=(
            jax.ShapeDtypeStruct((rows, width), jnp.bfloat16),
            jax.ShapeDtypeStruct((rows, 1), jnp.float32),
        ),
        in_specs=[tile(step, width), fixed(weights.shape)],
        out_specs=(tile(step, width), tile(step, 1)),
        name="apply_weights",
    )(queries, weights)


def fits(n, rows, units, heads, width):
    inner = inner_size(n)
    return (
        inner == 2
        and n // inner >= 2
        and units % 8 == 0
        and heads % 2 == 0
        and heads <= 8
        and width % 128 == 64
        and rows % 512 == 0
        and rows * heads * width <= 2048 * 1280
    )


class Plan:
    def __init__(self, n, peers, rows, units, heads, width, width_all):
        self.n, self.peers, self.rows, self.units = n, peers, rows, units
        self.heads, self.width, self.width_all = heads, width, width_all
        self.inner = 2
        self.outer = n // 2
        self.step = 512
        self.window = width + 64
        self.packed = 2 * width + self.window
        self.starts = (0, width - 64, 2 * width)
        self.shifts = (0, 64, 0)

    def columns(self, h):
        start = (h // 2) * 2 * self.width + (h % 2) * (self.width - 64)
        return slice(start, start + self.window)

    def move(self, x, old, new):
        size = x.shape[1]
        if old != new:
            x = pltpu.roll(x, (new - old) % size, 1)
        lane = lax.broadcasted_iota(jnp.int32, x.shape, 1)
        return jnp.where((lane >= new) & (lane < new + self.width), x, 0.0)

    def pack(self, gate, up, down):
        first = self.width - 64
        shared = gate[:, first:] + up[:, :128]
        return jnp.concatenate([gate[:, :first], shared, up[:, 128:], down], axis=1)


def fused_kernel(
    plan, key_hbm, value_hbm, query_hbm, rate_ref, gate_ref, up_ref, down_ref, gain_ref,
    out_hbm, fresh_ref,
    keys, values, queries, rate, old, new, own, ups, downs, side, updated, weights, acc,
    squares_old, outs, squares, row, rows_in,
    load_sem, store_sem,
    line_send, line_recv, cross_send, cross_recv,
    part_send, part_recv, side_send, side_recv, row_send, row_recv,
):
    f32, b16 = jnp.float32, jnp.bfloat16
    n, outer, heads, units, width = plan.n, plan.outer, plan.heads, plan.units, plan.width
    window, step, tokens = plan.window, plan.step, plan.rows
    me = lax.axis_index("ctx")
    z, x = me // 2, lax.rem(me, 2)
    mine = lax.axis_index("head")
    other = z * 2 + 1 - x

    loads = []
    half = 2 * width
    for p in range(heads // 2):
        cut = slice(p * half, (p + 1) * half)
        for i, (src, dst) in enumerate(((key_hbm, keys), (value_hbm, values), (query_hbm, queries))):
            copy = pltpu.make_async_copy(src.at[:, cut], dst.at[:, cut], load_sem.at[i, p])
            if i < 2:
                copy.start()
            loads.append((i, p, copy))
    for i, p, copy in loads:
        if i == 2:
            copy.start()

    barrier = pltpu.get_barrier_semaphore()
    pl.semaphore_signal(barrier, inc=1, device_id={"ctx": other})
    for t in range(1, plan.peers):
        pl.semaphore_signal(barrier, inc=1, device_id={"head": lax.rem(mine + t, plan.peers)})

    hops = sorted({1, outer - 1})
    for t in hops:
        pl.semaphore_signal(barrier, inc=1, device_id={"ctx": lax.rem(z + t, outer) * 2 + x})

    for h in range(heads):
        parts = []
        for j, ref in enumerate((gate_ref, up_ref, down_ref)):
            piece = ref[:, h, :].astype(f32)
            piece = jnp.concatenate([piece, jnp.zeros((units, 64), f32)], axis=1)
            parts.append(plan.move(piece, 0, plan.shifts[j]))
        old[h, me] = plan.pack(*parts).astype(b16)

    pl.semaphore_wait(barrier, plan.peers + len(hops))

    sends = []

    def send(when, make):
        def start():
            make().start()

        def finish():
            make().wait_send()

        if when is None:
            start()
            sends.append(finish)
        else:
            pl.when(when)(start)
            sends.append(lambda: pl.when(when)(finish))

    def line_copy(g, h, origin, up):
        buf = (old, new)[g]
        block = origin * 2 + x
        return pltpu.make_async_remote_copy(
            src_ref=buf.at[h, block], dst_ref=buf.at[h, block],
            send_sem=line_send.at[g, h, up, origin], recv_sem=line_recv.at[g, h, origin],
            device_id={"ctx": me + (2 if up else -2)},
        )

    def cross_copy(g, h, origin):
        buf = (old, new)[g]
        block = origin * 2 + x
        return pltpu.make_async_remote_copy(
            src_ref=buf.at[h, block], dst_ref=buf.at[h, block],
            send_sem=cross_send.at[g, h, origin], recv_sem=cross_recv.at[g, h, origin],
            device_id={"ctx": other},
        )

    def issue(g, h):
        send(z < outer - 1, lambda: line_copy(g, h, z, 1))
        send(z > 0, lambda: line_copy(g, h, z, 0))
        send(None, lambda: cross_copy(g, h, z))

    def relay(g, h, d):
        low, high = z - d, z + d

        @pl.when(low >= 0)
        def _():
            line_copy(g, h, low, 1).wait_recv()

        send((low >= 0) & (z < outer - 1), lambda: line_copy(g, h, low, 1))
        send(low >= 0, lambda: cross_copy(g, h, low))

        @pl.when(high < outer)
        def _():
            line_copy(g, h, high, 0).wait_recv()

        send((high < outer) & (z > 0), lambda: line_copy(g, h, high, 0))
        send(high < outer, lambda: cross_copy(g, h, high))

    def arrived(g, h):
        for o in range(outer):
            cross_copy(g, h, o).wait_recv()

    def part_copy(h, up, to):
        buf = (downs, ups)[up]
        return pltpu.make_async_remote_copy(
            src_ref=own.at[h, pl.ds(to * 2, 2)], dst_ref=buf.at[h, to],
            send_sem=part_send.at[h, up, to], recv_sem=part_recv.at[h, up, to],
            device_id={"ctx": me + (2 if up else -2)},
        )

    def add_part(h, up, to):
        buf = (downs, ups)[up]
        part_copy(h, up, to).wait_recv()
        total = own[h, pl.ds(to * 2, 2)].astype(f32) + buf[h, to].astype(f32)
        own[h, pl.ds(to * 2, 2)] = total.astype(b16)

    def reduce_start(h):
        for to in range(outer - 1, 0, -1):
            send(z == 0, functools.partial(part_copy, h, 1, to))
            send(z == outer - 1, functools.partial(part_copy, h, 0, outer - 1 - to))

    def reduce_relay(h, to):
        back = outer - 1 - to

        @pl.when((z > 0) & (z < to))
        def _():
            add_part(h, 1, to)

        send((z > 0) & (z < to), lambda: part_copy(h, 1, to))

        @pl.when((z < outer - 1) & (z > back))
        def _():
            add_part(h, 0, back)

        send((z < outer - 1) & (z > back), lambda: part_copy(h, 0, back))

    def side_copy(h):
        return pltpu.make_async_remote_copy(
            src_ref=own.at[h, other], dst_ref=side.at[h],
            send_sem=side_send.at[h], recv_sem=side_recv.at[h],
            device_id={"ctx": other},
        )

    def reduce_side(h):
        @pl.when(z > 0)
        def _():
            add_part(h, 1, z)

        @pl.when(z < outer - 1)
        def _():
            add_part(h, 0, z)

        send(None, lambda: side_copy(h))

    def reduce_end(h):
        side_copy(h).wait_recv()
        total = own[h, me].astype(f32) + side[h].astype(f32) + old[h, me].astype(f32)
        updated[h] = total
        new[h, me] = total.astype(b16)
        issue(1, h)

    def pieces(g, h, j):
        buf = (old, new)[g]
        start, shift = plan.starts[j], plan.shifts[j]
        for b in range(n):
            piece = buf[h, b, :, start : start + window].astype(f32)
            yield b, plan.move(piece, shift, 64 * (h % 2))

    def prepare_old(h):
        for j in range(3):
            total = jnp.zeros((1, window), f32)
            for b, piece in pieces(0, h, j):
                weights[j, b * units : (b + 1) * units] = piece.astype(b16)
                total = total + jnp.sum(piece * piece, axis=0, keepdims=True)
            squares_old[3 * h + j : 3 * h + j + 1, :] = total

    def prepare_new(h):
        for j in range(3):
            total = jnp.zeros((1, window), f32)
            for b, piece in pieces(1, h, j):
                total = total + jnp.sum(piece * piece, axis=0, keepdims=True)
            scale = jnp.sqrt(squares_old[3 * h + j : 3 * h + j + 1, :]) * lax.rsqrt(total + EPS)
            for b, piece in pieces(1, h, j):
                weights[j, b * units : (b + 1) * units] = (piece * scale).astype(b16)
            start, shift = plan.starts[j], plan.shifts[j]
            exact = plan.move(updated[h, :, start : start + window], shift, 64 * (h % 2)) * scale
            fresh_ref[j, h] = plan.move(exact, 64 * (h % 2), 0)[:, :width].astype(b16)

    def at_steps(i, slots):
        for k, events in slots.items():
            if events:
                def run(events=events):
                    for event in events:
                        event()
                pl.when(i == k)(run)

    def grads(h, slots):
        for j in range(3):
            acc[j] = jnp.zeros(acc.shape[1:], f32)
        cut = plan.columns(h)

        for k in range(tokens // step):
            for event in slots.get(k, ()):
                event()

        def body(i, _):
            span = pl.ds(pl.multiple_of(i * step, step), step)
            key = keys[span, cut]
            scaled = (values[span, cut].astype(f32) * rate[span, h : h + 1]).astype(b16)
            gpre = dot(weights[0], key, 1, 1)
            upre = dot(weights[1], key, 1, 1)
            back = dot(weights[2], scaled, 1, 1)
            sig = jax.nn.sigmoid(gpre)
            act = gpre * sig
            slope = sig * (1.0 + gpre * (1.0 - sig))
            acc[0] += dot((back * upre * slope).astype(b16), key, 1, 0)
            acc[1] += dot((back * act).astype(b16), key, 1, 0)
            acc[2] += dot((act * upre).astype(b16), scaled, 1, 0)
            return 0

        lax.fori_loop(0, tokens // step, body, 0)
        shift = 64 * (h % 2)
        for b in range(n):
            parts = [
                plan.move(acc[j, b * units : (b + 1) * units], shift, plan.shifts[j]) for j in range(3)
            ]
            own[h, b] = plan.pack(*parts).astype(b16)
        reduce_start(h)

    def apply_head(h):
        cut = plan.columns(h)

        def body(i, _):
            span = pl.ds(pl.multiple_of(i * step, step), step)
            query = queries[span, cut]
            gate = dot(query, weights[0], 1, 1)
            up = dot(query, weights[1], 1, 1)
            mixed = (jax.nn.silu(gate) * up).astype(b16)
            out = dot(mixed, weights[2], 1, 0)
            if h % 2:
                shared = slice(cut.start, cut.start + 128)
                outs[span, shared] = outs[span, shared] + out[:, :128]
                outs[span, cut.start + 128 : cut.stop] = out[:, 128:]
            else:
                outs[span, cut] = out
            part = out * out
            total = part[:, :128]
            for c in range(128, window, 128):
                total = total + part[:, c : c + 128]
            squares[span, :] = total if h == 0 else squares[span, :] + total
            return 0

        lax.fori_loop(0, tokens // step, body, 0)

    issue(0, 0)
    if heads > 1:
        issue(0, 1)
    turned = jnp.concatenate([rate_ref[...], jnp.zeros((8 - heads, tokens), f32)], axis=0) if heads < 8 else rate_ref[...]
    rate[...] = turned.T
    for h in range(heads):
        for d in range(1, outer):
            relay(0, h, d)
        if h + 2 < heads:
            issue(0, h + 2)
    for h in range(heads):
        if h % 2 == 0:
            for i, p, copy in loads:
                if p == h // 2 and i < 2:
                    copy.wait()
        arrived(0, h)
        prepare_old(h)
        grads(h, {})
        if h > 0:
            for to in range(outer - 1, 0, -1):
                reduce_relay(h - 1, to)
            reduce_side(h - 1)
    for to in range(outer - 1, 0, -1):
        reduce_relay(heads - 1, to)
    reduce_side(heads - 1)
    for h in range(heads):
        reduce_end(h)
        for d in range(1, outer):
            relay(1, h, d)
    for h in range(heads):
        if h % 2 == 0:
            for i, p, copy in loads:
                if p == h // 2 and i == 2:
                    copy.wait()
        arrived(1, h)
        prepare_new(h)
        apply_head(h)

    row[...] = jnp.sum(squares[...].T, axis=0, keepdims=True)

    def row_copy(t):
        return pltpu.make_async_remote_copy(
            src_ref=row, dst_ref=rows_in.at[t - 1],
            send_sem=row_send.at[t - 1], recv_sem=row_recv.at[t - 1],
            device_id={"head": lax.rem(mine + t, plan.peers)},
        )

    for t in range(1, plan.peers):
        send(None, functools.partial(row_copy, t))
    total = row[...]
    for t in range(1, plan.peers):
        row_copy(t).wait_recv()
        total = total + rows_in[t - 1]
    row_scale = lax.rsqrt(total / plan.width_all + EPS)
    column = jnp.broadcast_to(row_scale, (128, tokens)).T
    squares[...] = column

    def finish(i):
        span = pl.ds(pl.multiple_of(i * step, step), step)
        return pltpu.make_async_copy(keys.at[span], out_hbm.at[span], store_sem.at[i])

    def body(i, _):
        span = pl.ds(pl.multiple_of(i * step, step), step)
        for c in range(0, heads * width, 128):
            scaled = outs[span, c : c + 128] * squares[span, :] * gain_ref[:, c : c + 128]
            keys[span, c : c + 128] = scaled.astype(b16)
        finish(i).start()
        return 0

    lax.fori_loop(0, tokens // step, body, 0)
    for done in sends:
        done()
    for i in range(tokens // step):
        finish(i).wait()


def fused(n, peers, width_all, keys, values, queries, rates, w_gate, w_up, w_down, gain):
    rows = keys.shape[0]
    units, heads, width = w_gate.shape
    plan = Plan(n, peers, rows, units, heads, width, width_all)
    f32, b16 = jnp.float32, jnp.bfloat16
    outer = plan.outer
    hbm = pl.BlockSpec(memory_space=pl.ANY)
    block = (units, plan.packed)
    dma = pltpu.SemaphoreType.DMA
    return pl.pallas_call(
        functools.partial(fused_kernel, plan),
        out_shape=(
            jax.ShapeDtypeStruct(keys.shape, b16),
            jax.ShapeDtypeStruct((3, heads, units, width), b16),
        ),
        in_specs=[hbm] * 3 + vmem(5),
        out_specs=(hbm, vmem(1)[0]),
        scratch_shapes=[
            pltpu.VMEM(keys.shape, b16),
            pltpu.VMEM(keys.shape, b16),
            pltpu.VMEM(keys.shape, b16),
            pltpu.VMEM((rows, 8), f32),
            pltpu.VMEM((heads, n) + block, b16),
            pltpu.VMEM((heads, n) + block, b16),
            pltpu.VMEM((heads, n) + block, b16),
            pltpu.VMEM((heads, outer, 2) + block, b16),
            pltpu.VMEM((heads, outer, 2) + block, b16),
            pltpu.VMEM((heads,) + block, b16),
            pltpu.VMEM((heads,) + block, f32),
            pltpu.VMEM((3, n * units, plan.window), b16),
            pltpu.VMEM((3, n * units, plan.window), f32),
            pltpu.VMEM((3 * heads, plan.window), f32),
            pltpu.VMEM(keys.shape, f32),
            pltpu.VMEM((rows, 128), f32),
            pltpu.VMEM((1, rows), f32),
            pltpu.VMEM((peers - 1, 1, rows), f32),
            dma((3, heads // 2)),
            dma((rows // plan.step,)),
            dma((2, heads, 2, outer)),
            dma((2, heads, outer)),
            dma((2, heads, outer)),
            dma((2, heads, outer)),
            dma((heads, 2, outer)),
            dma((heads, 2, outer)),
            dma((heads,)),
            dma((heads,)),
            dma((peers - 1,)),
            dma((peers - 1,)),
        ],
        compiler_params=pltpu.CompilerParams(
            collective_id=2, has_side_effects=True, vmem_limit_bytes=67043328
        ),
        name="fused_layer",
    )(keys, values, queries, rates.T, w_gate, w_up, w_down, gain[None])


def per_device(n, peers, width_all, keys, values, queries, rates, w_gate, w_up, w_down, gain):
    rows = keys.shape[0]
    units, heads, width = w_gate.shape
    f32 = jnp.float32
    if fits(n, rows, units, heads, width):
        output, fresh = fused(
            n, peers, width_all, keys, values, queries, rates, w_gate, w_up, w_down, gain
        )
        fresh = fresh.transpose(0, 2, 1, 3)
        return (output, fresh[0], fresh[1], fresh[2])
    own = jnp.stack([w_gate, w_up, w_down]).transpose(0, 2, 1, 3)
    own = own.reshape(3 * heads, units, width)
    full = gather(own, n).transpose(1, 3, 0, 2)
    full = full.reshape(3, heads, width, n * units)
    grads = token_grads(keys, values, rates, full)
    block = (n, 3 * heads * width // n, n * units)
    old = lax.dynamic_index_in_dim(full.reshape(block), lax.axis_index("ctx"), 0, keepdims=False)
    fresh = update(grads.reshape(block), old, n).reshape(full.shape)
    mine = lax.dynamic_slice_in_dim(fresh, lax.axis_index("ctx") * units, units, 3)
    mine = mine.transpose(0, 3, 1, 2)
    outs, squares = apply(queries, fresh)
    squares = lax.psum(squares.reshape(rows), "head")
    scale = lax.rsqrt(squares / width_all + EPS)
    output = (outs.astype(f32) * scale[:, None] * gain[None]).astype(jnp.bfloat16)
    return (output, mine[0], mine[1], mine[2])


def solution(mesh):
    weight = P("ctx", "head", None)
    token = P("ctx", "head")

    def whole(keys, *rest):
        body = functools.partial(
            per_device, mesh.shape["ctx"], mesh.shape["head"], keys.shape[1]
        )
        return jax.shard_map(
            body,
            mesh=mesh,
            in_specs=(token,) * 4 + (weight,) * 3 + (P("head"),),
            out_specs=(token, weight, weight, weight),
            check_vma=False,
        )(keys, *rest)

    return whole
```

```python
import functools
import math

import jax
import jax.numpy as jnp
from jax import lax
from jax.experimental import pallas as pl
from jax.experimental.pallas import tpu as pltpu
from jax.sharding import PartitionSpec as P

EPS = 1e-06

ISSUE, RELAY, CROSS, READY, STEP, START, SIDE, PART, END, FINISH = range(10)
ORDERS = {
    (4, 4, 4): (
        (0, 1, 1, 1),
        ((0, 0, 0, 0), (0, 1, 0, 1)),
        (
            (ISSUE, 0, 0), (ISSUE, 0, 1), (RELAY, 0, 0, 1), (RELAY, 0, 1, 1), (RELAY, 0, 0, 2),
            (RELAY, 0, 1, 2), (RELAY, 0, 0, 3), (ISSUE, 0, 2), (RELAY, 0, 1, 3), (ISSUE, 0, 3),
            (RELAY, 0, 2, 1), (READY, 0, 0), (STEP, 0, 0, 0), (STEP, 0, 0, 1), (RELAY, 0, 2, 2),
            (STEP, 0, 0, 2), (RELAY, 0, 3, 1), (STEP, 0, 0, 3), (RELAY, 0, 2, 3), (START, 0),
            (READY, 0, 1), (STEP, 0, 1, 0), (RELAY, 0, 3, 2), (STEP, 0, 1, 1), (STEP, 0, 1, 2),
            (RELAY, 0, 3, 3), (STEP, 0, 1, 3), (PART, 0, 3, 1), (START, 1), (READY, 0, 2),
            (STEP, 0, 2, 0), (STEP, 0, 2, 1), (STEP, 0, 2, 2), (PART, 0, 2, 1), (PART, 0, 3, 2),
            (STEP, 0, 2, 3), (SIDE, 1, 0), (START, 2), (SIDE, 1, 3), (READY, 0, 3), (SIDE, 1, 2),
            (STEP, 0, 3, 0), (SIDE, 1, 1), (STEP, 0, 3, 1), (PART, 1, 3, 1), (STEP, 0, 3, 2),
            (SIDE, 2, 3), (PART, 1, 2, 1), (END, 0), (SIDE, 2, 0), (STEP, 0, 3, 3),
            (PART, 1, 3, 2), (PART, 2, 3, 1), (START, 3), (SIDE, 2, 2), (FINISH, 0), (SIDE, 2, 1),
            (END, 1), (FINISH, 1), (SIDE, 3, 3), (PART, 2, 3, 2), (RELAY, 1, 0, 1),
            (PART, 2, 2, 1), (SIDE, 3, 0), (SIDE, 3, 2), (RELAY, 1, 0, 2), (RELAY, 1, 1, 1),
            (PART, 3, 3, 1), (SIDE, 3, 1), (END, 2), (RELAY, 1, 0, 3), (RELAY, 1, 1, 2),
            (FINISH, 2), (PART, 3, 2, 1), (PART, 3, 3, 2), (RELAY, 1, 1, 3), (CROSS, 1, 1),
            (RELAY, 1, 2, 1), (END, 3), (READY, 1, 0), (FINISH, 3), (STEP, 1, 0, 0),
            (STEP, 1, 0, 1), (STEP, 1, 0, 2), (RELAY, 1, 2, 2), (STEP, 1, 0, 3), (READY, 1, 1),
            (RELAY, 1, 3, 1), (STEP, 1, 1, 0), (RELAY, 1, 2, 3), (STEP, 1, 1, 1), (STEP, 1, 1, 2),
            (RELAY, 1, 3, 2), (STEP, 1, 1, 3), (CROSS, 1, 3), (READY, 1, 2), (RELAY, 1, 3, 3),
            (STEP, 1, 2, 0), (STEP, 1, 2, 1), (STEP, 1, 2, 2), (STEP, 1, 2, 3), (READY, 1, 3),
            (STEP, 1, 3, 0), (STEP, 1, 3, 1), (STEP, 1, 3, 2), (STEP, 1, 3, 3),
        ),
    ),
}


def inner_size(n):
    inner = 1
    while inner * inner * 4 <= n and n % (inner * 2) == 0:
        inner *= 2
    return inner if inner > 1 or n % 2 else 2


def place(n, inner):
    me = lax.axis_index("ctx")
    return me, me // inner, lax.rem(me, inner), n // inner


def greet(z, x, outer, inner):
    barrier = pltpu.get_barrier_semaphore()
    for s in range(1, outer):
        pl.semaphore_signal(barrier, inc=1, device_id={"ctx": lax.rem(z + s, outer) * inner + x})
    for t in range(1, inner):
        pl.semaphore_signal(barrier, inc=1, device_id={"ctx": z * inner + lax.rem(x + t, inner)})
    pl.semaphore_wait(barrier, outer + inner - 2)


def spread(z, x, outer, inner, own_ref, out_ref, send_sem, recv_sem):
    me = z * inner + x
    copies = {}

    def send(src, block, device, s, t):
        copy = pltpu.make_async_remote_copy(
            src_ref=src,
            dst_ref=out_ref.at[block],
            send_sem=send_sem.at[s, t],
            recv_sem=recv_sem.at[s, t],
            device_id={"ctx": device},
        )
        copy.start()
        copies[s, t] = copy

    for s in range(1, outer):
        send(own_ref, me, lax.rem(z + s, outer) * inner + x, s, 0)
    for t in range(1, inner):
        send(own_ref, me, z * inner + lax.rem(x + t, inner), 0, t)
    for s in range(1, outer):
        copies[s, 0].wait_recv()
        block = lax.rem(z + outer - s, outer) * inner + x
        for t in range(1, inner):
            send(out_ref.at[block], block, z * inner + lax.rem(x + t, inner), s, t)
    for (s, t), copy in copies.items():
        if t:
            copy.wait_recv()
    for copy in copies.values():
        copy.wait_send()


def gather_kernel(n, inner, own_ref, out_ref, local_sem, send_sem, recv_sem):
    me, z, x, outer = place(n, inner)
    greet(z, x, outer, inner)
    keep = pltpu.make_async_copy(own_ref, out_ref.at[me], local_sem)
    keep.start()
    spread(z, x, outer, inner, own_ref, out_ref, send_sem, recv_sem)
    keep.wait()


def update_kernel(
    n, inner, grad_ref, old_ref, out_ref, near, part, far, fresh,
    local_sem, near_send, near_recv, far_send, far_recv, send_sem, recv_sem,
):
    me, z, x, outer = place(n, inner)
    greet(z, x, outer, inner)
    order = list(range(1, outer)) + [0]
    first = {}
    for s in order:
        row = lax.rem(z + s, outer) * inner
        for t in range(1, inner):
            column = lax.rem(x + t, inner)
            copy = pltpu.make_async_remote_copy(
                src_ref=grad_ref.at[row + column],
                dst_ref=near.at[s, t - 1],
                send_sem=near_send.at[s, t],
                recv_sem=near_recv.at[s, t],
                device_id={"ctx": z * inner + column},
            )
            copy.start()
            first[s, t] = copy
    second = {}
    total = None
    for s in order:
        row = lax.rem(z + s, outer) * inner
        total = grad_ref[row + x].astype(jnp.float32)
        for t in range(1, inner):
            first[s, t].wait_recv()
            total = total + near[s, t - 1].astype(jnp.float32)
        if s:
            part[s] = total.astype(part.dtype)
            copy = pltpu.make_async_remote_copy(
                src_ref=part.at[s],
                dst_ref=far.at[s],
                send_sem=far_send.at[s],
                recv_sem=far_recv.at[s],
                device_id={"ctx": row + x},
            )
            copy.start()
            second[s] = copy
    for s, copy in second.items():
        copy.wait_recv()
        total = total + far[s].astype(jnp.float32)
    old = old_ref[...].astype(jnp.float32)
    updated = old + total
    old_sq = jnp.sum(old * old, axis=1, keepdims=True)
    new_sq = jnp.sum(updated * updated, axis=1, keepdims=True)
    fresh[...] = (updated * (jnp.sqrt(old_sq) * lax.rsqrt(new_sq + EPS))).astype(fresh.dtype)
    keep = pltpu.make_async_copy(fresh, out_ref.at[me], local_sem)
    keep.start()
    keep.wait()
    spread(z, x, outer, inner, out_ref.at[me], out_ref, send_sem, recv_sem)
    for copy in first.values():
        copy.wait_send()
    for copy in second.values():
        copy.wait_send()


def vmem(count):
    return [pl.BlockSpec(memory_space=pltpu.VMEM)] * count


def gather(own, n):
    inner = inner_size(n)
    outer = n // inner
    return pl.pallas_call(
        functools.partial(gather_kernel, n, inner),
        out_shape=jax.ShapeDtypeStruct((n,) + own.shape, own.dtype),
        in_specs=vmem(1),
        out_specs=vmem(1)[0],
        scratch_shapes=[pltpu.SemaphoreType.DMA]
        + [pltpu.SemaphoreType.DMA((outer, inner))] * 2,
        compiler_params=pltpu.CompilerParams(collective_id=0, has_side_effects=True),
        name="gather_weights",
    )(own)


def update(grads, old, n):
    inner = inner_size(n)
    outer = n // inner
    block = grads.shape[1:]
    return pl.pallas_call(
        functools.partial(update_kernel, n, inner),
        out_shape=jax.ShapeDtypeStruct(grads.shape, grads.dtype),
        in_specs=vmem(2),
        out_specs=vmem(1)[0],
        scratch_shapes=[
            pltpu.VMEM((outer, max(inner - 1, 1)) + block, grads.dtype),
            pltpu.VMEM((outer,) + block, grads.dtype),
            pltpu.VMEM((outer,) + block, grads.dtype),
            pltpu.VMEM(block, grads.dtype),
            pltpu.SemaphoreType.DMA,
        ]
        + [pltpu.SemaphoreType.DMA((outer, inner))] * 2
        + [pltpu.SemaphoreType.DMA((outer,))] * 2
        + [pltpu.SemaphoreType.DMA((outer, inner))] * 2,
        compiler_params=pltpu.CompilerParams(collective_id=1, has_side_effects=True),
        name="update_weights",
    )(grads, old)


def dot(a, b, left, right):
    return lax.dot_general(a, b, (((left,), (right,)), ((), ())), preferred_element_type=jnp.float32)


def grads_kernel(key_ref, value_ref, rate_ref, weight_ref, out_ref, acc):
    step = pl.program_id(0)

    @pl.when(step == 0)
    def _():
        acc[...] = jnp.zeros_like(acc)

    heads, width = weight_ref.shape[1:3]
    for h in range(heads):
        columns = slice(h * width, (h + 1) * width)
        key = key_ref[:, columns]
        gpre = dot(key, weight_ref[0, h], 1, 0)
        upre = dot(key, weight_ref[1, h], 1, 0)
        scaled = (value_ref[:, columns].astype(jnp.float32) * rate_ref[:, h : h + 1]).astype(jnp.bfloat16)
        back = dot(scaled, weight_ref[2, h], 1, 0)
        sig = jax.nn.sigmoid(gpre)
        act = gpre * sig
        slope = sig * (1.0 + gpre * (1.0 - sig))
        acc[0, h] += dot(key, (back * upre * slope).astype(jnp.bfloat16), 0, 0)
        acc[1, h] += dot(key, (back * act).astype(jnp.bfloat16), 0, 0)
        acc[2, h] += dot(scaled, (act * upre).astype(jnp.bfloat16), 0, 0)

    @pl.when(step == pl.num_programs(0) - 1)
    def _():
        out_ref[...] = acc[...].astype(out_ref.dtype)


def apply_kernel(query_ref, weight_ref, out_ref, square_ref):
    heads, width = weight_ref.shape[1:3]
    squares = None
    for h in range(heads):
        columns = slice(h * width, (h + 1) * width)
        query = query_ref[:, columns]
        gate = dot(query, weight_ref[0, h], 1, 0)
        up = dot(query, weight_ref[1, h], 1, 0)
        mixed = (jax.nn.silu(gate) * up).astype(jnp.bfloat16)
        out = dot(mixed, weight_ref[2, h], 1, 1)
        part = jnp.sum(out * out, axis=1, keepdims=True)
        squares = part if squares is None else squares + part
        out_ref[:, columns] = out.astype(out_ref.dtype)
    square_ref[...] = squares


def tile(rows, width):
    return pl.BlockSpec((rows, width), lambda i: (i, 0))


def fixed(shape):
    return pl.BlockSpec(shape, lambda i: (0,) * len(shape))


def token_grads(keys, values, rates, weights):
    rows, width = keys.shape
    step = math.gcd(rows, 512)
    return pl.pallas_call(
        grads_kernel,
        grid=(rows // step,),
        out_shape=jax.ShapeDtypeStruct(weights.shape, jnp.bfloat16),
        in_specs=[tile(step, width), tile(step, width), tile(step, rates.shape[1]), fixed(weights.shape)],
        out_specs=fixed(weights.shape),
        scratch_shapes=[pltpu.VMEM(weights.shape, jnp.float32)],
        name="token_grads",
    )(keys, values, rates, weights)


def apply(queries, weights):
    rows, width = queries.shape
    step = math.gcd(rows, 512)
    return pl.pallas_call(
        apply_kernel,
        grid=(rows // step,),
        out_shape=(
            jax.ShapeDtypeStruct((rows, width), jnp.bfloat16),
            jax.ShapeDtypeStruct((rows, 1), jnp.float32),
        ),
        in_specs=[tile(step, width), fixed(weights.shape)],
        out_specs=(tile(step, width), tile(step, 1)),
        name="apply_weights",
    )(queries, weights)


def fits(n, rows, units, heads, width):
    inner = inner_size(n)
    return (
        inner == 2
        and n // inner >= 2
        and units % 8 == 0
        and heads % 2 == 0
        and heads <= 8
        and width % 128 == 64
        and rows % 512 == 0
        and rows * heads * width <= 2048 * 1280
        and (n // inner, heads, rows // 512) in ORDERS
    )


class Plan:
    def __init__(self, n, peers, rows, units, heads, width, width_all):
        self.n, self.peers, self.rows, self.units = n, peers, rows, units
        self.heads, self.width, self.width_all = heads, width, width_all
        self.inner = 2
        self.outer = n // 2
        self.step = 512
        self.window = width + 64
        self.packed = 2 * width + self.window
        self.starts = (0, width - 64, 2 * width)
        self.shifts = (0, 64, 0)

    def columns(self, h):
        start = (h // 2) * 2 * self.width + (h % 2) * (self.width - 64)
        return slice(start, start + self.window)

    def move(self, x, old, new):
        size = x.shape[1]
        if old != new:
            x = pltpu.roll(x, (new - old) % size, 1)
        lane = lax.broadcasted_iota(jnp.int32, x.shape, 1)
        return jnp.where((lane >= new) & (lane < new + self.width), x, 0.0)

    def pack(self, gate, up, down):
        first = self.width - 64
        shared = gate[:, first:] + up[:, :128]
        return jnp.concatenate([gate[:, :first], shared, up[:, 128:], down], axis=1)


def fused_kernel(
    plan, key_hbm, value_hbm, query_hbm, rate_ref, gate_ref, up_ref, down_ref, gain_ref,
    out_hbm, fresh_ref,
    keys, values, queries, rate, old, new, own, ups, downs, side, updated, weights, acc,
    squares_old, outs, squares, row, rows_in,
    load_sem, store_sem,
    line_send, line_recv, cross_send, cross_recv, pass_send, pass_recv,
    part_send, part_recv, side_send, side_recv, row_send, row_recv,
):
    f32, b16 = jnp.float32, jnp.bfloat16
    n, outer, heads, units, width = plan.n, plan.outer, plan.heads, plan.units, plan.width
    window, step, tokens = plan.window, plan.step, plan.rows
    me = lax.axis_index("ctx")
    z, x = me // 2, lax.rem(me, 2)
    mine = lax.axis_index("head")
    other = z * 2 + 1 - x

    loads = []
    half = 2 * width
    for p in range(heads // 2):
        cut = slice(p * half, (p + 1) * half)
        for i, (src, dst) in enumerate(((key_hbm, keys), (value_hbm, values), (query_hbm, queries))):
            copy = pltpu.make_async_copy(src.at[:, cut], dst.at[:, cut], load_sem.at[i, p])
            if i < 2:
                copy.start()
            loads.append((i, p, copy))
    for i, p, copy in loads:
        if i == 2:
            copy.start()

    barrier = pltpu.get_barrier_semaphore()
    pl.semaphore_signal(barrier, inc=1, device_id={"ctx": other})
    for t in range(1, plan.peers):
        pl.semaphore_signal(barrier, inc=1, device_id={"head": lax.rem(mine + t, plan.peers)})

    hops = sorted({1, outer - 1})
    for t in hops:
        pl.semaphore_signal(barrier, inc=1, device_id={"ctx": lax.rem(z + t, outer) * 2 + x})

    for h in range(heads):
        parts = []
        for j, ref in enumerate((gate_ref, up_ref, down_ref)):
            piece = ref[:, h, :].astype(f32)
            piece = jnp.concatenate([piece, jnp.zeros((units, 64), f32)], axis=1)
            parts.append(plan.move(piece, 0, plan.shifts[j]))
        old[h, me] = plan.pack(*parts).astype(b16)

    pl.semaphore_wait(barrier, plan.peers + len(hops))

    sends = []
    side_first, passing, order = ORDERS[outer, heads, tokens // step]

    def send(when, make):
        def start():
            make().start()

        def finish():
            make().wait_send()

        if when is None:
            start()
            sends.append(finish)
        else:
            pl.when(when())(start)
            sends.append(lambda: pl.when(when())(finish))

    def line_copy(g, h, origin, up):
        buf = (old, new)[g]
        block = origin * 2 + x
        return pltpu.make_async_remote_copy(
            src_ref=buf.at[h, block], dst_ref=buf.at[h, block],
            send_sem=line_send.at[g, h, up, origin], recv_sem=line_recv.at[g, h, origin],
            device_id={"ctx": me + (2 if up else -2)},
        )

    def cross_copy(g, h, origin):
        buf = (old, new)[g]
        block = origin * 2 + x
        return pltpu.make_async_remote_copy(
            src_ref=buf.at[h, block], dst_ref=buf.at[h, block],
            send_sem=cross_send.at[g, h, origin], recv_sem=cross_recv.at[g, h, origin],
            device_id={"ctx": other},
        )

    def issue(g, h):
        send(lambda: z < outer - 1, lambda: line_copy(g, h, z, 1))
        send(lambda: z > 0, lambda: line_copy(g, h, z, 0))
        send(None, lambda: cross_copy(g, h, z))

    def relay(g, h, d):
        whole = d > 1 or not passing[g][h]

        @pl.when(z >= d)
        def _():
            line_copy(g, h, z - d, 1).wait_recv()

        send(lambda: (z >= d) & (z < outer - 1), lambda: line_copy(g, h, z - d, 1))
        if whole:
            send(lambda: z >= d, lambda: cross_copy(g, h, z - d))

        @pl.when(z + d < outer)
        def _():
            line_copy(g, h, z + d, 0).wait_recv()

        send(lambda: (z + d < outer) & (z > 0), lambda: line_copy(g, h, z + d, 0))
        if whole:
            send(lambda: z + d < outer, lambda: cross_copy(g, h, z + d))

    def pass_copy(g, h, up):
        buf = (old, new)[g]
        return pltpu.make_async_remote_copy(
            src_ref=buf.at[h, other], dst_ref=buf.at[h, other],
            send_sem=pass_send.at[g, h, up], recv_sem=pass_recv.at[g, h, up],
            device_id={"ctx": me + (2 if up else -2)},
        )

    def cross(g, h):
        cross_copy(g, h, z).wait_recv()
        send(lambda: z < outer - 1, lambda: pass_copy(g, h, 1))
        send(lambda: z > 0, lambda: pass_copy(g, h, 0))

    def arrived(g, h):
        if not passing[g][h]:
            for o in range(outer):
                cross_copy(g, h, o).wait_recv()
            return
        for o in range(outer):
            pl.when((o > z + 1) | (o < z - 1))(lambda: cross_copy(g, h, o).wait_recv())
        pl.when(z > 0)(lambda: pass_copy(g, h, 1).wait_recv())
        pl.when(z < outer - 1)(lambda: pass_copy(g, h, 0).wait_recv())

    def part_copy(h, up, to):
        buf = (downs, ups)[up]
        first, count = (to * 2 + x, 1) if side_first[h] else (to * 2, 2)
        return pltpu.make_async_remote_copy(
            src_ref=own.at[h, pl.ds(first, count)], dst_ref=buf.at[h, to, pl.ds(0, count)],
            send_sem=part_send.at[h, up, to], recv_sem=part_recv.at[h, up, to],
            device_id={"ctx": me + (2 if up else -2)},
        )

    def add_part(h, up, to):
        buf = (downs, ups)[up]
        part_copy(h, up, to).wait_recv()
        for c in range(1 if side_first[h] else 2):
            block = to * 2 + (x if side_first[h] else c)
            total = own[h, block].astype(f32) + buf[h, to, c].astype(f32)
            own[h, block] = total.astype(b16)

    def side_copy(h, to):
        return pltpu.make_async_remote_copy(
            src_ref=own.at[h, to * 2 + 1 - x], dst_ref=side.at[h, to if side_first[h] else 0],
            send_sem=side_send.at[h, to], recv_sem=side_recv.at[h, to],
            device_id={"ctx": other},
        )

    def reduce_start(h):
        if side_first[h]:
            for i in range(outer):
                send(None, functools.partial(side_copy, h, i // 2 if i % 2 else outer - 1 - i // 2))
            return
        for to in range(outer - 1, 0, -1):
            send(lambda: z == 0, functools.partial(part_copy, h, 1, to))
            send(lambda: z == outer - 1, functools.partial(part_copy, h, 0, outer - 1 - to))

    def reduce_beside(h, to):
        side_copy(h, to).wait_recv()
        total = own[h, to * 2 + x].astype(f32) + side[h, to].astype(f32)
        own[h, to * 2 + x] = total.astype(b16)
        if to > 0:
            send(lambda: z == 0, lambda: part_copy(h, 1, to))
        if to < outer - 1:
            send(lambda: z == outer - 1, lambda: part_copy(h, 0, to))

    def reduce_relay(h, to, d):
        back = outer - 1 - to

        @pl.when(z == d)
        def _():
            add_part(h, 1, to)

        send(lambda: z == d, lambda: part_copy(h, 1, to))

        @pl.when(z == outer - 1 - d)
        def _():
            add_part(h, 0, back)

        send(lambda: z == outer - 1 - d, lambda: part_copy(h, 0, back))

    def reduce_end(h):
        @pl.when(z > 0)
        def _():
            add_part(h, 1, z)

        @pl.when(z < outer - 1)
        def _():
            add_part(h, 0, z)

        if not side_first[h]:
            send(None, lambda: side_copy(h, z))

    def renew(h):
        total = own[h, me].astype(f32) + old[h, me].astype(f32)
        if not side_first[h]:
            side_copy(h, z).wait_recv()
            total = total + side[h, 0].astype(f32)
        updated[h] = total
        new[h, me] = total.astype(b16)
        issue(1, h)

    def pieces(g, h, j):
        buf = (old, new)[g]
        start, shift = plan.starts[j], plan.shifts[j]
        for b in range(n):
            piece = buf[h, b, :, start : start + window].astype(f32)
            yield b, plan.move(piece, shift, 64 * (h % 2))

    def prepare_old(h):
        for j in range(3):
            total = jnp.zeros((1, window), f32)
            for b, piece in pieces(0, h, j):
                weights[j, b * units : (b + 1) * units] = piece.astype(b16)
                total = total + jnp.sum(piece * piece, axis=0, keepdims=True)
            squares_old[3 * h + j : 3 * h + j + 1, :] = total

    def prepare_new(h):
        for j in range(3):
            total = jnp.zeros((1, window), f32)
            for b, piece in pieces(1, h, j):
                total = total + jnp.sum(piece * piece, axis=0, keepdims=True)
            scale = jnp.sqrt(squares_old[3 * h + j : 3 * h + j + 1, :]) * lax.rsqrt(total + EPS)
            for b, piece in pieces(1, h, j):
                weights[j, b * units : (b + 1) * units] = (piece * scale).astype(b16)
            start, shift = plan.starts[j], plan.shifts[j]
            exact = plan.move(updated[h, :, start : start + window], shift, 64 * (h % 2)) * scale
            fresh_ref[j, h] = plan.move(exact, 64 * (h % 2), 0)[:, :width].astype(b16)

    def at_steps(i, slots):
        for k, events in sorted(slots.items()):
            @pl.when(i == k)
            def _():
                for event in events:
                    event()

    def grads(h, slots):
        for j in range(3):
            acc[j] = jnp.zeros(acc.shape[1:], f32)
        cut = plan.columns(h)

        def body(i, _):
            at_steps(i, slots)
            span = pl.ds(pl.multiple_of(i * step, step), step)
            key = keys[span, cut]
            scaled = (values[span, cut].astype(f32) * rate[span, h : h + 1]).astype(b16)
            gpre = dot(weights[0], key, 1, 1)
            upre = dot(weights[1], key, 1, 1)
            back = dot(weights[2], scaled, 1, 1)
            sig = jax.nn.sigmoid(gpre)
            act = gpre * sig
            slope = sig * (1.0 + gpre * (1.0 - sig))
            acc[0] += dot((back * upre * slope).astype(b16), key, 1, 0)
            acc[1] += dot((back * act).astype(b16), key, 1, 0)
            acc[2] += dot((act * upre).astype(b16), scaled, 1, 0)
            return 0

        lax.fori_loop(0, tokens // step, body, 0)

    def start(h):
        shift = 64 * (h % 2)
        for b in range(n):
            parts = [
                plan.move(acc[j, b * units : (b + 1) * units], shift, plan.shifts[j]) for j in range(3)
            ]
            own[h, b] = plan.pack(*parts).astype(b16)
        reduce_start(h)

    def apply_head(h, slots):
        cut = plan.columns(h)

        def body(i, _):
            at_steps(i, slots)
            span = pl.ds(pl.multiple_of(i * step, step), step)
            query = queries[span, cut]
            gate = dot(query, weights[0], 1, 1)
            up = dot(query, weights[1], 1, 1)
            mixed = (jax.nn.silu(gate) * up).astype(b16)
            out = dot(mixed, weights[2], 1, 0)
            if h % 2:
                shared = slice(cut.start, cut.start + 128)
                outs[span, shared] = outs[span, shared] + out[:, :128]
                outs[span, cut.start + 128 : cut.stop] = out[:, 128:]
            else:
                outs[span, cut] = out
            part = out * out
            total = part[:, :128]
            for c in range(128, window, 128):
                total = total + part[:, c : c + 128]
            squares[span, :] = total if h == 0 else squares[span, :] + total
            return 0

        lax.fori_loop(0, tokens // step, body, 0)

    def loaded(h, kinds):
        if h % 2 == 0:
            for i, p, copy in loads:
                if p == h // 2 and i in kinds:
                    copy.wait()

    def ready(g, h):
        loaded(h, (2,) if g else (0, 1))
        arrived(g, h)
        (prepare_new if g else prepare_old)(h)

    handlers = {
        ISSUE: issue, RELAY: relay, CROSS: cross, READY: ready, START: start, SIDE: reduce_beside,
        PART: reduce_relay, END: reduce_end, FINISH: renew,
    }
    turned = rate_ref[...]
    if heads < 8:
        turned = jnp.concatenate([turned, jnp.zeros((8 - heads, tokens), f32)], axis=0)
    rate[...] = turned.T

    order = list(order)
    while order:
        event = order.pop(0)
        if event[0] != READY:
            handlers[event[0]](*event[1:])
            continue
        ready(*event[1:])
        slots = {}
        for k in range(tokens // step):
            while order[0][0] != STEP:
                kind, *rest = order.pop(0)
                slots.setdefault(k, []).append(functools.partial(handlers[kind], *rest))
            order.pop(0)
        (apply_head if event[1] else grads)(event[2], slots)

    row[...] = jnp.sum(squares[...].T, axis=0, keepdims=True)

    def row_copy(t):
        return pltpu.make_async_remote_copy(
            src_ref=row, dst_ref=rows_in.at[t - 1],
            send_sem=row_send.at[t - 1], recv_sem=row_recv.at[t - 1],
            device_id={"head": lax.rem(mine + t, plan.peers)},
        )

    for t in range(1, plan.peers):
        send(None, functools.partial(row_copy, t))
    total = row[...]
    for t in range(1, plan.peers):
        row_copy(t).wait_recv()
        total = total + rows_in[t - 1]
    row_scale = lax.rsqrt(total / plan.width_all + EPS)
    column = jnp.broadcast_to(row_scale, (128, tokens)).T
    squares[...] = column

    def finish(i):
        span = pl.ds(pl.multiple_of(i * step, step), step)
        return pltpu.make_async_copy(keys.at[span], out_hbm.at[span], store_sem.at[i])

    def body(i, _):
        span = pl.ds(pl.multiple_of(i * step, step), step)
        for c in range(0, heads * width, 128):
            scaled = outs[span, c : c + 128] * squares[span, :] * gain_ref[:, c : c + 128]
            keys[span, c : c + 128] = scaled.astype(b16)
        finish(i).start()
        return 0

    lax.fori_loop(0, tokens // step, body, 0)
    for done in sends:
        done()
    for i in range(tokens // step):
        finish(i).wait()


def fused(n, peers, width_all, keys, values, queries, rates, w_gate, w_up, w_down, gain):
    rows = keys.shape[0]
    units, heads, width = w_gate.shape
    plan = Plan(n, peers, rows, units, heads, width, width_all)
    f32, b16 = jnp.float32, jnp.bfloat16
    outer = plan.outer
    hbm = pl.BlockSpec(memory_space=pl.ANY)
    block = (units, plan.packed)
    dma = pltpu.SemaphoreType.DMA
    return pl.pallas_call(
        functools.partial(fused_kernel, plan),
        out_shape=(
            jax.ShapeDtypeStruct(keys.shape, b16),
            jax.ShapeDtypeStruct((3, heads, units, width), b16),
        ),
        in_specs=[hbm] * 3 + vmem(5),
        out_specs=(hbm, vmem(1)[0]),
        scratch_shapes=[
            pltpu.VMEM(keys.shape, b16),
            pltpu.VMEM(keys.shape, b16),
            pltpu.VMEM(keys.shape, b16),
            pltpu.VMEM((rows, 8), f32),
            pltpu.VMEM((heads, n) + block, b16),
            pltpu.VMEM((heads, n) + block, b16),
            pltpu.VMEM((heads, n) + block, b16),
            pltpu.VMEM((heads, outer, 2) + block, b16),
            pltpu.VMEM((heads, outer, 2) + block, b16),
            pltpu.VMEM((heads, outer) + block, b16),
            pltpu.VMEM((heads,) + block, f32),
            pltpu.VMEM((3, n * units, plan.window), b16),
            pltpu.VMEM((3, n * units, plan.window), f32),
            pltpu.VMEM((3 * heads, plan.window), f32),
            pltpu.VMEM(keys.shape, f32),
            pltpu.VMEM((rows, 128), f32),
            pltpu.VMEM((1, rows), f32),
            pltpu.VMEM((peers - 1, 1, rows), f32),
            dma((3, heads // 2)),
            dma((rows // plan.step,)),
            dma((2, heads, 2, outer)),
            dma((2, heads, outer)),
            dma((2, heads, outer)),
            dma((2, heads, outer)),
            dma((2, heads, 2)),
            dma((2, heads, 2)),
            dma((heads, 2, outer)),
            dma((heads, 2, outer)),
            dma((heads, outer)),
            dma((heads, outer)),
            dma((peers - 1,)),
            dma((peers - 1,)),
        ],
        compiler_params=pltpu.CompilerParams(
            collective_id=2, has_side_effects=True, vmem_limit_bytes=67043328
        ),
        name="fused_layer",
    )(keys, values, queries, rates.T, w_gate, w_up, w_down, gain[None])


def per_device(n, peers, width_all, keys, values, queries, rates, w_gate, w_up, w_down, gain):
    rows = keys.shape[0]
    units, heads, width = w_gate.shape
    f32 = jnp.float32
    if fits(n, rows, units, heads, width):
        output, fresh = fused(
            n, peers, width_all, keys, values, queries, rates, w_gate, w_up, w_down, gain
        )
        fresh = fresh.transpose(0, 2, 1, 3)
        return (output, fresh[0], fresh[1], fresh[2])
    own = jnp.stack([w_gate, w_up, w_down]).transpose(0, 2, 1, 3)
    own = own.reshape(3 * heads, units, width)
    full = gather(own, n).transpose(1, 3, 0, 2)
    full = full.reshape(3, heads, width, n * units)
    grads = token_grads(keys, values, rates, full)
    block = (n, 3 * heads * width // n, n * units)
    old = lax.dynamic_index_in_dim(full.reshape(block), lax.axis_index("ctx"), 0, keepdims=False)
    fresh = update(grads.reshape(block), old, n).reshape(full.shape)
    mine = lax.dynamic_slice_in_dim(fresh, lax.axis_index("ctx") * units, units, 3)
    mine = mine.transpose(0, 3, 1, 2)
    outs, squares = apply(queries, fresh)
    squares = lax.psum(squares.reshape(rows), "head")
    scale = lax.rsqrt(squares / width_all + EPS)
    output = (outs.astype(f32) * scale[:, None] * gain[None]).astype(jnp.bfloat16)
    return (output, mine[0], mine[1], mine[2])


def solution(mesh):
    weight = P("ctx", "head", None)
    token = P("ctx", "head")

    def whole(keys, *rest):
        body = functools.partial(
            per_device, mesh.shape["ctx"], mesh.shape["head"], keys.shape[1]
        )
        return jax.shard_map(
            body,
            mesh=mesh,
            in_specs=(token,) * 4 + (weight,) * 3 + (P("head"),),
            out_specs=(token, weight, weight, weight),
            check_vma=False,
        )(keys, *rest)

    return whole
```

```python
import functools
import math

import jax
import jax.numpy as jnp
from jax import lax
from jax.experimental import pallas as pl
from jax.experimental.pallas import tpu as pltpu
from jax.sharding import PartitionSpec as P

EPS = 1e-06

VMEM_LIMIT = 50 * 1024 * 1024
ISSUE, RELAY, CROSS, READY, STEP, START, SIDE, PART, END, FINISH = range(10)
ORDERS = {
    (4, 4, 4): (
        (0, 1, 1, 1),
        ((0, 1, 0, 1), (0, 1, 0, 1)),
        (
            (ISSUE, 0, 0), (ISSUE, 0, 1), (RELAY, 0, 0, 1), (RELAY, 0, 1, 1), (RELAY, 0, 0, 2),
            (RELAY, 0, 1, 2), (RELAY, 0, 0, 3), (ISSUE, 0, 2), (CROSS, 0, 1), (RELAY, 0, 1, 3),
            (ISSUE, 0, 3), (READY, 0, 0), (STEP, 0, 0, 0), (RELAY, 0, 2, 1), (STEP, 0, 0, 1),
            (STEP, 0, 0, 2), (STEP, 0, 0, 3), (RELAY, 0, 2, 2), (START, 0), (RELAY, 0, 3, 1),
            (READY, 0, 1), (RELAY, 0, 2, 3), (STEP, 0, 1, 0), (STEP, 0, 1, 1), (RELAY, 0, 3, 2),
            (CROSS, 0, 3), (STEP, 0, 1, 2), (RELAY, 0, 3, 3), (STEP, 0, 1, 3), (START, 1),
            (PART, 0, 3, 1), (READY, 0, 2), (STEP, 0, 2, 0), (STEP, 0, 2, 1), (STEP, 0, 2, 2),
            (PART, 0, 2, 1), (SIDE, 1, 3), (STEP, 0, 2, 3), (START, 2), (SIDE, 1, 0), (SIDE, 1, 2),
            (PART, 0, 3, 2), (READY, 0, 3), (STEP, 0, 3, 0), (STEP, 0, 3, 1), (SIDE, 1, 1),
            (STEP, 0, 3, 2), (SIDE, 2, 0), (PART, 1, 3, 1), (SIDE, 2, 3), (END, 0),
            (PART, 1, 2, 1), (STEP, 0, 3, 3), (PART, 1, 3, 2), (PART, 2, 3, 1), (SIDE, 2, 2),
            (START, 3), (FINISH, 0), (SIDE, 2, 1), (END, 1), (FINISH, 1), (PART, 2, 3, 2),
            (RELAY, 1, 0, 1), (SIDE, 3, 3), (PART, 2, 2, 1), (SIDE, 3, 0), (RELAY, 1, 1, 1),
            (SIDE, 3, 2), (RELAY, 1, 0, 2), (SIDE, 3, 1), (PART, 3, 3, 1), (END, 2),
            (RELAY, 1, 1, 2), (RELAY, 1, 0, 3), (FINISH, 2), (PART, 3, 2, 1), (PART, 3, 3, 2),
            (CROSS, 1, 1), (END, 3), (RELAY, 1, 1, 3), (RELAY, 1, 2, 1), (FINISH, 3),
            (READY, 1, 0), (STEP, 1, 0, 0), (STEP, 1, 0, 1), (STEP, 1, 0, 2), (RELAY, 1, 2, 2),
            (STEP, 1, 0, 3), (RELAY, 1, 3, 1), (READY, 1, 1), (RELAY, 1, 2, 3), (STEP, 1, 1, 0),
            (STEP, 1, 1, 1), (RELAY, 1, 3, 2), (STEP, 1, 1, 2), (CROSS, 1, 3), (STEP, 1, 1, 3),
            (RELAY, 1, 3, 3), (READY, 1, 2), (STEP, 1, 2, 0), (STEP, 1, 2, 1), (STEP, 1, 2, 2),
            (STEP, 1, 2, 3), (READY, 1, 3), (STEP, 1, 3, 0), (STEP, 1, 3, 1), (STEP, 1, 3, 2),
            (STEP, 1, 3, 3),
        ),
    ),
}


def inner_size(n):
    inner = 1
    while inner * inner * 4 <= n and n % (inner * 2) == 0:
        inner *= 2
    return inner if inner > 1 or n % 2 else 2


def place(n, inner):
    me = lax.axis_index("ctx")
    return me, me // inner, lax.rem(me, inner), n // inner


def greet(z, x, outer, inner):
    barrier = pltpu.get_barrier_semaphore()
    for s in range(1, outer):
        pl.semaphore_signal(barrier, inc=1, device_id={"ctx": lax.rem(z + s, outer) * inner + x})
    for t in range(1, inner):
        pl.semaphore_signal(barrier, inc=1, device_id={"ctx": z * inner + lax.rem(x + t, inner)})
    pl.semaphore_wait(barrier, outer + inner - 2)


def spread(z, x, outer, inner, own_ref, out_ref, send_sem, recv_sem):
    me = z * inner + x
    copies = {}

    def send(src, block, device, s, t):
        copy = pltpu.make_async_remote_copy(
            src_ref=src,
            dst_ref=out_ref.at[block],
            send_sem=send_sem.at[s, t],
            recv_sem=recv_sem.at[s, t],
            device_id={"ctx": device},
        )
        copy.start()
        copies[s, t] = copy

    for s in range(1, outer):
        send(own_ref, me, lax.rem(z + s, outer) * inner + x, s, 0)
    for t in range(1, inner):
        send(own_ref, me, z * inner + lax.rem(x + t, inner), 0, t)
    for s in range(1, outer):
        copies[s, 0].wait_recv()
        block = lax.rem(z + outer - s, outer) * inner + x
        for t in range(1, inner):
            send(out_ref.at[block], block, z * inner + lax.rem(x + t, inner), s, t)
    for (s, t), copy in copies.items():
        if t:
            copy.wait_recv()
    for copy in copies.values():
        copy.wait_send()


def gather_kernel(n, inner, own_ref, out_ref, local_sem, send_sem, recv_sem):
    me, z, x, outer = place(n, inner)
    greet(z, x, outer, inner)
    keep = pltpu.make_async_copy(own_ref, out_ref.at[me], local_sem)
    keep.start()
    spread(z, x, outer, inner, own_ref, out_ref, send_sem, recv_sem)
    keep.wait()


def update_kernel(
    n, inner, grad_ref, old_ref, out_ref, near, part, far, fresh,
    local_sem, near_send, near_recv, far_send, far_recv, send_sem, recv_sem,
):
    me, z, x, outer = place(n, inner)
    greet(z, x, outer, inner)
    order = list(range(1, outer)) + [0]
    first = {}
    for s in order:
        row = lax.rem(z + s, outer) * inner
        for t in range(1, inner):
            column = lax.rem(x + t, inner)
            copy = pltpu.make_async_remote_copy(
                src_ref=grad_ref.at[row + column],
                dst_ref=near.at[s, t - 1],
                send_sem=near_send.at[s, t],
                recv_sem=near_recv.at[s, t],
                device_id={"ctx": z * inner + column},
            )
            copy.start()
            first[s, t] = copy
    second = {}
    total = None
    for s in order:
        row = lax.rem(z + s, outer) * inner
        total = grad_ref[row + x].astype(jnp.float32)
        for t in range(1, inner):
            first[s, t].wait_recv()
            total = total + near[s, t - 1].astype(jnp.float32)
        if s:
            part[s] = total.astype(part.dtype)
            copy = pltpu.make_async_remote_copy(
                src_ref=part.at[s],
                dst_ref=far.at[s],
                send_sem=far_send.at[s],
                recv_sem=far_recv.at[s],
                device_id={"ctx": row + x},
            )
            copy.start()
            second[s] = copy
    for s, copy in second.items():
        copy.wait_recv()
        total = total + far[s].astype(jnp.float32)
    old = old_ref[...].astype(jnp.float32)
    updated = old + total
    old_sq = jnp.sum(old * old, axis=1, keepdims=True)
    new_sq = jnp.sum(updated * updated, axis=1, keepdims=True)
    fresh[...] = (updated * (jnp.sqrt(old_sq) * lax.rsqrt(new_sq + EPS))).astype(fresh.dtype)
    keep = pltpu.make_async_copy(fresh, out_ref.at[me], local_sem)
    keep.start()
    keep.wait()
    spread(z, x, outer, inner, out_ref.at[me], out_ref, send_sem, recv_sem)
    for copy in first.values():
        copy.wait_send()
    for copy in second.values():
        copy.wait_send()


def vmem(count):
    return [pl.BlockSpec(memory_space=pltpu.VMEM)] * count


def gather(own, n):
    inner = inner_size(n)
    outer = n // inner
    return pl.pallas_call(
        functools.partial(gather_kernel, n, inner),
        out_shape=jax.ShapeDtypeStruct((n,) + own.shape, own.dtype),
        in_specs=vmem(1),
        out_specs=vmem(1)[0],
        scratch_shapes=[pltpu.SemaphoreType.DMA]
        + [pltpu.SemaphoreType.DMA((outer, inner))] * 2,
        compiler_params=pltpu.CompilerParams(collective_id=0, has_side_effects=True),
        name="gather_weights",
    )(own)


def update(grads, old, n):
    inner = inner_size(n)
    outer = n // inner
    block = grads.shape[1:]
    return pl.pallas_call(
        functools.partial(update_kernel, n, inner),
        out_shape=jax.ShapeDtypeStruct(grads.shape, grads.dtype),
        in_specs=vmem(2),
        out_specs=vmem(1)[0],
        scratch_shapes=[
            pltpu.VMEM((outer, max(inner - 1, 1)) + block, grads.dtype),
            pltpu.VMEM((outer,) + block, grads.dtype),
            pltpu.VMEM((outer,) + block, grads.dtype),
            pltpu.VMEM(block, grads.dtype),
            pltpu.SemaphoreType.DMA,
        ]
        + [pltpu.SemaphoreType.DMA((outer, inner))] * 2
        + [pltpu.SemaphoreType.DMA((outer,))] * 2
        + [pltpu.SemaphoreType.DMA((outer, inner))] * 2,
        compiler_params=pltpu.CompilerParams(collective_id=1, has_side_effects=True),
        name="update_weights",
    )(grads, old)


def dot(a, b, left, right):
    return lax.dot_general(a, b, (((left,), (right,)), ((), ())), preferred_element_type=jnp.float32)


def grads_kernel(key_ref, value_ref, rate_ref, weight_ref, out_ref, acc):
    step = pl.program_id(0)

    @pl.when(step == 0)
    def _():
        acc[...] = jnp.zeros_like(acc)

    heads, width = weight_ref.shape[1:3]
    for h in range(heads):
        columns = slice(h * width, (h + 1) * width)
        key = key_ref[:, columns]
        gpre = dot(key, weight_ref[0, h], 1, 0)
        upre = dot(key, weight_ref[1, h], 1, 0)
        scaled = (value_ref[:, columns].astype(jnp.float32) * rate_ref[:, h : h + 1]).astype(jnp.bfloat16)
        back = dot(scaled, weight_ref[2, h], 1, 0)
        sig = jax.nn.sigmoid(gpre)
        act = gpre * sig
        slope = sig * (1.0 + gpre * (1.0 - sig))
        acc[0, h] += dot(key, (back * upre * slope).astype(jnp.bfloat16), 0, 0)
        acc[1, h] += dot(key, (back * act).astype(jnp.bfloat16), 0, 0)
        acc[2, h] += dot(scaled, (act * upre).astype(jnp.bfloat16), 0, 0)

    @pl.when(step == pl.num_programs(0) - 1)
    def _():
        out_ref[...] = acc[...].astype(out_ref.dtype)


def apply_kernel(query_ref, weight_ref, out_ref, square_ref):
    heads, width = weight_ref.shape[1:3]
    squares = None
    for h in range(heads):
        columns = slice(h * width, (h + 1) * width)
        query = query_ref[:, columns]
        gate = dot(query, weight_ref[0, h], 1, 0)
        up = dot(query, weight_ref[1, h], 1, 0)
        mixed = (jax.nn.silu(gate) * up).astype(jnp.bfloat16)
        out = dot(mixed, weight_ref[2, h], 1, 1)
        part = jnp.sum(out * out, axis=1, keepdims=True)
        squares = part if squares is None else squares + part
        out_ref[:, columns] = out.astype(out_ref.dtype)
    square_ref[...] = squares


def tile(rows, width):
    return pl.BlockSpec((rows, width), lambda i: (i, 0))


def fixed(shape):
    return pl.BlockSpec(shape, lambda i: (0,) * len(shape))


def token_grads(keys, values, rates, weights):
    rows, width = keys.shape
    step = math.gcd(rows, 512)
    return pl.pallas_call(
        grads_kernel,
        grid=(rows // step,),
        out_shape=jax.ShapeDtypeStruct(weights.shape, jnp.bfloat16),
        in_specs=[tile(step, width), tile(step, width), tile(step, rates.shape[1]), fixed(weights.shape)],
        out_specs=fixed(weights.shape),
        scratch_shapes=[pltpu.VMEM(weights.shape, jnp.float32)],
        name="token_grads",
    )(keys, values, rates, weights)


def apply(queries, weights):
    rows, width = queries.shape
    step = math.gcd(rows, 512)
    return pl.pallas_call(
        apply_kernel,
        grid=(rows // step,),
        out_shape=(
            jax.ShapeDtypeStruct((rows, width), jnp.bfloat16),
            jax.ShapeDtypeStruct((rows, 1), jnp.float32),
        ),
        in_specs=[tile(step, width), fixed(weights.shape)],
        out_specs=(tile(step, width), tile(step, 1)),
        name="apply_weights",
    )(queries, weights)


def fits(n, rows, units, heads, width):
    inner = inner_size(n)
    return (
        inner == 2
        and n // inner >= 2
        and units % 8 == 0
        and heads % 2 == 0
        and heads <= 8
        and width % 128 == 64
        and rows % 512 == 0
        and rows * heads * width <= 2048 * 1280
        and (n // inner, heads, rows // 512) in ORDERS
    )


class Plan:
    def __init__(self, n, peers, rows, units, heads, width, width_all):
        self.n, self.peers, self.rows, self.units = n, peers, rows, units
        self.heads, self.width, self.width_all = heads, width, width_all
        self.inner = 2
        self.outer = n // 2
        self.step = 512
        self.window = width + 64
        self.packed = 2 * width + self.window
        self.starts = (0, width - 64, 2 * width)
        self.shifts = (0, 64, 0)

    def columns(self, h):
        start = (h // 2) * 2 * self.width + (h % 2) * (self.width - 64)
        return slice(start, start + self.window)

    def move(self, x, old, new):
        size = x.shape[1]
        if old != new:
            x = pltpu.roll(x, (new - old) % size, 1)
        lane = lax.broadcasted_iota(jnp.int32, x.shape, 1)
        return jnp.where((lane >= new) & (lane < new + self.width), x, 0.0)

    def pack(self, gate, up, down):
        first = self.width - 64
        shared = gate[:, first:] + up[:, :128]
        return jnp.concatenate([gate[:, :first], shared, up[:, 128:], down], axis=1)


def fused_kernel(
    plan, key_hbm, value_hbm, query_hbm, rate_ref, gate_ref, up_ref, down_ref,
    outs, row_out, fresh_ref,
    keys, values, rate, old, new, own, ups, downs, side, updated, weights, acc,
    squares_old, squares, row, rows_in,
    load_sem,
    line_send, line_recv, cross_send, cross_recv, pass_send, pass_recv,
    part_send, part_recv, side_send, side_recv, row_send, row_recv,
):
    f32, b16 = jnp.float32, jnp.bfloat16
    n, outer, heads, units, width = plan.n, plan.outer, plan.heads, plan.units, plan.width
    window, step, tokens = plan.window, plan.step, plan.rows
    me = lax.axis_index("ctx")
    z, x = me // 2, lax.rem(me, 2)
    mine = lax.axis_index("head")
    other = z * 2 + 1 - x

    half = 2 * width

    def load(i, p):
        cut = slice(p * half, (p + 1) * half)
        src, dst = ((key_hbm, keys), (value_hbm, values), (query_hbm, keys))[i]
        return pltpu.make_async_copy(src.at[:, cut], dst.at[:, cut], load_sem.at[i, p])

    for p in range(heads // 2):
        load(0, p).start()
        load(1, p).start()

    barrier = pltpu.get_barrier_semaphore()
    pl.semaphore_signal(barrier, inc=1, device_id={"ctx": other})
    for t in range(1, plan.peers):
        pl.semaphore_signal(barrier, inc=1, device_id={"head": lax.rem(mine + t, plan.peers)})

    hops = sorted({1, outer - 1})
    for t in hops:
        pl.semaphore_signal(barrier, inc=1, device_id={"ctx": lax.rem(z + t, outer) * 2 + x})

    def pack_own(h):
        parts = []
        for j, ref in enumerate((gate_ref, up_ref, down_ref)):
            piece = ref[:, h, :].astype(f32)
            piece = jnp.concatenate([piece, jnp.zeros((units, 64), f32)], axis=1)
            parts.append(plan.move(piece, 0, plan.shifts[j]))
        old[h, me] = plan.pack(*parts).astype(b16)

    pack_own(0)
    pl.semaphore_wait(barrier, plan.peers + len(hops))

    sends = []
    side_first, passing, order = ORDERS[outer, heads, tokens // step]

    def send(when, make):
        def start():
            make().start()

        def finish():
            make().wait_send()

        if when is None:
            start()
            sends.append(finish)
        else:
            pl.when(when())(start)
            sends.append(lambda: pl.when(when())(finish))

    def line_copy(g, h, origin, up):
        buf = (old, new)[g]
        block = origin * 2 + x
        return pltpu.make_async_remote_copy(
            src_ref=buf.at[h, block], dst_ref=buf.at[h, block],
            send_sem=line_send.at[g, h, up, origin], recv_sem=line_recv.at[g, h, origin],
            device_id={"ctx": me + (2 if up else -2)},
        )

    def cross_copy(g, h, origin):
        buf = (old, new)[g]
        block = origin * 2 + x
        return pltpu.make_async_remote_copy(
            src_ref=buf.at[h, block], dst_ref=buf.at[h, block],
            send_sem=cross_send.at[g, h, origin], recv_sem=cross_recv.at[g, h, origin],
            device_id={"ctx": other},
        )

    def issue(g, h):
        if g == 0 and h > 0:
            pack_own(h)
        send(lambda: z < outer - 1, lambda: line_copy(g, h, z, 1))
        send(lambda: z > 0, lambda: line_copy(g, h, z, 0))
        send(None, lambda: cross_copy(g, h, z))

    def relay(g, h, d):
        whole = d > 1 or not passing[g][h]

        @pl.when(z >= d)
        def _():
            line_copy(g, h, z - d, 1).wait_recv()

        send(lambda: (z >= d) & (z < outer - 1), lambda: line_copy(g, h, z - d, 1))
        if whole:
            send(lambda: z >= d, lambda: cross_copy(g, h, z - d))

        @pl.when(z + d < outer)
        def _():
            line_copy(g, h, z + d, 0).wait_recv()

        send(lambda: (z + d < outer) & (z > 0), lambda: line_copy(g, h, z + d, 0))
        if whole:
            send(lambda: z + d < outer, lambda: cross_copy(g, h, z + d))

    def pass_copy(g, h, up):
        buf = (old, new)[g]
        return pltpu.make_async_remote_copy(
            src_ref=buf.at[h, other], dst_ref=buf.at[h, other],
            send_sem=pass_send.at[g, h, up], recv_sem=pass_recv.at[g, h, up],
            device_id={"ctx": me + (2 if up else -2)},
        )

    def cross(g, h):
        cross_copy(g, h, z).wait_recv()
        send(lambda: z < outer - 1, lambda: pass_copy(g, h, 1))
        send(lambda: z > 0, lambda: pass_copy(g, h, 0))

    def arrived(g, h):
        if not passing[g][h]:
            for o in range(outer):
                cross_copy(g, h, o).wait_recv()
            return
        for o in range(outer):
            pl.when((o > z + 1) | (o < z - 1))(lambda: cross_copy(g, h, o).wait_recv())
        pl.when(z > 0)(lambda: pass_copy(g, h, 1).wait_recv())
        pl.when(z < outer - 1)(lambda: pass_copy(g, h, 0).wait_recv())

    def part_copy(h, up, to):
        buf = (downs, ups)[up]
        first, count = (to * 2 + x, 1) if side_first[h] else (to * 2, 2)
        return pltpu.make_async_remote_copy(
            src_ref=own.at[h, pl.ds(first, count)], dst_ref=buf.at[h, to, pl.ds(0, count)],
            send_sem=part_send.at[h, up, to], recv_sem=part_recv.at[h, up, to],
            device_id={"ctx": me + (2 if up else -2)},
        )

    def add_part(h, up, to):
        buf = (downs, ups)[up]
        part_copy(h, up, to).wait_recv()
        for c in range(1 if side_first[h] else 2):
            block = to * 2 + (x if side_first[h] else c)
            total = own[h, block].astype(f32) + buf[h, to, c].astype(f32)
            own[h, block] = total.astype(b16)

    def side_copy(h, to):
        return pltpu.make_async_remote_copy(
            src_ref=own.at[h, to * 2 + 1 - x], dst_ref=side.at[h, to if side_first[h] else 0],
            send_sem=side_send.at[h, to], recv_sem=side_recv.at[h, to],
            device_id={"ctx": other},
        )

    def reduce_start(h):
        if side_first[h]:
            for i in range(outer):
                send(None, functools.partial(side_copy, h, i // 2 if i % 2 else outer - 1 - i // 2))
            return
        for to in range(outer - 1, 0, -1):
            send(lambda: z == 0, functools.partial(part_copy, h, 1, to))
            send(lambda: z == outer - 1, functools.partial(part_copy, h, 0, outer - 1 - to))

    def reduce_beside(h, to):
        side_copy(h, to).wait_recv()
        total = own[h, to * 2 + x].astype(f32) + side[h, to].astype(f32)
        own[h, to * 2 + x] = total.astype(b16)
        if to > 0:
            send(lambda: z == 0, lambda: part_copy(h, 1, to))
        if to < outer - 1:
            send(lambda: z == outer - 1, lambda: part_copy(h, 0, to))

    def reduce_relay(h, to, d):
        back = outer - 1 - to

        @pl.when(z == d)
        def _():
            add_part(h, 1, to)

        send(lambda: z == d, lambda: part_copy(h, 1, to))

        @pl.when(z == outer - 1 - d)
        def _():
            add_part(h, 0, back)

        send(lambda: z == outer - 1 - d, lambda: part_copy(h, 0, back))

    def reduce_end(h):
        @pl.when(z > 0)
        def _():
            add_part(h, 1, z)

        @pl.when(z < outer - 1)
        def _():
            add_part(h, 0, z)

        if not side_first[h]:
            send(None, lambda: side_copy(h, z))

    def renew(h):
        total = own[h, me].astype(f32) + old[h, me].astype(f32)
        if not side_first[h]:
            side_copy(h, z).wait_recv()
            total = total + side[h, 0].astype(f32)
        updated[h] = total
        new[h, me] = total.astype(b16)
        issue(1, h)

    def pieces(g, h, j):
        buf = (old, new)[g]
        start, shift = plan.starts[j], plan.shifts[j]
        for b in range(n):
            piece = buf[h, b, :, start : start + window].astype(f32)
            yield b, plan.move(piece, shift, 64 * (h % 2))

    def prepare_old(h):
        for j in range(3):
            total = jnp.zeros((1, window), f32)
            for b, piece in pieces(0, h, j):
                weights[j, b * units : (b + 1) * units] = piece.astype(b16)
                total = total + jnp.sum(piece * piece, axis=0, keepdims=True)
            squares_old[3 * h + j : 3 * h + j + 1, :] = total

    def prepare_new(h):
        for j in range(3):
            total = jnp.zeros((1, window), f32)
            for b, piece in pieces(1, h, j):
                total = total + jnp.sum(piece * piece, axis=0, keepdims=True)
            scale = jnp.sqrt(squares_old[3 * h + j : 3 * h + j + 1, :]) * lax.rsqrt(total + EPS)
            for b, piece in pieces(1, h, j):
                weights[j, b * units : (b + 1) * units] = (piece * scale).astype(b16)
            start, shift = plan.starts[j], plan.shifts[j]
            exact = plan.move(updated[h, :, start : start + window], shift, 64 * (h % 2)) * scale
            fresh_ref[j, h] = plan.move(exact, 64 * (h % 2), 0)[:, :width].astype(b16)

    def at_steps(i, slots):
        for k, events in sorted(slots.items()):
            @pl.when(i == k)
            def _():
                for event in events:
                    event()

    def grads(h, slots):
        for j in range(3):
            acc[j] = jnp.zeros(acc.shape[1:], f32)
        cut = plan.columns(h)

        def body(i, _):
            at_steps(i, slots)
            span = pl.ds(pl.multiple_of(i * step, step), step)
            key = keys[span, cut]
            scaled = (values[span, cut].astype(f32) * rate[span, h : h + 1]).astype(b16)
            gpre = dot(weights[0], key, 1, 1)
            upre = dot(weights[1], key, 1, 1)
            back = dot(weights[2], scaled, 1, 1)
            sig = jax.nn.sigmoid(gpre)
            act = gpre * sig
            slope = sig * (1.0 + gpre * (1.0 - sig))
            acc[0] += dot((back * upre * slope).astype(b16), key, 1, 0)
            acc[1] += dot((back * act).astype(b16), key, 1, 0)
            acc[2] += dot((act * upre).astype(b16), scaled, 1, 0)
            return 0

        lax.fori_loop(0, tokens // step, body, 0)

    def start(h):
        if h % 2:
            load(2, h // 2).start()
        shift = 64 * (h % 2)
        for b in range(n):
            parts = [
                plan.move(acc[j, b * units : (b + 1) * units], shift, plan.shifts[j]) for j in range(3)
            ]
            own[h, b] = plan.pack(*parts).astype(b16)
        reduce_start(h)

    def apply_head(h, slots):
        cut = plan.columns(h)

        def body(i, _):
            at_steps(i, slots)
            span = pl.ds(pl.multiple_of(i * step, step), step)
            query = keys[span, cut]
            gate = dot(query, weights[0], 1, 1)
            up = dot(query, weights[1], 1, 1)
            mixed = (jax.nn.silu(gate) * up).astype(b16)
            out = dot(mixed, weights[2], 1, 0)
            if h % 2:
                shared = slice(cut.start, cut.start + 128)
                outs[span, shared] = outs[span, shared] + out[:, :128]
                outs[span, cut.start + 128 : cut.stop] = out[:, 128:]
            else:
                outs[span, cut] = out
            part = out * out
            total = part[:, :128]
            for c in range(128, window, 128):
                total = total + part[:, c : c + 128]
            if h > 0:
                total = squares[span, :] + total
            if h < heads - 1:
                squares[span, :] = total
            else:
                row[:, span] = jnp.sum(total.T, axis=0, keepdims=True)
            return 0

        lax.fori_loop(0, tokens // step, body, 0)

    def ready(g, h):
        if h % 2 == 0:
            for i in (2,) if g else (0, 1):
                load(i, h // 2).wait()
        arrived(g, h)
        (prepare_new if g else prepare_old)(h)

    handlers = {
        ISSUE: issue, RELAY: relay, CROSS: cross, READY: ready, START: start, SIDE: reduce_beside,
        PART: reduce_relay, END: reduce_end, FINISH: renew,
    }
    def turn_rates():
        turned = rate_ref[...]
        if heads < 8:
            turned = jnp.concatenate([turned, jnp.zeros((8 - heads, tokens), f32)], axis=0)
        rate[...] = turned.T

    order = list(order)
    while order:
        event = order.pop(0)
        if event == (RELAY, 0, 0, 1):
            turn_rates()
        if event[0] != READY:
            handlers[event[0]](*event[1:])
            continue
        ready(*event[1:])
        slots = {}
        for k in range(tokens // step):
            while order[0][0] != STEP:
                kind, *rest = order.pop(0)
                slots.setdefault(k, []).append(functools.partial(handlers[kind], *rest))
            order.pop(0)
        (apply_head if event[1] else grads)(event[2], slots)

    def row_copy(t):
        return pltpu.make_async_remote_copy(
            src_ref=row, dst_ref=rows_in.at[t - 1],
            send_sem=row_send.at[t - 1], recv_sem=row_recv.at[t - 1],
            device_id={"head": lax.rem(mine + t, plan.peers)},
        )

    for t in range(1, plan.peers):
        send(None, functools.partial(row_copy, t))
    total = row[...]
    for t in range(1, plan.peers):
        row_copy(t).wait_recv()
        total = total + rows_in[t - 1]
    row_out[...] = lax.rsqrt(total / plan.width_all + EPS)
    for done in sends:
        done()


def finish_kernel(step, outs_ref, row_ref, gain_ref, fresh_ref, out_hbm, gate_ref, up_ref, down_ref, staged, sem):
    tokens, width = outs_ref.shape

    def store(i):
        span = pl.ds(i * step, step)
        return pltpu.make_async_copy(staged.at[span], out_hbm.at[span], sem.at[i])

    for i in range(tokens // step):
        span = slice(i * step, (i + 1) * step)
        scale = jnp.broadcast_to(row_ref[:, span], (128, step)).T
        for c in range(0, width, 128):
            cut = slice(c, c + 128)
            staged[span, cut] = (outs_ref[span, cut] * scale * gain_ref[cut][None]).astype(staged.dtype)
        store(i).start()
    for j, ref in enumerate((gate_ref, up_ref, down_ref)):
        heads = [fresh_ref[j, h].astype(jnp.float32) for h in range(fresh_ref.shape[1])]
        ref[...] = jnp.stack(heads, axis=1).astype(ref.dtype)
    for i in range(tokens // step):
        store(i).wait()


def finish(outs, row, gain, fresh):
    rows, width = outs.shape
    units, heads = fresh.shape[2], fresh.shape[1]
    weight = jax.ShapeDtypeStruct((units, heads, fresh.shape[3]), fresh.dtype)
    step = 256
    return pl.pallas_call(
        functools.partial(finish_kernel, step),
        out_shape=(jax.ShapeDtypeStruct(outs.shape, jnp.bfloat16),) + (weight,) * 3,
        in_specs=vmem(4),
        out_specs=(pl.BlockSpec(memory_space=pl.ANY),) + tuple(vmem(3)),
        scratch_shapes=[
            pltpu.VMEM(outs.shape, jnp.bfloat16),
            pltpu.SemaphoreType.DMA((rows // step,)),
        ],
        compiler_params=pltpu.CompilerParams(vmem_limit_bytes=32 * 1024 * 1024),
        name="finish_rows",
    )(outs, row, gain, fresh)


def fused(n, peers, width_all, keys, values, queries, rates, w_gate, w_up, w_down):
    rows = keys.shape[0]
    units, heads, width = w_gate.shape
    plan = Plan(n, peers, rows, units, heads, width, width_all)
    f32, b16 = jnp.float32, jnp.bfloat16
    outer = plan.outer
    hbm = pl.BlockSpec(memory_space=pl.ANY)
    block = (units, plan.packed)
    dma = pltpu.SemaphoreType.DMA
    return pl.pallas_call(
        functools.partial(fused_kernel, plan),
        out_shape=(
            pltpu.VMEM(keys.shape, f32),
            pltpu.VMEM((1, rows), f32),
            pltpu.VMEM((3, heads, units, width), b16),
        ),
        in_specs=[hbm] * 3 + vmem(4),
        out_specs=tuple(vmem(3)),
        scratch_shapes=[
            pltpu.VMEM(keys.shape, b16),
            pltpu.VMEM(keys.shape, b16),
            pltpu.VMEM((rows, 8), f32),
            pltpu.VMEM((heads, n) + block, b16),
            pltpu.VMEM((heads, n) + block, b16),
            pltpu.VMEM((heads, n) + block, b16),
            pltpu.VMEM((heads, outer, 2) + block, b16),
            pltpu.VMEM((heads, outer, 2) + block, b16),
            pltpu.VMEM((heads, outer) + block, b16),
            pltpu.VMEM((heads,) + block, f32),
            pltpu.VMEM((3, n * units, plan.window), b16),
            pltpu.VMEM((3, n * units, plan.window), f32),
            pltpu.VMEM((3 * heads, plan.window), f32),
            pltpu.VMEM((rows, 128), f32),
            pltpu.VMEM((1, rows), f32),
            pltpu.VMEM((peers - 1, 1, rows), f32),
            dma((3, heads // 2)),
            dma((2, heads, 2, outer)),
            dma((2, heads, outer)),
            dma((2, heads, outer)),
            dma((2, heads, outer)),
            dma((2, heads, 2)),
            dma((2, heads, 2)),
            dma((heads, 2, outer)),
            dma((heads, 2, outer)),
            dma((heads, outer)),
            dma((heads, outer)),
            dma((peers - 1,)),
            dma((peers - 1,)),
        ],
        compiler_params=pltpu.CompilerParams(
            collective_id=2, has_side_effects=True, vmem_limit_bytes=VMEM_LIMIT
        ),
        name="fused_layer",
    )(keys, values, queries, rates.T, w_gate, w_up, w_down)


def per_device(n, peers, width_all, keys, values, queries, rates, w_gate, w_up, w_down, gain):
    rows = keys.shape[0]
    units, heads, width = w_gate.shape
    f32 = jnp.float32
    if fits(n, rows, units, heads, width):
        outs, row, fresh = fused(
            n, peers, width_all, keys, values, queries, rates, w_gate, w_up, w_down
        )
        return finish(outs, row, gain, fresh)
    own = jnp.stack([w_gate, w_up, w_down]).transpose(0, 2, 1, 3)
    own = own.reshape(3 * heads, units, width)
    full = gather(own, n).transpose(1, 3, 0, 2)
    full = full.reshape(3, heads, width, n * units)
    grads = token_grads(keys, values, rates, full)
    block = (n, 3 * heads * width // n, n * units)
    old = lax.dynamic_index_in_dim(full.reshape(block), lax.axis_index("ctx"), 0, keepdims=False)
    fresh = update(grads.reshape(block), old, n).reshape(full.shape)
    mine = lax.dynamic_slice_in_dim(fresh, lax.axis_index("ctx") * units, units, 3)
    mine = mine.transpose(0, 3, 1, 2)
    outs, squares = apply(queries, fresh)
    squares = lax.psum(squares.reshape(rows), "head")
    scale = lax.rsqrt(squares / width_all + EPS)
    output = (outs.astype(f32) * scale[:, None] * gain[None]).astype(jnp.bfloat16)
    return (output, mine[0], mine[1], mine[2])


def solution(mesh):
    weight = P("ctx", "head", None)
    token = P("ctx", "head")

    def whole(keys, *rest):
        body = functools.partial(
            per_device, mesh.shape["ctx"], mesh.shape["head"], keys.shape[1]
        )
        return jax.shard_map(
            body,
            mesh=mesh,
            in_specs=(token,) * 4 + (weight,) * 3 + (P("head"),),
            out_specs=(token, weight, weight, weight),
            check_vma=False,
        )(keys, *rest)

    return whole
```

```python
import functools
import math

import jax
import jax.numpy as jnp
from jax import lax
from jax.experimental import pallas as pl
from jax.experimental.pallas import tpu as pltpu
from jax.sharding import PartitionSpec as P

EPS = 1e-06

VMEM_LIMIT = 50 * 1024 * 1024
STEPS = (1024, 1024)
ISSUE, RELAY, CROSS, READY, STEP, START, SIDE, PART, END, FINISH = range(10)
ORDERS = {
    (4, 4, 2048): (
        ((0, 0), (0, 1), (1, 1), (1, 1)),
        (((0, 1), (0, 1), (0, 1), (0, 1)), ((0, 1), (0, 1), (0, 1), (2, 2))),
        (
            (ISSUE, 0, 0, 0), (ISSUE, 0, 0, 1), (ISSUE, 0, 1, 0), (ISSUE, 0, 1, 1),
            (RELAY, 0, 0, 0, 1), (RELAY, 0, 0, 1, 1), (RELAY, 0, 1, 0, 1), (CROSS, 0, 0, 1),
            (RELAY, 0, 0, 0, 2), (RELAY, 0, 0, 1, 2), (RELAY, 0, 1, 1, 1), (ISSUE, 0, 2, 0),
            (ISSUE, 0, 2, 1), (CROSS, 0, 1, 1), (RELAY, 0, 0, 0, 3), (RELAY, 0, 0, 1, 3),
            (RELAY, 0, 1, 1, 2), (RELAY, 0, 1, 0, 2), (ISSUE, 0, 3, 0), (ISSUE, 0, 3, 1),
            (READY, 0, 0), (RELAY, 0, 2, 0, 1), (STEP, 0, 0, 0), (RELAY, 0, 1, 1, 3),
            (RELAY, 0, 1, 0, 3), (RELAY, 0, 2, 1, 1), (CROSS, 0, 2, 1), (STEP, 0, 0, 1),
            (CROSS, 0, 3, 1), (START, 0), (RELAY, 0, 2, 0, 2), (RELAY, 0, 2, 1, 2),
            (RELAY, 0, 3, 0, 1), (READY, 0, 1), (STEP, 0, 1, 0), (RELAY, 0, 2, 0, 3),
            (RELAY, 0, 2, 1, 3), (STEP, 0, 1, 1), (RELAY, 0, 3, 0, 2), (RELAY, 0, 3, 0, 3),
            (RELAY, 0, 3, 1, 1), (START, 1), (READY, 0, 2), (STEP, 0, 2, 0), (RELAY, 0, 3, 1, 2),
            (RELAY, 0, 3, 1, 3), (PART, 0, 0, 3, 1), (PART, 0, 0, 2, 1), (STEP, 0, 2, 1),
            (START, 2), (SIDE, 1, 1, 1), (PART, 0, 1, 3, 1), (SIDE, 1, 1, 2), (SIDE, 1, 1, 3),
            (PART, 0, 0, 3, 2), (SIDE, 1, 1, 0), (PART, 0, 1, 2, 1), (READY, 0, 3),
            (STEP, 0, 3, 0), (PART, 0, 1, 3, 2), (SIDE, 2, 0, 3), (END, 0, 0), (SIDE, 2, 0, 2),
            (SIDE, 2, 0, 0), (END, 0, 1), (SIDE, 2, 0, 1), (PART, 1, 0, 3, 1), (PART, 1, 0, 2, 1),
            (STEP, 0, 3, 1), (START, 3), (PART, 1, 1, 3, 1), (FINISH, 0, 0), (FINISH, 0, 1),
            (SIDE, 2, 1, 2), (PART, 1, 1, 2, 1), (SIDE, 2, 1, 0), (PART, 1, 0, 3, 2),
            (PART, 2, 0, 3, 1), (PART, 2, 0, 2, 1), (SIDE, 2, 1, 3), (SIDE, 2, 1, 1),
            (PART, 1, 1, 3, 2), (END, 1, 0), (RELAY, 1, 0, 0, 1), (RELAY, 1, 0, 1, 1),
            (SIDE, 3, 0, 3), (END, 1, 1), (FINISH, 1, 1), (SIDE, 3, 0, 0), (PART, 2, 0, 3, 2),
            (SIDE, 3, 1, 0), (SIDE, 3, 0, 1), (SIDE, 3, 1, 3), (RELAY, 1, 0, 0, 2),
            (RELAY, 1, 0, 0, 3), (PART, 2, 1, 3, 1), (SIDE, 3, 0, 2), (PART, 2, 1, 2, 1),
            (RELAY, 1, 0, 1, 2), (END, 2, 0), (FINISH, 2, 0), (SIDE, 3, 1, 2), (RELAY, 1, 1, 1, 1),
            (FINISH, 1, 0), (RELAY, 1, 0, 1, 3), (PART, 3, 0, 3, 1), (PART, 2, 1, 3, 2),
            (END, 2, 1), (FINISH, 2, 1), (RELAY, 1, 1, 1, 2), (PART, 3, 1, 3, 1),
            (RELAY, 1, 2, 0, 1), (PART, 3, 0, 3, 2), (PART, 3, 0, 2, 1), (RELAY, 1, 1, 0, 1),
            (SIDE, 3, 1, 1), (PART, 3, 1, 3, 2), (CROSS, 1, 0, 1), (RELAY, 1, 2, 1, 1),
            (PART, 3, 1, 2, 1), (RELAY, 1, 2, 0, 2), (END, 3, 0), (RELAY, 1, 1, 0, 2),
            (FINISH, 3, 0), (RELAY, 1, 2, 1, 2), (RELAY, 1, 1, 0, 3), (RELAY, 1, 1, 1, 3),
            (CROSS, 1, 1, 1), (END, 3, 1), (FINISH, 3, 1), (READY, 1, 0), (STEP, 1, 0, 0),
            (RELAY, 1, 2, 0, 3), (RELAY, 1, 3, 0, 1), (RELAY, 1, 3, 0, 2), (CROSS, 1, 2, 1),
            (RELAY, 1, 2, 1, 3), (STEP, 1, 0, 1), (READY, 1, 1), (RELAY, 1, 3, 0, 3),
            (STEP, 1, 1, 0), (RELAY, 1, 3, 1, 1), (RELAY, 1, 3, 1, 2), (RELAY, 1, 3, 1, 3),
            (STEP, 1, 1, 1), (READY, 1, 2), (STEP, 1, 2, 0), (STEP, 1, 2, 1), (READY, 1, 3),
            (STEP, 1, 3, 0), (STEP, 1, 3, 1),
        ),
    ),
}


def inner_size(n):
    inner = 1
    while inner * inner * 4 <= n and n % (inner * 2) == 0:
        inner *= 2
    return inner if inner > 1 or n % 2 else 2


def place(n, inner):
    me = lax.axis_index("ctx")
    return me, me // inner, lax.rem(me, inner), n // inner


def greet(z, x, outer, inner):
    barrier = pltpu.get_barrier_semaphore()
    for s in range(1, outer):
        pl.semaphore_signal(barrier, inc=1, device_id={"ctx": lax.rem(z + s, outer) * inner + x})
    for t in range(1, inner):
        pl.semaphore_signal(barrier, inc=1, device_id={"ctx": z * inner + lax.rem(x + t, inner)})
    pl.semaphore_wait(barrier, outer + inner - 2)


def spread(z, x, outer, inner, own_ref, out_ref, send_sem, recv_sem):
    me = z * inner + x
    copies = {}

    def send(src, block, device, s, t):
        copy = pltpu.make_async_remote_copy(
            src_ref=src,
            dst_ref=out_ref.at[block],
            send_sem=send_sem.at[s, t],
            recv_sem=recv_sem.at[s, t],
            device_id={"ctx": device},
        )
        copy.start()
        copies[s, t] = copy

    for s in range(1, outer):
        send(own_ref, me, lax.rem(z + s, outer) * inner + x, s, 0)
    for t in range(1, inner):
        send(own_ref, me, z * inner + lax.rem(x + t, inner), 0, t)
    for s in range(1, outer):
        copies[s, 0].wait_recv()
        block = lax.rem(z + outer - s, outer) * inner + x
        for t in range(1, inner):
            send(out_ref.at[block], block, z * inner + lax.rem(x + t, inner), s, t)
    for (s, t), copy in copies.items():
        if t:
            copy.wait_recv()
    for copy in copies.values():
        copy.wait_send()


def gather_kernel(n, inner, own_ref, out_ref, local_sem, send_sem, recv_sem):
    me, z, x, outer = place(n, inner)
    greet(z, x, outer, inner)
    keep = pltpu.make_async_copy(own_ref, out_ref.at[me], local_sem)
    keep.start()
    spread(z, x, outer, inner, own_ref, out_ref, send_sem, recv_sem)
    keep.wait()


def update_kernel(
    n, inner, grad_ref, old_ref, out_ref, near, part, far, fresh,
    local_sem, near_send, near_recv, far_send, far_recv, send_sem, recv_sem,
):
    me, z, x, outer = place(n, inner)
    greet(z, x, outer, inner)
    order = list(range(1, outer)) + [0]
    first = {}
    for s in order:
        row = lax.rem(z + s, outer) * inner
        for t in range(1, inner):
            column = lax.rem(x + t, inner)
            copy = pltpu.make_async_remote_copy(
                src_ref=grad_ref.at[row + column],
                dst_ref=near.at[s, t - 1],
                send_sem=near_send.at[s, t],
                recv_sem=near_recv.at[s, t],
                device_id={"ctx": z * inner + column},
            )
            copy.start()
            first[s, t] = copy
    second = {}
    total = None
    for s in order:
        row = lax.rem(z + s, outer) * inner
        total = grad_ref[row + x].astype(jnp.float32)
        for t in range(1, inner):
            first[s, t].wait_recv()
            total = total + near[s, t - 1].astype(jnp.float32)
        if s:
            part[s] = total.astype(part.dtype)
            copy = pltpu.make_async_remote_copy(
                src_ref=part.at[s],
                dst_ref=far.at[s],
                send_sem=far_send.at[s],
                recv_sem=far_recv.at[s],
                device_id={"ctx": row + x},
            )
            copy.start()
            second[s] = copy
    for s, copy in second.items():
        copy.wait_recv()
        total = total + far[s].astype(jnp.float32)
    old = old_ref[...].astype(jnp.float32)
    updated = old + total
    old_sq = jnp.sum(old * old, axis=1, keepdims=True)
    new_sq = jnp.sum(updated * updated, axis=1, keepdims=True)
    fresh[...] = (updated * (jnp.sqrt(old_sq) * lax.rsqrt(new_sq + EPS))).astype(fresh.dtype)
    keep = pltpu.make_async_copy(fresh, out_ref.at[me], local_sem)
    keep.start()
    keep.wait()
    spread(z, x, outer, inner, out_ref.at[me], out_ref, send_sem, recv_sem)
    for copy in first.values():
        copy.wait_send()
    for copy in second.values():
        copy.wait_send()


def vmem(count):
    return [pl.BlockSpec(memory_space=pltpu.VMEM)] * count


def gather(own, n):
    inner = inner_size(n)
    outer = n // inner
    return pl.pallas_call(
        functools.partial(gather_kernel, n, inner),
        out_shape=jax.ShapeDtypeStruct((n,) + own.shape, own.dtype),
        in_specs=vmem(1),
        out_specs=vmem(1)[0],
        scratch_shapes=[pltpu.SemaphoreType.DMA]
        + [pltpu.SemaphoreType.DMA((outer, inner))] * 2,
        compiler_params=pltpu.CompilerParams(collective_id=0, has_side_effects=True),
        name="gather_weights",
    )(own)


def update(grads, old, n):
    inner = inner_size(n)
    outer = n // inner
    block = grads.shape[1:]
    return pl.pallas_call(
        functools.partial(update_kernel, n, inner),
        out_shape=jax.ShapeDtypeStruct(grads.shape, grads.dtype),
        in_specs=vmem(2),
        out_specs=vmem(1)[0],
        scratch_shapes=[
            pltpu.VMEM((outer, max(inner - 1, 1)) + block, grads.dtype),
            pltpu.VMEM((outer,) + block, grads.dtype),
            pltpu.VMEM((outer,) + block, grads.dtype),
            pltpu.VMEM(block, grads.dtype),
            pltpu.SemaphoreType.DMA,
        ]
        + [pltpu.SemaphoreType.DMA((outer, inner))] * 2
        + [pltpu.SemaphoreType.DMA((outer,))] * 2
        + [pltpu.SemaphoreType.DMA((outer, inner))] * 2,
        compiler_params=pltpu.CompilerParams(collective_id=1, has_side_effects=True),
        name="update_weights",
    )(grads, old)


def dot(a, b, left, right):
    return lax.dot_general(a, b, (((left,), (right,)), ((), ())), preferred_element_type=jnp.float32)


def grads_kernel(key_ref, value_ref, rate_ref, weight_ref, out_ref, acc):
    step = pl.program_id(0)

    @pl.when(step == 0)
    def _():
        acc[...] = jnp.zeros_like(acc)

    heads, width = weight_ref.shape[1:3]
    for h in range(heads):
        columns = slice(h * width, (h + 1) * width)
        key = key_ref[:, columns]
        gpre = dot(key, weight_ref[0, h], 1, 0)
        upre = dot(key, weight_ref[1, h], 1, 0)
        scaled = (value_ref[:, columns].astype(jnp.float32) * rate_ref[:, h : h + 1]).astype(jnp.bfloat16)
        back = dot(scaled, weight_ref[2, h], 1, 0)
        sig = jax.nn.sigmoid(gpre)
        act = gpre * sig
        slope = sig * (1.0 + gpre * (1.0 - sig))
        acc[0, h] += dot(key, (back * upre * slope).astype(jnp.bfloat16), 0, 0)
        acc[1, h] += dot(key, (back * act).astype(jnp.bfloat16), 0, 0)
        acc[2, h] += dot(scaled, (act * upre).astype(jnp.bfloat16), 0, 0)

    @pl.when(step == pl.num_programs(0) - 1)
    def _():
        out_ref[...] = acc[...].astype(out_ref.dtype)


def apply_kernel(query_ref, weight_ref, out_ref, square_ref):
    heads, width = weight_ref.shape[1:3]
    squares = None
    for h in range(heads):
        columns = slice(h * width, (h + 1) * width)
        query = query_ref[:, columns]
        gate = dot(query, weight_ref[0, h], 1, 0)
        up = dot(query, weight_ref[1, h], 1, 0)
        mixed = (jax.nn.silu(gate) * up).astype(jnp.bfloat16)
        out = dot(mixed, weight_ref[2, h], 1, 1)
        part = jnp.sum(out * out, axis=1, keepdims=True)
        squares = part if squares is None else squares + part
        out_ref[:, columns] = out.astype(out_ref.dtype)
    square_ref[...] = squares


def tile(rows, width):
    return pl.BlockSpec((rows, width), lambda i: (i, 0))


def fixed(shape):
    return pl.BlockSpec(shape, lambda i: (0,) * len(shape))


def token_grads(keys, values, rates, weights):
    rows, width = keys.shape
    step = math.gcd(rows, 512)
    return pl.pallas_call(
        grads_kernel,
        grid=(rows // step,),
        out_shape=jax.ShapeDtypeStruct(weights.shape, jnp.bfloat16),
        in_specs=[tile(step, width), tile(step, width), tile(step, rates.shape[1]), fixed(weights.shape)],
        out_specs=fixed(weights.shape),
        scratch_shapes=[pltpu.VMEM(weights.shape, jnp.float32)],
        name="token_grads",
    )(keys, values, rates, weights)


def apply(queries, weights):
    rows, width = queries.shape
    step = math.gcd(rows, 512)
    return pl.pallas_call(
        apply_kernel,
        grid=(rows // step,),
        out_shape=(
            jax.ShapeDtypeStruct((rows, width), jnp.bfloat16),
            jax.ShapeDtypeStruct((rows, 1), jnp.float32),
        ),
        in_specs=[tile(step, width), fixed(weights.shape)],
        out_specs=(tile(step, width), tile(step, 1)),
        name="apply_weights",
    )(queries, weights)


def fits(n, rows, units, heads, width):
    inner = inner_size(n)
    return (
        inner == 2
        and n // inner >= 2
        and units % 8 == 0
        and heads % 2 == 0
        and heads <= 8
        and width % 128 == 64
        and rows % max(STEPS) == 0
        and rows * heads * width <= 2048 * 1280
        and (n // inner, heads, rows) in ORDERS
    )


class Plan:
    def __init__(self, n, peers, rows, units, heads, width, width_all):
        self.n, self.peers, self.rows, self.units = n, peers, rows, units
        self.heads, self.width, self.width_all = heads, width, width_all
        self.inner = 2
        self.outer = n // 2
        self.step, self.long = STEPS
        self.window = width + 64
        self.packed = 2 * width + self.window
        self.starts = (0, width - 64, 2 * width)
        self.shifts = (0, 64, 0)

    def columns(self, h):
        start = (h // 2) * 2 * self.width + (h % 2) * (self.width - 64)
        return slice(start, start + self.window)

    def move(self, x, old, new):
        size = x.shape[1]
        if old != new:
            x = pltpu.roll(x, (new - old) % size, 1)
        lane = lax.broadcasted_iota(jnp.int32, x.shape, 1)
        return jnp.where((lane >= new) & (lane < new + self.width), x, 0.0)

    def pack(self, gate, up, down):
        first = self.width - 64
        shared = gate[:, first:] + up[:, :128]
        return jnp.concatenate([gate[:, :first], shared, up[:, 128:], down], axis=1)


def fused_kernel(
    plan, key_hbm, value_hbm, query_hbm, rate_ref, gate_ref, up_ref, down_ref,
    outs, row_out, fresh_ref,
    keys, values, rate, old, new, own, ups, downs, side, updated, weights, acc,
    squares_old, squares, row, rows_in,
    load_sem,
    line_send, line_recv, cross_send, cross_recv, pass_send, pass_recv,
    part_send, part_recv, side_send, side_recv, row_send, row_recv,
):
    f32, b16 = jnp.float32, jnp.bfloat16
    n, outer, heads, units, width = plan.n, plan.outer, plan.heads, plan.units, plan.width
    window, step, long, tokens = plan.window, plan.step, plan.long, plan.rows
    me = lax.axis_index("ctx")
    z, x = me // 2, lax.rem(me, 2)
    mine = lax.axis_index("head")
    other = z * 2 + 1 - x

    half = 2 * width

    def load(i, p):
        cut = slice(p * half, (p + 1) * half)
        src, dst = ((key_hbm, keys), (value_hbm, values), (query_hbm, keys))[i]
        return pltpu.make_async_copy(src.at[:, cut], dst.at[:, cut], load_sem.at[i, p])

    for p in range(heads // 2):
        load(0, p).start()
        load(1, p).start()

    barrier = pltpu.get_barrier_semaphore()
    pl.semaphore_signal(barrier, inc=1, device_id={"ctx": other})
    for t in range(1, plan.peers):
        pl.semaphore_signal(barrier, inc=1, device_id={"head": lax.rem(mine + t, plan.peers)})

    for t in range(1, outer):
        pl.semaphore_signal(barrier, inc=1, device_id={"ctx": lax.rem(z + t, outer) * 2 + x})

    def pack_own(h):
        parts = []
        for j, ref in enumerate((gate_ref, up_ref, down_ref)):
            piece = ref[:, h, :].astype(f32)
            piece = jnp.concatenate([piece, jnp.zeros((units, 64), f32)], axis=1)
            parts.append(plan.move(piece, 0, plan.shifts[j]))
        old[h, me] = plan.pack(*parts).astype(b16)

    pack_own(0)
    pl.semaphore_wait(barrier, plan.peers + outer - 1)

    sends = []
    side_first, passing, order = ORDERS[outer, heads, tokens]

    def send(when, make):
        def start():
            make().start()

        def finish():
            make().wait_send()

        if when is None:
            start()
            sends.append(finish)
        else:
            pl.when(when())(start)
            sends.append(lambda: pl.when(when())(finish))

    parts = 2
    share = plan.packed // parts
    lanes = lambda p: slice(p * share, (p + 1) * share)

    def line_copy(g, h, p, origin, up):
        buf = (old, new)[g]
        block = origin * 2 + x
        return pltpu.make_async_remote_copy(
            src_ref=buf.at[h, block, :, lanes(p)], dst_ref=buf.at[h, block, :, lanes(p)],
            send_sem=line_send.at[g, h * parts + p, up, origin], recv_sem=line_recv.at[g, h * parts + p, origin],
            device_id={"ctx": me + (2 if up else -2)},
        )

    def cross_copy(g, h, p, origin):
        buf = (old, new)[g]
        block = origin * 2 + x
        return pltpu.make_async_remote_copy(
            src_ref=buf.at[h, block, :, lanes(p)], dst_ref=buf.at[h, block, :, lanes(p)],
            send_sem=cross_send.at[g, h * parts + p, origin], recv_sem=cross_recv.at[g, h * parts + p, origin],
            device_id={"ctx": other},
        )

    def far_copy(g, h, p, to):
        buf = (old, new)[g]
        return pltpu.make_async_remote_copy(
            src_ref=buf.at[h, me, :, lanes(p)], dst_ref=buf.at[h, me, :, lanes(p)],
            send_sem=line_send.at[g, h * parts + p, 0, to], recv_sem=line_recv.at[g, h * parts + p, z],
            device_id={"ctx": to * 2 + x},
        )

    def issue(g, h, p):
        if g == 0 and h > 0 and p == 0:
            pack_own(h)
        if passing[g][h][p] > 1:
            for d in range(outer - 1, 0, -1):
                send(lambda d=d: z + d < outer, lambda d=d: far_copy(g, h, p, z + d))
                send(lambda d=d: z >= d, lambda d=d: far_copy(g, h, p, z - d))
            send(None, lambda: cross_copy(g, h, p, z))
            return
        send(lambda: z < outer - 1, lambda: line_copy(g, h, p, z, 1))
        send(lambda: z > 0, lambda: line_copy(g, h, p, z, 0))
        send(None, lambda: cross_copy(g, h, p, z))

    def relay(g, h, p, d):
        whole = d > 1 or not passing[g][h][p] & 1
        onward = passing[g][h][p] < 2

        @pl.when(z >= d)
        def _():
            line_copy(g, h, p, z - d, 1).wait_recv()

        if onward:
            send(lambda: (z >= d) & (z < outer - 1), lambda: line_copy(g, h, p, z - d, 1))
        if whole:
            send(lambda: z >= d, lambda: cross_copy(g, h, p, z - d))

        @pl.when(z + d < outer)
        def _():
            line_copy(g, h, p, z + d, 0).wait_recv()

        if onward:
            send(lambda: (z + d < outer) & (z > 0), lambda: line_copy(g, h, p, z + d, 0))
        if whole:
            send(lambda: z + d < outer, lambda: cross_copy(g, h, p, z + d))

    def pass_copy(g, h, p, up):
        buf = (old, new)[g]
        return pltpu.make_async_remote_copy(
            src_ref=buf.at[h, other, :, lanes(p)], dst_ref=buf.at[h, other, :, lanes(p)],
            send_sem=pass_send.at[g, h * parts + p, up], recv_sem=pass_recv.at[g, h * parts + p, up],
            device_id={"ctx": me + (2 if up else -2)},
        )

    def cross(g, h, p):
        cross_copy(g, h, p, z).wait_recv()
        send(lambda: z < outer - 1, lambda: pass_copy(g, h, p, 1))
        send(lambda: z > 0, lambda: pass_copy(g, h, p, 0))

    def arrived(g, h, p):
        if not passing[g][h][p] & 1:
            for o in range(outer):
                cross_copy(g, h, p, o).wait_recv()
            return
        for o in range(outer):
            pl.when((o > z + 1) | (o < z - 1))(lambda: cross_copy(g, h, p, o).wait_recv())
        pl.when(z > 0)(lambda: pass_copy(g, h, p, 1).wait_recv())
        pl.when(z < outer - 1)(lambda: pass_copy(g, h, p, 0).wait_recv())

    def part_copy(h, p, up, to):
        buf = (downs, ups)[up]
        first, count = (to * 2 + x, 1) if side_first[h][p] else (to * 2, 2)
        return pltpu.make_async_remote_copy(
            src_ref=own.at[h, pl.ds(first, count), :, lanes(p)], dst_ref=buf.at[h, to, pl.ds(0, count), :, lanes(p)],
            send_sem=part_send.at[h * parts + p, up, to], recv_sem=part_recv.at[h * parts + p, up, to],
            device_id={"ctx": me + (2 if up else -2)},
        )

    def add_part(h, p, up, to):
        buf = (downs, ups)[up]
        part_copy(h, p, up, to).wait_recv()
        for c in range(1 if side_first[h][p] else 2):
            block = to * 2 + (x if side_first[h][p] else c)
            total = own[h, block, :, lanes(p)].astype(f32) + buf[h, to, c, :, lanes(p)].astype(f32)
            own[h, block, :, lanes(p)] = total.astype(b16)

    def far_part(h, p, to, slot):
        return pltpu.make_async_remote_copy(
            src_ref=own.at[h, to * 2 + x, :, lanes(p)], dst_ref=ups.at[h, slot, 0, :, lanes(p)],
            send_sem=part_send.at[h * parts + p, 0, to], recv_sem=part_recv.at[h * parts + p, 1, slot],
            device_id={"ctx": to * 2 + x},
        )

    def side_copy(h, p, to):
        return pltpu.make_async_remote_copy(
            src_ref=own.at[h, to * 2 + 1 - x, :, lanes(p)], dst_ref=side.at[h, to if side_first[h][p] else 0, :, lanes(p)],
            send_sem=side_send.at[h * parts + p, to], recv_sem=side_recv.at[h * parts + p, to],
            device_id={"ctx": other},
        )

    def reduce_start(h, p):
        if side_first[h][p]:
            for i in range(outer):
                send(None, functools.partial(side_copy, h, p, i // 2 if i % 2 else outer - 1 - i // 2))
            return
        for to in range(outer - 1, 0, -1):
            send(lambda: z == 0, functools.partial(part_copy, h, p, 1, to))
            send(lambda: z == outer - 1, functools.partial(part_copy, h, p, 0, outer - 1 - to))

    def reduce_beside(h, p, to):
        side_copy(h, p, to).wait_recv()
        total = own[h, to * 2 + x, :, lanes(p)].astype(f32) + side[h, to, :, lanes(p)].astype(f32)
        own[h, to * 2 + x, :, lanes(p)] = total.astype(b16)
        if side_first[h][p] > 1:
            send(lambda: z != to, lambda: far_part(h, p, to, z))
            return
        if to > 0:
            send(lambda: z == 0, lambda: part_copy(h, p, 1, to))
        if to < outer - 1:
            send(lambda: z == outer - 1, lambda: part_copy(h, p, 0, to))

    def reduce_relay(h, p, to, d):
        back = outer - 1 - to

        @pl.when(z == d)
        def _():
            add_part(h, p, 1, to)

        send(lambda: z == d, lambda: part_copy(h, p, 1, to))

        @pl.when(z == outer - 1 - d)
        def _():
            add_part(h, p, 0, back)

        send(lambda: z == outer - 1 - d, lambda: part_copy(h, p, 0, back))

    def reduce_end(h, p):
        if side_first[h][p] > 1:
            total = own[h, me, :, lanes(p)].astype(f32)
            for d in range(1, outer):
                source = lax.rem(z + d, outer)
                far_part(h, p, source, source).wait_recv()
                total = total + ups[h, source, 0, :, lanes(p)].astype(f32)
            updated[h, :, lanes(p)] = total
            return

        @pl.when(z > 0)
        def _():
            add_part(h, p, 1, z)

        @pl.when(z < outer - 1)
        def _():
            add_part(h, p, 0, z)

        if not side_first[h][p]:
            send(None, lambda: side_copy(h, p, z))

    def renew(h, p):
        if side_first[h][p] > 1:
            total = updated[h, :, lanes(p)]
        else:
            total = own[h, me, :, lanes(p)].astype(f32)
        total = total + old[h, me, :, lanes(p)].astype(f32)
        if not side_first[h][p]:
            side_copy(h, p, z).wait_recv()
            total = total + side[h, 0, :, lanes(p)].astype(f32)
        updated[h, :, lanes(p)] = total
        new[h, me, :, lanes(p)] = total.astype(b16)
        issue(1, h, p)

    def pieces(g, h, j):
        buf = (old, new)[g]
        start, shift = plan.starts[j], plan.shifts[j]
        for b in range(n):
            piece = buf[h, b, :, start : start + window].astype(f32)
            yield b, plan.move(piece, shift, 64 * (h % 2))

    def prepare_old(h):
        for j in range(3):
            total = jnp.zeros((1, window), f32)
            for b, piece in pieces(0, h, j):
                weights[j, b * units : (b + 1) * units] = piece.astype(b16)
                total = total + jnp.sum(piece * piece, axis=0, keepdims=True)
            squares_old[3 * h + j : 3 * h + j + 1, :] = total

    def prepare_new(h):
        for j in range(3):
            total = jnp.zeros((1, window), f32)
            for b, piece in pieces(1, h, j):
                total = total + jnp.sum(piece * piece, axis=0, keepdims=True)
            scale = jnp.sqrt(squares_old[3 * h + j : 3 * h + j + 1, :]) * lax.rsqrt(total + EPS)
            for b, piece in pieces(1, h, j):
                weights[j, b * units : (b + 1) * units] = (piece * scale).astype(b16)
            start, shift = plan.starts[j], plan.shifts[j]
            exact = plan.move(updated[h, :, start : start + window], shift, 64 * (h % 2)) * scale
            fresh_ref[j, h] = plan.move(exact, 64 * (h % 2), 0)[:, :width].astype(b16)

    def at_steps(i, slots):
        for k, events in sorted(slots.items()):
            @pl.when(i == k)
            def _():
                for event in events:
                    event()

    def grads(h, slots):
        for j in range(3):
            acc[j] = jnp.zeros(acc.shape[1:], f32)
        cut = plan.columns(h)

        def body(i, _):
            at_steps(i, slots)
            span = pl.ds(pl.multiple_of(i * step, step), step)
            key = keys[span, cut]
            scaled = (values[span, cut].astype(f32) * rate[span, h : h + 1]).astype(b16)
            gpre = dot(weights[0], key, 1, 1)
            upre = dot(weights[1], key, 1, 1)
            back = dot(weights[2], scaled, 1, 1)
            sig = jax.nn.sigmoid(gpre)
            act = gpre * sig
            slope = sig * (1.0 + gpre * (1.0 - sig))
            acc[0] += dot((back * upre * slope).astype(b16), key, 1, 0)
            acc[1] += dot((back * act).astype(b16), key, 1, 0)
            acc[2] += dot((act * upre).astype(b16), scaled, 1, 0)
            return 0

        lax.fori_loop(0, tokens // step, body, 0)

    def start(h):
        if h % 2:
            load(2, h // 2).start()
        shift = 64 * (h % 2)
        for b in range(n):
            pieces_of = [
                plan.move(acc[j, b * units : (b + 1) * units], shift, plan.shifts[j]) for j in range(3)
            ]
            own[h, b] = plan.pack(*pieces_of).astype(b16)
        for p in range(parts):
            reduce_start(h, p)

    def apply_head(h, slots):
        cut = plan.columns(h)

        def body(i, _):
            at_steps(i, slots)
            span = pl.ds(pl.multiple_of(i * long, long), long)
            query = keys[span, cut]
            gate = dot(weights[0], query, 1, 1)
            up = dot(weights[1], query, 1, 1)
            mixed = (jax.nn.silu(gate) * up).astype(b16)
            out = dot(mixed, weights[2], 0, 0)
            if h % 2:
                shared = slice(cut.start, cut.start + 128)
                outs[span, shared] = outs[span, shared] + out[:, :128]
                outs[span, cut.start + 128 : cut.stop] = out[:, 128:]
            else:
                outs[span, cut] = out
            part = out * out
            total = part[:, :128]
            for c in range(128, window, 128):
                total = total + part[:, c : c + 128]
            if h > 0:
                total = squares[span, :] + total
            if h < heads - 1:
                squares[span, :] = total
            else:
                row[:, span] = jnp.sum(total.T, axis=0, keepdims=True)
            return 0

        lax.fori_loop(0, tokens // long, body, 0)

    def ready(g, h):
        if h % 2 == 0:
            for i in (2,) if g else (0, 1):
                load(i, h // 2).wait()
        for p in range(parts):
            arrived(g, h, p)
        (prepare_new if g else prepare_old)(h)

    handlers = {
        ISSUE: issue, RELAY: relay, CROSS: cross, READY: ready, START: start, SIDE: reduce_beside,
        PART: reduce_relay, END: reduce_end, FINISH: renew,
    }
    def turn_rates():
        turned = rate_ref[...]
        if heads < 8:
            turned = jnp.concatenate([turned, jnp.zeros((8 - heads, tokens), f32)], axis=0)
        rate[...] = turned.T

    order = list(order)
    while order:
        event = order.pop(0)
        if event == (RELAY, 0, 0, 0, 1):
            turn_rates()
        if event[0] != READY:
            handlers[event[0]](*event[1:])
            continue
        ready(*event[1:])
        slots = {}
        for k in range(tokens // (long if event[1] else step)):
            while order[0][0] != STEP:
                kind, *rest = order.pop(0)
                slots.setdefault(k, []).append(functools.partial(handlers[kind], *rest))
            order.pop(0)
        (apply_head if event[1] else grads)(event[2], slots)

    def row_copy(t):
        return pltpu.make_async_remote_copy(
            src_ref=row, dst_ref=rows_in.at[t - 1],
            send_sem=row_send.at[t - 1], recv_sem=row_recv.at[t - 1],
            device_id={"head": lax.rem(mine + t, plan.peers)},
        )

    for t in range(1, plan.peers):
        send(None, functools.partial(row_copy, t))
    total = row[...]
    for t in range(1, plan.peers):
        row_copy(t).wait_recv()
        total = total + rows_in[t - 1]
    row_out[...] = lax.rsqrt(total / plan.width_all + EPS)
    for done in sends:
        done()


def finish_kernel(step, outs_ref, row_ref, gain_ref, fresh_ref, out_hbm, *rest):
    weights, laid, staged, sem, weight_sem = rest[:3], rest[3], rest[4], rest[5], rest[6]
    tokens, width = outs_ref.shape

    def store(i):
        span = pl.ds(i * step, step)
        return pltpu.make_async_copy(staged.at[span], out_hbm.at[span], sem.at[i])

    def lay(j):
        return pltpu.make_async_copy(laid.at[j], weights[j], weight_sem.at[j])

    for i in range(tokens // step):
        span = slice(i * step, (i + 1) * step)
        scale = jnp.broadcast_to(row_ref[:, span], (128, step)).T
        for c in range(0, width, 128):
            cut = slice(c, c + 128)
            staged[span, cut] = (outs_ref[span, cut] * scale * gain_ref[cut][None]).astype(staged.dtype)
        store(i).start()
        if i < len(weights):
            heads = [fresh_ref[i, h].astype(jnp.float32) for h in range(fresh_ref.shape[1])]
            laid[i] = jnp.stack(heads, axis=1).astype(laid.dtype)
            lay(i).start()
    for i in range(tokens // step):
        store(i).wait()
    for j in range(len(weights)):
        lay(j).wait()


def finish(outs, row, gain, fresh):
    rows, width = outs.shape
    units, heads = fresh.shape[2], fresh.shape[1]
    weight = jax.ShapeDtypeStruct((units, heads, fresh.shape[3]), fresh.dtype)
    step = 256
    return pl.pallas_call(
        functools.partial(finish_kernel, step),
        out_shape=(jax.ShapeDtypeStruct(outs.shape, jnp.bfloat16),) + (weight,) * 3,
        in_specs=vmem(4),
        out_specs=(pl.BlockSpec(memory_space=pl.ANY),) * 4,
        scratch_shapes=[
            pltpu.VMEM((3,) + weight.shape, weight.dtype),
            pltpu.VMEM(outs.shape, jnp.bfloat16),
            pltpu.SemaphoreType.DMA((rows // step,)),
            pltpu.SemaphoreType.DMA((3,)),
        ],
        compiler_params=pltpu.CompilerParams(vmem_limit_bytes=32 * 1024 * 1024),
        name="finish_rows",
    )(outs, row, gain, fresh)


def fused(n, peers, width_all, keys, values, queries, rates, w_gate, w_up, w_down):
    rows = keys.shape[0]
    units, heads, width = w_gate.shape
    plan = Plan(n, peers, rows, units, heads, width, width_all)
    f32, b16 = jnp.float32, jnp.bfloat16
    outer = plan.outer
    hbm = pl.BlockSpec(memory_space=pl.ANY)
    block = (units, plan.packed)
    dma = pltpu.SemaphoreType.DMA
    copies = 2 * heads
    return pl.pallas_call(
        functools.partial(fused_kernel, plan),
        out_shape=(
            pltpu.VMEM(keys.shape, f32),
            pltpu.VMEM((1, rows), f32),
            pltpu.VMEM((3, heads, units, width), b16),
        ),
        in_specs=[hbm] * 3 + vmem(4),
        out_specs=tuple(vmem(3)),
        scratch_shapes=[
            pltpu.VMEM(keys.shape, b16),
            pltpu.VMEM(keys.shape, b16),
            pltpu.VMEM((rows, 8), f32),
            pltpu.VMEM((heads, n) + block, b16),
            pltpu.VMEM((heads, n) + block, b16),
            pltpu.VMEM((heads, n) + block, b16),
            pltpu.VMEM((heads, outer, 2) + block, b16),
            pltpu.VMEM((heads, outer, 2) + block, b16),
            pltpu.VMEM((heads, outer) + block, b16),
            pltpu.VMEM((heads,) + block, f32),
            pltpu.VMEM((3, n * units, plan.window), b16),
            pltpu.VMEM((3, n * units, plan.window), f32),
            pltpu.VMEM((3 * heads, plan.window), f32),
            pltpu.VMEM((rows, 128), f32),
            pltpu.VMEM((1, rows), f32),
            pltpu.VMEM((peers - 1, 1, rows), f32),
            dma((3, heads // 2)),
            dma((2, copies, 2, outer)),
            dma((2, copies, outer)),
            dma((2, copies, outer)),
            dma((2, copies, outer)),
            dma((2, copies, 2)),
            dma((2, copies, 2)),
            dma((copies, 2, outer)),
            dma((copies, 2, outer)),
            dma((copies, outer)),
            dma((copies, outer)),
            dma((peers - 1,)),
            dma((peers - 1,)),
        ],
        compiler_params=pltpu.CompilerParams(
            collective_id=2, has_side_effects=True, vmem_limit_bytes=VMEM_LIMIT
        ),
        name="fused_layer",
    )(keys, values, queries, rates.T, w_gate, w_up, w_down)


def per_device(n, peers, width_all, keys, values, queries, rates, w_gate, w_up, w_down, gain):
    rows = keys.shape[0]
    units, heads, width = w_gate.shape
    f32 = jnp.float32
    if fits(n, rows, units, heads, width):
        outs, row, fresh = fused(
            n, peers, width_all, keys, values, queries, rates, w_gate, w_up, w_down
        )
        return finish(outs, row, gain, fresh)
    own = jnp.stack([w_gate, w_up, w_down]).transpose(0, 2, 1, 3)
    own = own.reshape(3 * heads, units, width)
    full = gather(own, n).transpose(1, 3, 0, 2)
    full = full.reshape(3, heads, width, n * units)
    grads = token_grads(keys, values, rates, full)
    block = (n, 3 * heads * width // n, n * units)
    old = lax.dynamic_index_in_dim(full.reshape(block), lax.axis_index("ctx"), 0, keepdims=False)
    fresh = update(grads.reshape(block), old, n).reshape(full.shape)
    mine = lax.dynamic_slice_in_dim(fresh, lax.axis_index("ctx") * units, units, 3)
    mine = mine.transpose(0, 3, 1, 2)
    outs, squares = apply(queries, fresh)
    squares = lax.psum(squares.reshape(rows), "head")
    scale = lax.rsqrt(squares / width_all + EPS)
    output = (outs.astype(f32) * scale[:, None] * gain[None]).astype(jnp.bfloat16)
    return (output, mine[0], mine[1], mine[2])


def solution(mesh):
    weight = P("ctx", "head", None)
    token = P("ctx", "head")

    def whole(keys, *rest):
        body = functools.partial(
            per_device, mesh.shape["ctx"], mesh.shape["head"], keys.shape[1]
        )
        return jax.shard_map(
            body,
            mesh=mesh,
            in_specs=(token,) * 4 + (weight,) * 3 + (P("head"),),
            out_specs=(token, weight, weight, weight),
            check_vma=False,
        )(keys, *rest)

    return whole
```

```python
import functools
import math

import jax
import jax.numpy as jnp
from jax import lax
from jax.experimental import pallas as pl
from jax.experimental.pallas import tpu as pltpu
from jax.sharding import PartitionSpec as P

EPS = 1e-06

VMEM_LIMIT = 50 * 1024 * 1024
STEPS = (1024, 2048)
ISSUE, RELAY, CROSS, READY, STEP, START, SIDE, PART, END, FINISH = range(10)
ORDERS = {
    (4, 4, 2048): (
        ((0, 0), (0, 1), (1, 1), (1, 1)),
        (((0, 1), (0, 1), (0, 1), (0, 1)), ((0, 1), (0, 1), (0, 1), (2, 2))),
        (
            (ISSUE, 0, 0, 0), (ISSUE, 0, 0, 1), (ISSUE, 0, 1, 0), (ISSUE, 0, 1, 1),
            (RELAY, 0, 0, 0, 1), (RELAY, 0, 0, 1, 1), (CROSS, 0, 0, 1), (RELAY, 0, 1, 0, 1),
            (RELAY, 0, 0, 0, 2), (RELAY, 0, 0, 1, 2), (RELAY, 0, 1, 1, 1), (ISSUE, 0, 2, 0),
            (ISSUE, 0, 2, 1), (CROSS, 0, 1, 1), (RELAY, 0, 0, 0, 3), (RELAY, 0, 0, 1, 3),
            (RELAY, 0, 1, 1, 2), (RELAY, 0, 1, 0, 2), (ISSUE, 0, 3, 0), (ISSUE, 0, 3, 1),
            (READY, 0, 0), (RELAY, 0, 2, 0, 1), (STEP, 0, 0, 0), (RELAY, 0, 1, 1, 3),
            (RELAY, 0, 1, 0, 3), (RELAY, 0, 2, 1, 1), (CROSS, 0, 2, 1), (STEP, 0, 0, 1),
            (CROSS, 0, 3, 1), (START, 0), (RELAY, 0, 2, 1, 2), (RELAY, 0, 2, 0, 2),
            (RELAY, 0, 3, 0, 1), (READY, 0, 1), (STEP, 0, 1, 0), (RELAY, 0, 2, 1, 3),
            (RELAY, 0, 2, 0, 3), (STEP, 0, 1, 1), (RELAY, 0, 3, 0, 2), (RELAY, 0, 3, 0, 3),
            (RELAY, 0, 3, 1, 1), (START, 1), (READY, 0, 2), (STEP, 0, 2, 0), (RELAY, 0, 3, 1, 2),
            (RELAY, 0, 3, 1, 3), (PART, 0, 0, 3, 1), (PART, 0, 0, 2, 1), (STEP, 0, 2, 1),
            (START, 2), (PART, 0, 1, 3, 1), (SIDE, 1, 1, 0), (SIDE, 1, 1, 2), (SIDE, 1, 1, 1),
            (PART, 0, 0, 3, 2), (SIDE, 1, 1, 3), (PART, 0, 1, 2, 1), (READY, 0, 3),
            (STEP, 0, 3, 0), (PART, 0, 1, 3, 2), (SIDE, 2, 0, 3), (END, 0, 0), (SIDE, 2, 0, 1),
            (SIDE, 2, 0, 2), (PART, 1, 0, 3, 1), (SIDE, 2, 0, 0), (PART, 1, 0, 2, 1), (END, 0, 1),
            (STEP, 0, 3, 1), (START, 3), (PART, 1, 1, 3, 1), (FINISH, 0, 0), (PART, 1, 1, 2, 1),
            (SIDE, 2, 1, 3), (FINISH, 0, 1), (SIDE, 2, 1, 0), (PART, 1, 0, 3, 2),
            (PART, 2, 0, 3, 1), (PART, 2, 0, 2, 1), (SIDE, 3, 0, 3), (SIDE, 2, 1, 2),
            (PART, 1, 1, 3, 2), (SIDE, 2, 1, 1), (END, 1, 0), (RELAY, 1, 0, 0, 1), (SIDE, 3, 0, 0),
            (END, 1, 1), (FINISH, 1, 1), (SIDE, 3, 0, 2), (RELAY, 1, 0, 1, 1), (SIDE, 3, 1, 3),
            (PART, 2, 0, 3, 2), (SIDE, 3, 0, 1), (END, 2, 0), (FINISH, 2, 0), (PART, 2, 1, 3, 1),
            (PART, 2, 1, 2, 1), (SIDE, 3, 1, 0), (RELAY, 1, 0, 0, 2), (RELAY, 1, 0, 0, 3),
            (SIDE, 3, 1, 1), (RELAY, 1, 0, 1, 2), (RELAY, 1, 0, 1, 3), (PART, 3, 0, 3, 1),
            (RELAY, 1, 1, 1, 1), (FINISH, 1, 0), (PART, 2, 1, 3, 2), (SIDE, 3, 1, 2),
            (CROSS, 1, 0, 1), (END, 2, 1), (FINISH, 2, 1), (PART, 3, 1, 3, 1), (RELAY, 1, 1, 1, 2),
            (PART, 3, 0, 3, 2), (RELAY, 1, 1, 1, 3), (RELAY, 1, 1, 0, 1), (RELAY, 1, 2, 0, 1),
            (PART, 3, 0, 2, 1), (READY, 1, 0), (PART, 3, 1, 3, 2), (RELAY, 1, 2, 1, 1),
            (RELAY, 1, 1, 0, 2), (PART, 3, 1, 2, 1), (CROSS, 1, 1, 1), (RELAY, 1, 2, 0, 2),
            (END, 3, 0), (FINISH, 3, 0), (RELAY, 1, 1, 0, 3), (RELAY, 1, 2, 1, 2), (END, 3, 1),
            (FINISH, 3, 1), (STEP, 1, 0, 0), (RELAY, 1, 2, 0, 3), (READY, 1, 1),
            (RELAY, 1, 3, 0, 1), (RELAY, 1, 3, 0, 2), (CROSS, 1, 2, 1), (RELAY, 1, 2, 1, 3),
            (RELAY, 1, 3, 0, 3), (RELAY, 1, 3, 1, 1), (RELAY, 1, 3, 1, 2), (RELAY, 1, 3, 1, 3),
            (STEP, 1, 1, 0), (READY, 1, 2), (STEP, 1, 2, 0), (READY, 1, 3), (STEP, 1, 3, 0),
        ),
    ),
}


def inner_size(n):
    inner = 1
    while inner * inner * 4 <= n and n % (inner * 2) == 0:
        inner *= 2
    return inner if inner > 1 or n % 2 else 2


def place(n, inner):
    me = lax.axis_index("ctx")
    return me, me // inner, lax.rem(me, inner), n // inner


def greet(z, x, outer, inner):
    barrier = pltpu.get_barrier_semaphore()
    for s in range(1, outer):
        pl.semaphore_signal(barrier, inc=1, device_id={"ctx": lax.rem(z + s, outer) * inner + x})
    for t in range(1, inner):
        pl.semaphore_signal(barrier, inc=1, device_id={"ctx": z * inner + lax.rem(x + t, inner)})
    pl.semaphore_wait(barrier, outer + inner - 2)


def spread(z, x, outer, inner, own_ref, out_ref, send_sem, recv_sem):
    me = z * inner + x
    copies = {}

    def send(src, block, device, s, t):
        copy = pltpu.make_async_remote_copy(
            src_ref=src,
            dst_ref=out_ref.at[block],
            send_sem=send_sem.at[s, t],
            recv_sem=recv_sem.at[s, t],
            device_id={"ctx": device},
        )
        copy.start()
        copies[s, t] = copy

    for s in range(1, outer):
        send(own_ref, me, lax.rem(z + s, outer) * inner + x, s, 0)
    for t in range(1, inner):
        send(own_ref, me, z * inner + lax.rem(x + t, inner), 0, t)
    for s in range(1, outer):
        copies[s, 0].wait_recv()
        block = lax.rem(z + outer - s, outer) * inner + x
        for t in range(1, inner):
            send(out_ref.at[block], block, z * inner + lax.rem(x + t, inner), s, t)
    for (s, t), copy in copies.items():
        if t:
            copy.wait_recv()
    for copy in copies.values():
        copy.wait_send()


def gather_kernel(n, inner, own_ref, out_ref, local_sem, send_sem, recv_sem):
    me, z, x, outer = place(n, inner)
    greet(z, x, outer, inner)
    keep = pltpu.make_async_copy(own_ref, out_ref.at[me], local_sem)
    keep.start()
    spread(z, x, outer, inner, own_ref, out_ref, send_sem, recv_sem)
    keep.wait()


def update_kernel(
    n, inner, grad_ref, old_ref, out_ref, near, part, far, fresh,
    local_sem, near_send, near_recv, far_send, far_recv, send_sem, recv_sem,
):
    me, z, x, outer = place(n, inner)
    greet(z, x, outer, inner)
    order = list(range(1, outer)) + [0]
    first = {}
    for s in order:
        row = lax.rem(z + s, outer) * inner
        for t in range(1, inner):
            column = lax.rem(x + t, inner)
            copy = pltpu.make_async_remote_copy(
                src_ref=grad_ref.at[row + column],
                dst_ref=near.at[s, t - 1],
                send_sem=near_send.at[s, t],
                recv_sem=near_recv.at[s, t],
                device_id={"ctx": z * inner + column},
            )
            copy.start()
            first[s, t] = copy
    second = {}
    total = None
    for s in order:
        row = lax.rem(z + s, outer) * inner
        total = grad_ref[row + x].astype(jnp.float32)
        for t in range(1, inner):
            first[s, t].wait_recv()
            total = total + near[s, t - 1].astype(jnp.float32)
        if s:
            part[s] = total.astype(part.dtype)
            copy = pltpu.make_async_remote_copy(
                src_ref=part.at[s],
                dst_ref=far.at[s],
                send_sem=far_send.at[s],
                recv_sem=far_recv.at[s],
                device_id={"ctx": row + x},
            )
            copy.start()
            second[s] = copy
    for s, copy in second.items():
        copy.wait_recv()
        total = total + far[s].astype(jnp.float32)
    old = old_ref[...].astype(jnp.float32)
    updated = old + total
    old_sq = jnp.sum(old * old, axis=1, keepdims=True)
    new_sq = jnp.sum(updated * updated, axis=1, keepdims=True)
    fresh[...] = (updated * (jnp.sqrt(old_sq) * lax.rsqrt(new_sq + EPS))).astype(fresh.dtype)
    keep = pltpu.make_async_copy(fresh, out_ref.at[me], local_sem)
    keep.start()
    keep.wait()
    spread(z, x, outer, inner, out_ref.at[me], out_ref, send_sem, recv_sem)
    for copy in first.values():
        copy.wait_send()
    for copy in second.values():
        copy.wait_send()


def vmem(count):
    return [pl.BlockSpec(memory_space=pltpu.VMEM)] * count


def gather(own, n):
    inner = inner_size(n)
    outer = n // inner
    return pl.pallas_call(
        functools.partial(gather_kernel, n, inner),
        out_shape=jax.ShapeDtypeStruct((n,) + own.shape, own.dtype),
        in_specs=vmem(1),
        out_specs=vmem(1)[0],
        scratch_shapes=[pltpu.SemaphoreType.DMA]
        + [pltpu.SemaphoreType.DMA((outer, inner))] * 2,
        compiler_params=pltpu.CompilerParams(collective_id=0, has_side_effects=True),
        name="gather_weights",
    )(own)


def update(grads, old, n):
    inner = inner_size(n)
    outer = n // inner
    block = grads.shape[1:]
    return pl.pallas_call(
        functools.partial(update_kernel, n, inner),
        out_shape=jax.ShapeDtypeStruct(grads.shape, grads.dtype),
        in_specs=vmem(2),
        out_specs=vmem(1)[0],
        scratch_shapes=[
            pltpu.VMEM((outer, max(inner - 1, 1)) + block, grads.dtype),
            pltpu.VMEM((outer,) + block, grads.dtype),
            pltpu.VMEM((outer,) + block, grads.dtype),
            pltpu.VMEM(block, grads.dtype),
            pltpu.SemaphoreType.DMA,
        ]
        + [pltpu.SemaphoreType.DMA((outer, inner))] * 2
        + [pltpu.SemaphoreType.DMA((outer,))] * 2
        + [pltpu.SemaphoreType.DMA((outer, inner))] * 2,
        compiler_params=pltpu.CompilerParams(collective_id=1, has_side_effects=True),
        name="update_weights",
    )(grads, old)


def dot(a, b, left, right):
    return lax.dot_general(a, b, (((left,), (right,)), ((), ())), preferred_element_type=jnp.float32)


def grads_kernel(key_ref, value_ref, rate_ref, weight_ref, out_ref, acc):
    step = pl.program_id(0)

    @pl.when(step == 0)
    def _():
        acc[...] = jnp.zeros_like(acc)

    heads, width = weight_ref.shape[1:3]
    for h in range(heads):
        columns = slice(h * width, (h + 1) * width)
        key = key_ref[:, columns]
        gpre = dot(key, weight_ref[0, h], 1, 0)
        upre = dot(key, weight_ref[1, h], 1, 0)
        scaled = (value_ref[:, columns].astype(jnp.float32) * rate_ref[:, h : h + 1]).astype(jnp.bfloat16)
        back = dot(scaled, weight_ref[2, h], 1, 0)
        sig = jax.nn.sigmoid(gpre)
        act = gpre * sig
        slope = sig * (1.0 + gpre * (1.0 - sig))
        acc[0, h] += dot(key, (back * upre * slope).astype(jnp.bfloat16), 0, 0)
        acc[1, h] += dot(key, (back * act).astype(jnp.bfloat16), 0, 0)
        acc[2, h] += dot(scaled, (act * upre).astype(jnp.bfloat16), 0, 0)

    @pl.when(step == pl.num_programs(0) - 1)
    def _():
        out_ref[...] = acc[...].astype(out_ref.dtype)


def apply_kernel(query_ref, weight_ref, out_ref, square_ref):
    heads, width = weight_ref.shape[1:3]
    squares = None
    for h in range(heads):
        columns = slice(h * width, (h + 1) * width)
        query = query_ref[:, columns]
        gate = dot(query, weight_ref[0, h], 1, 0)
        up = dot(query, weight_ref[1, h], 1, 0)
        mixed = (jax.nn.silu(gate) * up).astype(jnp.bfloat16)
        out = dot(mixed, weight_ref[2, h], 1, 1)
        part = jnp.sum(out * out, axis=1, keepdims=True)
        squares = part if squares is None else squares + part
        out_ref[:, columns] = out.astype(out_ref.dtype)
    square_ref[...] = squares


def tile(rows, width):
    return pl.BlockSpec((rows, width), lambda i: (i, 0))


def fixed(shape):
    return pl.BlockSpec(shape, lambda i: (0,) * len(shape))


def token_grads(keys, values, rates, weights):
    rows, width = keys.shape
    step = math.gcd(rows, 512)
    return pl.pallas_call(
        grads_kernel,
        grid=(rows // step,),
        out_shape=jax.ShapeDtypeStruct(weights.shape, jnp.bfloat16),
        in_specs=[tile(step, width), tile(step, width), tile(step, rates.shape[1]), fixed(weights.shape)],
        out_specs=fixed(weights.shape),
        scratch_shapes=[pltpu.VMEM(weights.shape, jnp.float32)],
        name="token_grads",
    )(keys, values, rates, weights)


def apply(queries, weights):
    rows, width = queries.shape
    step = math.gcd(rows, 512)
    return pl.pallas_call(
        apply_kernel,
        grid=(rows // step,),
        out_shape=(
            jax.ShapeDtypeStruct((rows, width), jnp.bfloat16),
            jax.ShapeDtypeStruct((rows, 1), jnp.float32),
        ),
        in_specs=[tile(step, width), fixed(weights.shape)],
        out_specs=(tile(step, width), tile(step, 1)),
        name="apply_weights",
    )(queries, weights)


def fits(n, rows, units, heads, width):
    inner = inner_size(n)
    return (
        inner == 2
        and n // inner >= 2
        and units % 8 == 0
        and heads % 2 == 0
        and heads <= 8
        and width % 128 == 64
        and rows % max(STEPS) == 0
        and rows * heads * width <= 2048 * 1280
        and (n // inner, heads, rows) in ORDERS
    )


class Plan:
    def __init__(self, n, peers, rows, units, heads, width, width_all):
        self.n, self.peers, self.rows, self.units = n, peers, rows, units
        self.heads, self.width, self.width_all = heads, width, width_all
        self.inner = 2
        self.outer = n // 2
        self.step, self.long = STEPS
        self.window = width + 64
        self.packed = 2 * width + self.window
        self.starts = (0, width - 64, 2 * width)
        self.shifts = (0, 64, 0)

    def columns(self, h):
        start = (h // 2) * 2 * self.width + (h % 2) * (self.width - 64)
        return slice(start, start + self.window)

    def move(self, x, old, new):
        size = x.shape[1]
        if old != new:
            x = pltpu.roll(x, (new - old) % size, 1)
        lane = lax.broadcasted_iota(jnp.int32, x.shape, 1)
        return jnp.where((lane >= new) & (lane < new + self.width), x, 0.0)

    def pack(self, gate, up, down):
        first = self.width - 64
        shared = gate[:, first:] + up[:, :128]
        return jnp.concatenate([gate[:, :first], shared, up[:, 128:], down], axis=1)


def fused_kernel(
    plan, key_hbm, value_hbm, query_hbm, rate_ref, gate_ref, up_ref, down_ref,
    outs, row_out, fresh_ref,
    keys, values, rate, old, new, own, ups, downs, side, updated, weights, acc,
    squares_old, squares, row, rows_in,
    load_sem,
    line_send, line_recv, cross_send, cross_recv, pass_send, pass_recv,
    part_send, part_recv, side_send, side_recv, row_send, row_recv,
):
    f32, b16 = jnp.float32, jnp.bfloat16
    n, outer, heads, units, width = plan.n, plan.outer, plan.heads, plan.units, plan.width
    window, step, long, tokens = plan.window, plan.step, plan.long, plan.rows
    me = lax.axis_index("ctx")
    z, x = me // 2, lax.rem(me, 2)
    mine = lax.axis_index("head")
    other = z * 2 + 1 - x

    half = 2 * width

    def load(i, p):
        cut = slice(p * half, (p + 1) * half)
        src, dst = ((key_hbm, keys), (value_hbm, values), (query_hbm, keys))[i]
        return pltpu.make_async_copy(src.at[:, cut], dst.at[:, cut], load_sem.at[i, p])

    for p in range(heads // 2):
        load(0, p).start()
        load(1, p).start()

    barrier = pltpu.get_barrier_semaphore()
    pl.semaphore_signal(barrier, inc=1, device_id={"ctx": other})
    for t in range(1, plan.peers):
        pl.semaphore_signal(barrier, inc=1, device_id={"head": lax.rem(mine + t, plan.peers)})

    for t in range(1, outer):
        pl.semaphore_signal(barrier, inc=1, device_id={"ctx": lax.rem(z + t, outer) * 2 + x})

    def pack_own(h):
        parts = []
        for j, ref in enumerate((gate_ref, up_ref, down_ref)):
            piece = ref[:, h, :].astype(f32)
            piece = jnp.concatenate([piece, jnp.zeros((units, 64), f32)], axis=1)
            parts.append(plan.move(piece, 0, plan.shifts[j]))
        old[h, me] = plan.pack(*parts).astype(b16)

    pack_own(0)
    pl.semaphore_wait(barrier, plan.peers + outer - 1)

    sends = []
    side_first, passing, order = ORDERS[outer, heads, tokens]

    def send(when, make):
        def start():
            make().start()

        def finish():
            make().wait_send()

        if when is None:
            start()
            sends.append(finish)
        else:
            pl.when(when())(start)
            sends.append(lambda: pl.when(when())(finish))

    parts = 2
    share = plan.packed // parts
    lanes = lambda p: slice(p * share, (p + 1) * share)

    def line_copy(g, h, p, origin, up):
        buf = (old, new)[g]
        block = origin * 2 + x
        return pltpu.make_async_remote_copy(
            src_ref=buf.at[h, block, :, lanes(p)], dst_ref=buf.at[h, block, :, lanes(p)],
            send_sem=line_send.at[g, h * parts + p, up, origin], recv_sem=line_recv.at[g, h * parts + p, origin],
            device_id={"ctx": me + (2 if up else -2)},
        )

    def cross_copy(g, h, p, origin):
        buf = (old, new)[g]
        block = origin * 2 + x
        return pltpu.make_async_remote_copy(
            src_ref=buf.at[h, block, :, lanes(p)], dst_ref=buf.at[h, block, :, lanes(p)],
            send_sem=cross_send.at[g, h * parts + p, origin], recv_sem=cross_recv.at[g, h * parts + p, origin],
            device_id={"ctx": other},
        )

    def far_copy(g, h, p, to):
        buf = (old, new)[g]
        return pltpu.make_async_remote_copy(
            src_ref=buf.at[h, me, :, lanes(p)], dst_ref=buf.at[h, me, :, lanes(p)],
            send_sem=line_send.at[g, h * parts + p, 0, to], recv_sem=line_recv.at[g, h * parts + p, z],
            device_id={"ctx": to * 2 + x},
        )

    def issue(g, h, p):
        if g == 0 and h > 0 and p == 0:
            pack_own(h)
        if passing[g][h][p] > 1:
            for d in range(outer - 1, 0, -1):
                send(lambda d=d: z + d < outer, lambda d=d: far_copy(g, h, p, z + d))
                send(lambda d=d: z >= d, lambda d=d: far_copy(g, h, p, z - d))
            send(None, lambda: cross_copy(g, h, p, z))
            return
        send(lambda: z < outer - 1, lambda: line_copy(g, h, p, z, 1))
        send(lambda: z > 0, lambda: line_copy(g, h, p, z, 0))
        send(None, lambda: cross_copy(g, h, p, z))

    def relay(g, h, p, d):
        whole = d > 1 or not passing[g][h][p] & 1
        onward = passing[g][h][p] < 2

        @pl.when(z >= d)
        def _():
            line_copy(g, h, p, z - d, 1).wait_recv()

        if onward:
            send(lambda: (z >= d) & (z < outer - 1), lambda: line_copy(g, h, p, z - d, 1))
        if whole:
            send(lambda: z >= d, lambda: cross_copy(g, h, p, z - d))

        @pl.when(z + d < outer)
        def _():
            line_copy(g, h, p, z + d, 0).wait_recv()

        if onward:
            send(lambda: (z + d < outer) & (z > 0), lambda: line_copy(g, h, p, z + d, 0))
        if whole:
            send(lambda: z + d < outer, lambda: cross_copy(g, h, p, z + d))

    def pass_copy(g, h, p, up):
        buf = (old, new)[g]
        return pltpu.make_async_remote_copy(
            src_ref=buf.at[h, other, :, lanes(p)], dst_ref=buf.at[h, other, :, lanes(p)],
            send_sem=pass_send.at[g, h * parts + p, up], recv_sem=pass_recv.at[g, h * parts + p, up],
            device_id={"ctx": me + (2 if up else -2)},
        )

    def cross(g, h, p):
        cross_copy(g, h, p, z).wait_recv()
        send(lambda: z < outer - 1, lambda: pass_copy(g, h, p, 1))
        send(lambda: z > 0, lambda: pass_copy(g, h, p, 0))

    def arrived(g, h, p):
        if not passing[g][h][p] & 1:
            for o in range(outer):
                cross_copy(g, h, p, o).wait_recv()
            return
        for o in range(outer):
            pl.when((o > z + 1) | (o < z - 1))(lambda: cross_copy(g, h, p, o).wait_recv())
        pl.when(z > 0)(lambda: pass_copy(g, h, p, 1).wait_recv())
        pl.when(z < outer - 1)(lambda: pass_copy(g, h, p, 0).wait_recv())

    def part_copy(h, p, up, to):
        buf = (downs, ups)[up]
        first, count = (to * 2 + x, 1) if side_first[h][p] else (to * 2, 2)
        return pltpu.make_async_remote_copy(
            src_ref=own.at[h, pl.ds(first, count), :, lanes(p)], dst_ref=buf.at[h, to, pl.ds(0, count), :, lanes(p)],
            send_sem=part_send.at[h * parts + p, up, to], recv_sem=part_recv.at[h * parts + p, up, to],
            device_id={"ctx": me + (2 if up else -2)},
        )

    def add_part(h, p, up, to):
        buf = (downs, ups)[up]
        part_copy(h, p, up, to).wait_recv()
        for c in range(1 if side_first[h][p] else 2):
            block = to * 2 + (x if side_first[h][p] else c)
            total = own[h, block, :, lanes(p)].astype(f32) + buf[h, to, c, :, lanes(p)].astype(f32)
            own[h, block, :, lanes(p)] = total.astype(b16)

    def far_part(h, p, to, slot):
        return pltpu.make_async_remote_copy(
            src_ref=own.at[h, to * 2 + x, :, lanes(p)], dst_ref=ups.at[h, slot, 0, :, lanes(p)],
            send_sem=part_send.at[h * parts + p, 0, to], recv_sem=part_recv.at[h * parts + p, 1, slot],
            device_id={"ctx": to * 2 + x},
        )

    def side_copy(h, p, to):
        return pltpu.make_async_remote_copy(
            src_ref=own.at[h, to * 2 + 1 - x, :, lanes(p)], dst_ref=side.at[h, to if side_first[h][p] else 0, :, lanes(p)],
            send_sem=side_send.at[h * parts + p, to], recv_sem=side_recv.at[h * parts + p, to],
            device_id={"ctx": other},
        )

    def reduce_start(h, p):
        if side_first[h][p]:
            for i in range(outer):
                send(None, functools.partial(side_copy, h, p, i // 2 if i % 2 else outer - 1 - i // 2))
            return
        for to in range(outer - 1, 0, -1):
            send(lambda: z == 0, functools.partial(part_copy, h, p, 1, to))
            send(lambda: z == outer - 1, functools.partial(part_copy, h, p, 0, outer - 1 - to))

    def reduce_beside(h, p, to):
        side_copy(h, p, to).wait_recv()
        total = own[h, to * 2 + x, :, lanes(p)].astype(f32) + side[h, to, :, lanes(p)].astype(f32)
        own[h, to * 2 + x, :, lanes(p)] = total.astype(b16)
        if side_first[h][p] > 1:
            send(lambda: z != to, lambda: far_part(h, p, to, z))
            return
        if to > 0:
            send(lambda: z == 0, lambda: part_copy(h, p, 1, to))
        if to < outer - 1:
            send(lambda: z == outer - 1, lambda: part_copy(h, p, 0, to))

    def reduce_relay(h, p, to, d):
        back = outer - 1 - to

        @pl.when(z == d)
        def _():
            add_part(h, p, 1, to)

        send(lambda: z == d, lambda: part_copy(h, p, 1, to))

        @pl.when(z == outer - 1 - d)
        def _():
            add_part(h, p, 0, back)

        send(lambda: z == outer - 1 - d, lambda: part_copy(h, p, 0, back))

    def reduce_end(h, p):
        if side_first[h][p] > 1:
            total = own[h, me, :, lanes(p)].astype(f32)
            for d in range(1, outer):
                source = lax.rem(z + d, outer)
                far_part(h, p, source, source).wait_recv()
                total = total + ups[h, source, 0, :, lanes(p)].astype(f32)
            updated[h, :, lanes(p)] = total
            return

        @pl.when(z > 0)
        def _():
            add_part(h, p, 1, z)

        @pl.when(z < outer - 1)
        def _():
            add_part(h, p, 0, z)

        if not side_first[h][p]:
            send(None, lambda: side_copy(h, p, z))

    def renew(h, p):
        if side_first[h][p] > 1:
            total = updated[h, :, lanes(p)]
        else:
            total = own[h, me, :, lanes(p)].astype(f32)
        total = total + old[h, me, :, lanes(p)].astype(f32)
        if not side_first[h][p]:
            side_copy(h, p, z).wait_recv()
            total = total + side[h, 0, :, lanes(p)].astype(f32)
        updated[h, :, lanes(p)] = total
        new[h, me, :, lanes(p)] = total.astype(b16)
        issue(1, h, p)

    def pieces(g, h, j):
        buf = (old, new)[g]
        start, shift = plan.starts[j], plan.shifts[j]
        for b in range(n):
            piece = buf[h, b, :, start : start + window].astype(f32)
            yield b, plan.move(piece, shift, 64 * (h % 2))

    def prepare_old(h):
        for j in range(3):
            total = jnp.zeros((1, window), f32)
            for b, piece in pieces(0, h, j):
                weights[j, b * units : (b + 1) * units] = piece.astype(b16)
                total = total + jnp.sum(piece * piece, axis=0, keepdims=True)
            squares_old[3 * h + j : 3 * h + j + 1, :] = total

    def prepare_new(h):
        for j in range(3):
            total = jnp.zeros((1, window), f32)
            for b, piece in pieces(1, h, j):
                total = total + jnp.sum(piece * piece, axis=0, keepdims=True)
            scale = jnp.sqrt(squares_old[3 * h + j : 3 * h + j + 1, :]) * lax.rsqrt(total + EPS)
            for b, piece in pieces(1, h, j):
                weights[j, b * units : (b + 1) * units] = (piece * scale).astype(b16)
            start, shift = plan.starts[j], plan.shifts[j]
            exact = plan.move(updated[h, :, start : start + window], shift, 64 * (h % 2)) * scale
            fresh_ref[j, h] = plan.move(exact, 64 * (h % 2), 0)[:, :width].astype(b16)

    def at_steps(i, slots):
        for k, events in sorted(slots.items()):
            @pl.when(i == k)
            def _():
                for event in events:
                    event()

    def grads(h, slots):
        for j in range(3):
            acc[j] = jnp.zeros(acc.shape[1:], f32)
        cut = plan.columns(h)

        def body(i, _):
            at_steps(i, slots)
            span = pl.ds(pl.multiple_of(i * step, step), step)
            key = keys[span, cut]
            scaled = (values[span, cut].astype(f32) * rate[span, h : h + 1]).astype(b16)
            gpre = dot(weights[0], key, 1, 1)
            upre = dot(weights[1], key, 1, 1)
            back = dot(weights[2], scaled, 1, 1)
            sig = jax.nn.sigmoid(gpre)
            act = gpre * sig
            slope = sig * (1.0 + gpre * (1.0 - sig))
            acc[0] += dot((back * upre * slope).astype(b16), key, 1, 0)
            acc[1] += dot((back * act).astype(b16), key, 1, 0)
            acc[2] += dot((act * upre).astype(b16), scaled, 1, 0)
            return 0

        lax.fori_loop(0, tokens // step, body, 0)

    def start(h):
        if h % 2:
            load(2, h // 2).start()
        shift = 64 * (h % 2)
        for b in range(n):
            pieces_of = [
                plan.move(acc[j, b * units : (b + 1) * units], shift, plan.shifts[j]) for j in range(3)
            ]
            own[h, b] = plan.pack(*pieces_of).astype(b16)
        for p in range(parts):
            reduce_start(h, p)

    def apply_head(h, slots):
        cut = plan.columns(h)

        def body(i, _):
            at_steps(i, slots)
            span = pl.ds(pl.multiple_of(i * long, long), long)
            query = keys[span, cut]
            gate = dot(weights[0], query, 1, 1)
            up = dot(weights[1], query, 1, 1)
            mixed = (jax.nn.silu(gate) * up).astype(b16)
            out = dot(mixed, weights[2], 0, 0)
            if h % 2:
                shared = slice(cut.start, cut.start + 128)
                outs[span, shared] = outs[span, shared] + out[:, :128]
                outs[span, cut.start + 128 : cut.stop] = out[:, 128:]
            else:
                outs[span, cut] = out
            part = out * out
            total = part[:, :128]
            for c in range(128, window, 128):
                total = total + part[:, c : c + 128]
            if h > 0:
                total = squares[span, :] + total
            if h < heads - 1:
                squares[span, :] = total
            else:
                row[:, span] = jnp.sum(total.T, axis=0, keepdims=True)
            return 0

        lax.fori_loop(0, tokens // long, body, 0)

    def ready(g, h):
        if h % 2 == 0:
            for i in (2,) if g else (0, 1):
                load(i, h // 2).wait()
        for p in range(parts):
            arrived(g, h, p)
        (prepare_new if g else prepare_old)(h)

    handlers = {
        ISSUE: issue, RELAY: relay, CROSS: cross, READY: ready, START: start, SIDE: reduce_beside,
        PART: reduce_relay, END: reduce_end, FINISH: renew,
    }
    def turn_rates():
        turned = rate_ref[...]
        if heads < 8:
            turned = jnp.concatenate([turned, jnp.zeros((8 - heads, tokens), f32)], axis=0)
        rate[...] = turned.T

    order = list(order)
    while order:
        event = order.pop(0)
        if event == (RELAY, 0, 0, 0, 1):
            turn_rates()
        if event[0] != READY:
            handlers[event[0]](*event[1:])
            continue
        ready(*event[1:])
        slots = {}
        for k in range(tokens // (long if event[1] else step)):
            while order[0][0] != STEP:
                kind, *rest = order.pop(0)
                slots.setdefault(k, []).append(functools.partial(handlers[kind], *rest))
            order.pop(0)
        (apply_head if event[1] else grads)(event[2], slots)

    def row_copy(t):
        return pltpu.make_async_remote_copy(
            src_ref=row, dst_ref=rows_in.at[t - 1],
            send_sem=row_send.at[t - 1], recv_sem=row_recv.at[t - 1],
            device_id={"head": lax.rem(mine + t, plan.peers)},
        )

    for t in range(1, plan.peers):
        send(None, functools.partial(row_copy, t))
    total = row[...]
    for t in range(1, plan.peers):
        row_copy(t).wait_recv()
        total = total + rows_in[t - 1]
    row_out[...] = lax.rsqrt(total / plan.width_all + EPS)
    for done in sends:
        done()


def finish_kernel(step, outs_ref, row_ref, gain_ref, fresh_ref, out_hbm, *rest):
    weights, laid, staged, sem, weight_sem = rest[:3], rest[3], rest[4], rest[5], rest[6]
    tokens, width = outs_ref.shape

    def store(i):
        span = pl.ds(i * step, step)
        return pltpu.make_async_copy(staged.at[span], out_hbm.at[span], sem.at[i])

    def lay(j):
        return pltpu.make_async_copy(laid.at[j], weights[j], weight_sem.at[j])

    for i in range(tokens // step):
        span = slice(i * step, (i + 1) * step)
        scale = jnp.broadcast_to(row_ref[:, span], (128, step)).T
        for c in range(0, width, 128):
            cut = slice(c, c + 128)
            staged[span, cut] = (outs_ref[span, cut] * scale * gain_ref[cut][None]).astype(staged.dtype)
        store(i).start()
        if i < len(weights):
            heads = [fresh_ref[i, h].astype(jnp.float32) for h in range(fresh_ref.shape[1])]
            laid[i] = jnp.stack(heads, axis=1).astype(laid.dtype)
            lay(i).start()
    for i in range(tokens // step):
        store(i).wait()
    for j in range(len(weights)):
        lay(j).wait()


def finish(outs, row, gain, fresh):
    rows, width = outs.shape
    units, heads = fresh.shape[2], fresh.shape[1]
    weight = jax.ShapeDtypeStruct((units, heads, fresh.shape[3]), fresh.dtype)
    step = 256
    return pl.pallas_call(
        functools.partial(finish_kernel, step),
        out_shape=(jax.ShapeDtypeStruct(outs.shape, jnp.bfloat16),) + (weight,) * 3,
        in_specs=vmem(4),
        out_specs=(pl.BlockSpec(memory_space=pl.ANY),) * 4,
        scratch_shapes=[
            pltpu.VMEM((3,) + weight.shape, weight.dtype),
            pltpu.VMEM(outs.shape, jnp.bfloat16),
            pltpu.SemaphoreType.DMA((rows // step,)),
            pltpu.SemaphoreType.DMA((3,)),
        ],
        compiler_params=pltpu.CompilerParams(vmem_limit_bytes=32 * 1024 * 1024),
        name="finish_rows",
    )(outs, row, gain, fresh)


def fused(n, peers, width_all, keys, values, queries, rates, w_gate, w_up, w_down):
    rows = keys.shape[0]
    units, heads, width = w_gate.shape
    plan = Plan(n, peers, rows, units, heads, width, width_all)
    f32, b16 = jnp.float32, jnp.bfloat16
    outer = plan.outer
    hbm = pl.BlockSpec(memory_space=pl.ANY)
    block = (units, plan.packed)
    dma = pltpu.SemaphoreType.DMA
    copies = 2 * heads
    return pl.pallas_call(
        functools.partial(fused_kernel, plan),
        out_shape=(
            pltpu.VMEM(keys.shape, f32),
            pltpu.VMEM((1, rows), f32),
            pltpu.VMEM((3, heads, units, width), b16),
        ),
        in_specs=[hbm] * 3 + vmem(4),
        out_specs=tuple(vmem(3)),
        scratch_shapes=[
            pltpu.VMEM(keys.shape, b16),
            pltpu.VMEM(keys.shape, b16),
            pltpu.VMEM((rows, 8), f32),
            pltpu.VMEM((heads, n) + block, b16),
            pltpu.VMEM((heads, n) + block, b16),
            pltpu.VMEM((heads, n) + block, b16),
            pltpu.VMEM((heads, outer, 2) + block, b16),
            pltpu.VMEM((heads, outer, 2) + block, b16),
            pltpu.VMEM((heads, outer) + block, b16),
            pltpu.VMEM((heads,) + block, f32),
            pltpu.VMEM((3, n * units, plan.window), b16),
            pltpu.VMEM((3, n * units, plan.window), f32),
            pltpu.VMEM((3 * heads, plan.window), f32),
            pltpu.VMEM((rows, 128), f32),
            pltpu.VMEM((1, rows), f32),
            pltpu.VMEM((peers - 1, 1, rows), f32),
            dma((3, heads // 2)),
            dma((2, copies, 2, outer)),
            dma((2, copies, outer)),
            dma((2, copies, outer)),
            dma((2, copies, outer)),
            dma((2, copies, 2)),
            dma((2, copies, 2)),
            dma((copies, 2, outer)),
            dma((copies, 2, outer)),
            dma((copies, outer)),
            dma((copies, outer)),
            dma((peers - 1,)),
            dma((peers - 1,)),
        ],
        compiler_params=pltpu.CompilerParams(
            collective_id=2, has_side_effects=True, vmem_limit_bytes=VMEM_LIMIT
        ),
        name="fused_layer",
    )(keys, values, queries, rates.T, w_gate, w_up, w_down)


def per_device(n, peers, width_all, keys, values, queries, rates, w_gate, w_up, w_down, gain):
    rows = keys.shape[0]
    units, heads, width = w_gate.shape
    f32 = jnp.float32
    if fits(n, rows, units, heads, width):
        outs, row, fresh = fused(
            n, peers, width_all, keys, values, queries, rates, w_gate, w_up, w_down
        )
        return finish(outs, row, gain, fresh)
    own = jnp.stack([w_gate, w_up, w_down]).transpose(0, 2, 1, 3)
    own = own.reshape(3 * heads, units, width)
    full = gather(own, n).transpose(1, 3, 0, 2)
    full = full.reshape(3, heads, width, n * units)
    grads = token_grads(keys, values, rates, full)
    block = (n, 3 * heads * width // n, n * units)
    old = lax.dynamic_index_in_dim(full.reshape(block), lax.axis_index("ctx"), 0, keepdims=False)
    fresh = update(grads.reshape(block), old, n).reshape(full.shape)
    mine = lax.dynamic_slice_in_dim(fresh, lax.axis_index("ctx") * units, units, 3)
    mine = mine.transpose(0, 3, 1, 2)
    outs, squares = apply(queries, fresh)
    squares = lax.psum(squares.reshape(rows), "head")
    scale = lax.rsqrt(squares / width_all + EPS)
    output = (outs.astype(f32) * scale[:, None] * gain[None]).astype(jnp.bfloat16)
    return (output, mine[0], mine[1], mine[2])


def solution(mesh):
    weight = P("ctx", "head", None)
    token = P("ctx", "head")

    def whole(keys, *rest):
        body = functools.partial(
            per_device, mesh.shape["ctx"], mesh.shape["head"], keys.shape[1]
        )
        return jax.shard_map(
            body,
            mesh=mesh,
            in_specs=(token,) * 4 + (weight,) * 3 + (P("head"),),
            out_specs=(token, weight, weight, weight),
            check_vma=False,
        )(keys, *rest)

    return whole
```

```python
import functools
import math

import jax
import jax.numpy as jnp
from jax import lax
from jax.experimental import pallas as pl
from jax.experimental.pallas import tpu as pltpu
from jax.sharding import PartitionSpec as P

EPS = 1e-06

VMEM_LIMIT = 50 * 1024 * 1024
STEPS = (1024, 2048)
ISSUE, RELAY, CROSS, READY, STEP, START, SIDE, PART, END, FINISH = range(10)
ORDERS = {
    (4, 4, 2048): (
        ((0, 0), (0, 1), (1, 1), (1, 1)),
        (((0, 1), (0, 1), (0, 1), (0, 1)), ((0, 1), (0, 1), (0, 1), (2, 2))),
        (
            (ISSUE, 0, 0, 0), (ISSUE, 0, 0, 1), (ISSUE, 0, 1, 0), (ISSUE, 0, 1, 1),
            (RELAY, 0, 0, 0, 1), (RELAY, 0, 0, 1, 1), (CROSS, 0, 0, 1), (RELAY, 0, 1, 0, 1),
            (RELAY, 0, 0, 0, 2), (RELAY, 0, 0, 1, 2), (RELAY, 0, 1, 1, 1), (ISSUE, 0, 2, 0),
            (ISSUE, 0, 2, 1), (CROSS, 0, 1, 1), (RELAY, 0, 0, 0, 3), (RELAY, 0, 0, 1, 3),
            (RELAY, 0, 1, 1, 2), (RELAY, 0, 1, 0, 2), (ISSUE, 0, 3, 0), (ISSUE, 0, 3, 1),
            (READY, 0, 0), (RELAY, 0, 2, 0, 1), (STEP, 0, 0, 0), (RELAY, 0, 1, 1, 3),
            (RELAY, 0, 1, 0, 3), (RELAY, 0, 2, 1, 1), (CROSS, 0, 2, 1), (STEP, 0, 0, 1),
            (CROSS, 0, 3, 1), (START, 0), (RELAY, 0, 2, 1, 2), (RELAY, 0, 2, 0, 2),
            (RELAY, 0, 3, 0, 1), (READY, 0, 1), (STEP, 0, 1, 0), (RELAY, 0, 2, 1, 3),
            (RELAY, 0, 2, 0, 3), (STEP, 0, 1, 1), (RELAY, 0, 3, 0, 2), (RELAY, 0, 3, 0, 3),
            (RELAY, 0, 3, 1, 1), (START, 1), (READY, 0, 2), (STEP, 0, 2, 0), (RELAY, 0, 3, 1, 2),
            (RELAY, 0, 3, 1, 3), (PART, 0, 0, 3, 1), (PART, 0, 0, 2, 1), (STEP, 0, 2, 1),
            (START, 2), (PART, 0, 1, 3, 1), (SIDE, 1, 1, 0), (SIDE, 1, 1, 2), (SIDE, 1, 1, 1),
            (PART, 0, 0, 3, 2), (SIDE, 1, 1, 3), (PART, 0, 1, 2, 1), (READY, 0, 3),
            (STEP, 0, 3, 0), (PART, 0, 1, 3, 2), (SIDE, 2, 0, 3), (END, 0, 0), (SIDE, 2, 0, 1),
            (SIDE, 2, 0, 2), (PART, 1, 0, 3, 1), (SIDE, 2, 0, 0), (PART, 1, 0, 2, 1), (END, 0, 1),
            (STEP, 0, 3, 1), (START, 3), (PART, 1, 1, 3, 1), (FINISH, 0, 0), (PART, 1, 1, 2, 1),
            (SIDE, 2, 1, 3), (FINISH, 0, 1), (SIDE, 2, 1, 0), (PART, 1, 0, 3, 2),
            (PART, 2, 0, 3, 1), (PART, 2, 0, 2, 1), (SIDE, 3, 0, 3), (SIDE, 2, 1, 2),
            (PART, 1, 1, 3, 2), (SIDE, 2, 1, 1), (END, 1, 0), (RELAY, 1, 0, 0, 1), (SIDE, 3, 0, 0),
            (END, 1, 1), (FINISH, 1, 1), (SIDE, 3, 0, 2), (RELAY, 1, 0, 1, 1), (SIDE, 3, 1, 3),
            (PART, 2, 0, 3, 2), (SIDE, 3, 0, 1), (END, 2, 0), (FINISH, 2, 0), (PART, 2, 1, 3, 1),
            (PART, 2, 1, 2, 1), (SIDE, 3, 1, 0), (RELAY, 1, 0, 0, 2), (RELAY, 1, 0, 0, 3),
            (SIDE, 3, 1, 1), (RELAY, 1, 0, 1, 2), (RELAY, 1, 0, 1, 3), (PART, 3, 0, 3, 1),
            (RELAY, 1, 1, 1, 1), (FINISH, 1, 0), (PART, 2, 1, 3, 2), (SIDE, 3, 1, 2),
            (CROSS, 1, 0, 1), (END, 2, 1), (FINISH, 2, 1), (PART, 3, 1, 3, 1), (RELAY, 1, 1, 1, 2),
            (PART, 3, 0, 3, 2), (RELAY, 1, 1, 1, 3), (RELAY, 1, 1, 0, 1), (RELAY, 1, 2, 0, 1),
            (PART, 3, 0, 2, 1), (READY, 1, 0), (PART, 3, 1, 3, 2), (RELAY, 1, 2, 1, 1),
            (RELAY, 1, 1, 0, 2), (PART, 3, 1, 2, 1), (CROSS, 1, 1, 1), (RELAY, 1, 2, 0, 2),
            (END, 3, 0), (FINISH, 3, 0), (RELAY, 1, 1, 0, 3), (RELAY, 1, 2, 1, 2), (END, 3, 1),
            (FINISH, 3, 1), (STEP, 1, 0, 0), (RELAY, 1, 2, 0, 3), (READY, 1, 1),
            (RELAY, 1, 3, 0, 1), (RELAY, 1, 3, 0, 2), (CROSS, 1, 2, 1), (RELAY, 1, 2, 1, 3),
            (RELAY, 1, 3, 0, 3), (RELAY, 1, 3, 1, 1), (RELAY, 1, 3, 1, 2), (RELAY, 1, 3, 1, 3),
            (STEP, 1, 1, 0), (READY, 1, 2), (STEP, 1, 2, 0), (READY, 1, 3), (STEP, 1, 3, 0),
        ),
    ),
}


def inner_size(n):
    inner = 1
    while inner * inner * 4 <= n and n % (inner * 2) == 0:
        inner *= 2
    return inner if inner > 1 or n % 2 else 2


def place(n, inner):
    me = lax.axis_index("ctx")
    return me, me // inner, lax.rem(me, inner), n // inner


def greet(z, x, outer, inner):
    barrier = pltpu.get_barrier_semaphore()
    for s in range(1, outer):
        pl.semaphore_signal(barrier, inc=1, device_id={"ctx": lax.rem(z + s, outer) * inner + x})
    for t in range(1, inner):
        pl.semaphore_signal(barrier, inc=1, device_id={"ctx": z * inner + lax.rem(x + t, inner)})
    pl.semaphore_wait(barrier, outer + inner - 2)


def spread(z, x, outer, inner, own_ref, out_ref, send_sem, recv_sem):
    me = z * inner + x
    copies = {}

    def send(src, block, device, s, t):
        copy = pltpu.make_async_remote_copy(
            src_ref=src,
            dst_ref=out_ref.at[block],
            send_sem=send_sem.at[s, t],
            recv_sem=recv_sem.at[s, t],
            device_id={"ctx": device},
        )
        copy.start()
        copies[s, t] = copy

    for s in range(1, outer):
        send(own_ref, me, lax.rem(z + s, outer) * inner + x, s, 0)
    for t in range(1, inner):
        send(own_ref, me, z * inner + lax.rem(x + t, inner), 0, t)
    for s in range(1, outer):
        copies[s, 0].wait_recv()
        block = lax.rem(z + outer - s, outer) * inner + x
        for t in range(1, inner):
            send(out_ref.at[block], block, z * inner + lax.rem(x + t, inner), s, t)
    for (s, t), copy in copies.items():
        if t:
            copy.wait_recv()
    for copy in copies.values():
        copy.wait_send()


def gather_kernel(n, inner, own_ref, out_ref, local_sem, send_sem, recv_sem):
    me, z, x, outer = place(n, inner)
    greet(z, x, outer, inner)
    keep = pltpu.make_async_copy(own_ref, out_ref.at[me], local_sem)
    keep.start()
    spread(z, x, outer, inner, own_ref, out_ref, send_sem, recv_sem)
    keep.wait()


def update_kernel(
    n, inner, grad_ref, old_ref, out_ref, near, part, far, fresh,
    local_sem, near_send, near_recv, far_send, far_recv, send_sem, recv_sem,
):
    me, z, x, outer = place(n, inner)
    greet(z, x, outer, inner)
    order = list(range(1, outer)) + [0]
    first = {}
    for s in order:
        row = lax.rem(z + s, outer) * inner
        for t in range(1, inner):
            column = lax.rem(x + t, inner)
            copy = pltpu.make_async_remote_copy(
                src_ref=grad_ref.at[row + column],
                dst_ref=near.at[s, t - 1],
                send_sem=near_send.at[s, t],
                recv_sem=near_recv.at[s, t],
                device_id={"ctx": z * inner + column},
            )
            copy.start()
            first[s, t] = copy
    second = {}
    total = None
    for s in order:
        row = lax.rem(z + s, outer) * inner
        total = grad_ref[row + x].astype(jnp.float32)
        for t in range(1, inner):
            first[s, t].wait_recv()
            total = total + near[s, t - 1].astype(jnp.float32)
        if s:
            part[s] = total.astype(part.dtype)
            copy = pltpu.make_async_remote_copy(
                src_ref=part.at[s],
                dst_ref=far.at[s],
                send_sem=far_send.at[s],
                recv_sem=far_recv.at[s],
                device_id={"ctx": row + x},
            )
            copy.start()
            second[s] = copy
    for s, copy in second.items():
        copy.wait_recv()
        total = total + far[s].astype(jnp.float32)
    old = old_ref[...].astype(jnp.float32)
    updated = old + total
    old_sq = jnp.sum(old * old, axis=1, keepdims=True)
    new_sq = jnp.sum(updated * updated, axis=1, keepdims=True)
    fresh[...] = (updated * (jnp.sqrt(old_sq) * lax.rsqrt(new_sq + EPS))).astype(fresh.dtype)
    keep = pltpu.make_async_copy(fresh, out_ref.at[me], local_sem)
    keep.start()
    keep.wait()
    spread(z, x, outer, inner, out_ref.at[me], out_ref, send_sem, recv_sem)
    for copy in first.values():
        copy.wait_send()
    for copy in second.values():
        copy.wait_send()


def vmem(count):
    return [pl.BlockSpec(memory_space=pltpu.VMEM)] * count


def gather(own, n):
    inner = inner_size(n)
    outer = n // inner
    return pl.pallas_call(
        functools.partial(gather_kernel, n, inner),
        out_shape=jax.ShapeDtypeStruct((n,) + own.shape, own.dtype),
        in_specs=vmem(1),
        out_specs=vmem(1)[0],
        scratch_shapes=[pltpu.SemaphoreType.DMA]
        + [pltpu.SemaphoreType.DMA((outer, inner))] * 2,
        compiler_params=pltpu.CompilerParams(collective_id=0, has_side_effects=True),
        name="gather_weights",
    )(own)


def update(grads, old, n):
    inner = inner_size(n)
    outer = n // inner
    block = grads.shape[1:]
    return pl.pallas_call(
        functools.partial(update_kernel, n, inner),
        out_shape=jax.ShapeDtypeStruct(grads.shape, grads.dtype),
        in_specs=vmem(2),
        out_specs=vmem(1)[0],
        scratch_shapes=[
            pltpu.VMEM((outer, max(inner - 1, 1)) + block, grads.dtype),
            pltpu.VMEM((outer,) + block, grads.dtype),
            pltpu.VMEM((outer,) + block, grads.dtype),
            pltpu.VMEM(block, grads.dtype),
            pltpu.SemaphoreType.DMA,
        ]
        + [pltpu.SemaphoreType.DMA((outer, inner))] * 2
        + [pltpu.SemaphoreType.DMA((outer,))] * 2
        + [pltpu.SemaphoreType.DMA((outer, inner))] * 2,
        compiler_params=pltpu.CompilerParams(collective_id=1, has_side_effects=True),
        name="update_weights",
    )(grads, old)


def dot(a, b, left, right):
    return lax.dot_general(a, b, (((left,), (right,)), ((), ())), preferred_element_type=jnp.float32)


def grads_kernel(key_ref, value_ref, rate_ref, weight_ref, out_ref, acc):
    step = pl.program_id(0)

    @pl.when(step == 0)
    def _():
        acc[...] = jnp.zeros_like(acc)

    heads, width = weight_ref.shape[1:3]
    for h in range(heads):
        columns = slice(h * width, (h + 1) * width)
        key = key_ref[:, columns]
        gpre = dot(key, weight_ref[0, h], 1, 0)
        upre = dot(key, weight_ref[1, h], 1, 0)
        scaled = (value_ref[:, columns].astype(jnp.float32) * rate_ref[:, h : h + 1]).astype(jnp.bfloat16)
        back = dot(scaled, weight_ref[2, h], 1, 0)
        sig = jax.nn.sigmoid(gpre)
        act = gpre * sig
        slope = sig * (1.0 + gpre * (1.0 - sig))
        acc[0, h] += dot(key, (back * upre * slope).astype(jnp.bfloat16), 0, 0)
        acc[1, h] += dot(key, (back * act).astype(jnp.bfloat16), 0, 0)
        acc[2, h] += dot(scaled, (act * upre).astype(jnp.bfloat16), 0, 0)

    @pl.when(step == pl.num_programs(0) - 1)
    def _():
        out_ref[...] = acc[...].astype(out_ref.dtype)


def apply_kernel(query_ref, weight_ref, out_ref, square_ref):
    heads, width = weight_ref.shape[1:3]
    squares = None
    for h in range(heads):
        columns = slice(h * width, (h + 1) * width)
        query = query_ref[:, columns]
        gate = dot(query, weight_ref[0, h], 1, 0)
        up = dot(query, weight_ref[1, h], 1, 0)
        mixed = (jax.nn.silu(gate) * up).astype(jnp.bfloat16)
        out = dot(mixed, weight_ref[2, h], 1, 1)
        part = jnp.sum(out * out, axis=1, keepdims=True)
        squares = part if squares is None else squares + part
        out_ref[:, columns] = out.astype(out_ref.dtype)
    square_ref[...] = squares


def tile(rows, width):
    return pl.BlockSpec((rows, width), lambda i: (i, 0))


def fixed(shape):
    return pl.BlockSpec(shape, lambda i: (0,) * len(shape))


def token_grads(keys, values, rates, weights):
    rows, width = keys.shape
    step = math.gcd(rows, 512)
    return pl.pallas_call(
        grads_kernel,
        grid=(rows // step,),
        out_shape=jax.ShapeDtypeStruct(weights.shape, jnp.bfloat16),
        in_specs=[tile(step, width), tile(step, width), tile(step, rates.shape[1]), fixed(weights.shape)],
        out_specs=fixed(weights.shape),
        scratch_shapes=[pltpu.VMEM(weights.shape, jnp.float32)],
        name="token_grads",
    )(keys, values, rates, weights)


def apply(queries, weights):
    rows, width = queries.shape
    step = math.gcd(rows, 512)
    return pl.pallas_call(
        apply_kernel,
        grid=(rows // step,),
        out_shape=(
            jax.ShapeDtypeStruct((rows, width), jnp.bfloat16),
            jax.ShapeDtypeStruct((rows, 1), jnp.float32),
        ),
        in_specs=[tile(step, width), fixed(weights.shape)],
        out_specs=(tile(step, width), tile(step, 1)),
        name="apply_weights",
    )(queries, weights)


def fits(n, rows, units, heads, width):
    inner = inner_size(n)
    return (
        inner == 2
        and n // inner >= 2
        and units % 8 == 0
        and heads % 2 == 0
        and heads <= 8
        and width % 128 == 64
        and rows % max(STEPS) == 0
        and rows * heads * width <= 2048 * 1280
        and (n // inner, heads, rows) in ORDERS
    )


class Plan:
    def __init__(self, n, peers, rows, units, heads, width, width_all):
        self.n, self.peers, self.rows, self.units = n, peers, rows, units
        self.heads, self.width, self.width_all = heads, width, width_all
        self.inner = 2
        self.outer = n // 2
        self.step, self.long = STEPS
        self.window = width + 64
        self.packed = 2 * width + self.window
        self.starts = (0, width - 64, 2 * width)
        self.shifts = (0, 64, 0)

    def columns(self, h):
        start = (h // 2) * 2 * self.width + (h % 2) * (self.width - 64)
        return slice(start, start + self.window)

    def move(self, x, old, new):
        size = x.shape[1]
        if old != new:
            x = pltpu.roll(x, (new - old) % size, 1)
        lane = lax.broadcasted_iota(jnp.int32, x.shape, 1)
        return jnp.where((lane >= new) & (lane < new + self.width), x, 0.0)

    def pack(self, gate, up, down):
        first = self.width - 64
        shared = gate[:, first:] + up[:, :128]
        return jnp.concatenate([gate[:, :first], shared, up[:, 128:], down], axis=1)


def fused_kernel(
    plan, key_hbm, value_hbm, query_hbm, rate_ref, gate_ref, up_ref, down_ref,
    outs, row_out, fresh_ref,
    keys, values, rate, old, new, own, ups, downs, side, updated, weights, acc,
    squares_old, squares, row, rows_in,
    load_sem,
    line_send, line_recv, cross_send, cross_recv, pass_send, pass_recv,
    part_send, part_recv, side_send, side_recv, row_send, row_recv,
):
    f32, b16 = jnp.float32, jnp.bfloat16
    n, outer, heads, units, width = plan.n, plan.outer, plan.heads, plan.units, plan.width
    window, step, long, tokens = plan.window, plan.step, plan.long, plan.rows
    me = lax.axis_index("ctx")
    z, x = me // 2, lax.rem(me, 2)
    mine = lax.axis_index("head")
    other = z * 2 + 1 - x

    half = 2 * width

    def load(i, p):
        cut = slice(p * half, (p + 1) * half)
        src, dst = ((key_hbm, keys), (value_hbm, values), (query_hbm, keys))[i]
        return pltpu.make_async_copy(src.at[:, cut], dst.at[:, cut], load_sem.at[i, p])

    for p in range(heads // 2):
        load(0, p).start()
        load(1, p).start()

    barrier = pltpu.get_barrier_semaphore()
    pl.semaphore_signal(barrier, inc=1, device_id={"ctx": other})
    for t in range(1, plan.peers):
        pl.semaphore_signal(barrier, inc=1, device_id={"head": lax.rem(mine + t, plan.peers)})

    for t in range(1, outer):
        pl.semaphore_signal(barrier, inc=1, device_id={"ctx": lax.rem(z + t, outer) * 2 + x})

    def pack_own(h):
        parts = []
        for j, ref in enumerate((gate_ref, up_ref, down_ref)):
            piece = ref[:, h, :].astype(f32)
            piece = jnp.concatenate([piece, jnp.zeros((units, 64), f32)], axis=1)
            parts.append(plan.move(piece, 0, plan.shifts[j]))
        old[h, me] = plan.pack(*parts).astype(b16)

    pack_own(0)
    pl.semaphore_wait(barrier, plan.peers + outer - 1)

    sends = []
    side_first, passing, order = ORDERS[outer, heads, tokens]

    def send(when, make):
        def start():
            make().start()

        def finish():
            make().wait_send()

        if when is None:
            start()
            sends.append(finish)
        else:
            pl.when(when())(start)
            sends.append(lambda: pl.when(when())(finish))

    parts = 2
    share = plan.packed // parts
    lanes = lambda p: slice(p * share, (p + 1) * share)

    def line_copy(g, h, p, origin, up):
        buf = (old, new)[g]
        block = origin * 2 + x
        return pltpu.make_async_remote_copy(
            src_ref=buf.at[h, block, :, lanes(p)], dst_ref=buf.at[h, block, :, lanes(p)],
            send_sem=line_send.at[g, h * parts + p, up, origin], recv_sem=line_recv.at[g, h * parts + p, origin],
            device_id={"ctx": me + (2 if up else -2)},
        )

    def cross_copy(g, h, p, origin):
        buf = (old, new)[g]
        block = origin * 2 + x
        return pltpu.make_async_remote_copy(
            src_ref=buf.at[h, block, :, lanes(p)], dst_ref=buf.at[h, block, :, lanes(p)],
            send_sem=cross_send.at[g, h * parts + p, origin], recv_sem=cross_recv.at[g, h * parts + p, origin],
            device_id={"ctx": other},
        )

    def far_copy(g, h, p, to):
        buf = (old, new)[g]
        return pltpu.make_async_remote_copy(
            src_ref=buf.at[h, me, :, lanes(p)], dst_ref=buf.at[h, me, :, lanes(p)],
            send_sem=line_send.at[g, h * parts + p, 0, to], recv_sem=line_recv.at[g, h * parts + p, z],
            device_id={"ctx": to * 2 + x},
        )

    def issue(g, h, p):
        if g == 0 and h > 0 and p == 0:
            pack_own(h)
        if passing[g][h][p] > 1:
            for d in range(outer - 1, 0, -1):
                send(lambda d=d: z + d < outer, lambda d=d: far_copy(g, h, p, z + d))
                send(lambda d=d: z >= d, lambda d=d: far_copy(g, h, p, z - d))
            send(None, lambda: cross_copy(g, h, p, z))
            return
        send(lambda: z < outer - 1, lambda: line_copy(g, h, p, z, 1))
        send(lambda: z > 0, lambda: line_copy(g, h, p, z, 0))
        send(None, lambda: cross_copy(g, h, p, z))

    def relay(g, h, p, d):
        whole = d > 1 or not passing[g][h][p] & 1
        onward = passing[g][h][p] < 2

        @pl.when(z >= d)
        def _():
            line_copy(g, h, p, z - d, 1).wait_recv()

        if onward:
            send(lambda: (z >= d) & (z < outer - 1), lambda: line_copy(g, h, p, z - d, 1))
        if whole:
            send(lambda: z >= d, lambda: cross_copy(g, h, p, z - d))

        @pl.when(z + d < outer)
        def _():
            line_copy(g, h, p, z + d, 0).wait_recv()

        if onward:
            send(lambda: (z + d < outer) & (z > 0), lambda: line_copy(g, h, p, z + d, 0))
        if whole:
            send(lambda: z + d < outer, lambda: cross_copy(g, h, p, z + d))

    def pass_copy(g, h, p, up):
        buf = (old, new)[g]
        return pltpu.make_async_remote_copy(
            src_ref=buf.at[h, other, :, lanes(p)], dst_ref=buf.at[h, other, :, lanes(p)],
            send_sem=pass_send.at[g, h * parts + p, up], recv_sem=pass_recv.at[g, h * parts + p, up],
            device_id={"ctx": me + (2 if up else -2)},
        )

    def cross(g, h, p):
        cross_copy(g, h, p, z).wait_recv()
        send(lambda: z < outer - 1, lambda: pass_copy(g, h, p, 1))
        send(lambda: z > 0, lambda: pass_copy(g, h, p, 0))

    def arrived(g, h, p):
        if not passing[g][h][p] & 1:
            for o in range(outer):
                cross_copy(g, h, p, o).wait_recv()
            return
        for o in range(outer):
            pl.when((o > z + 1) | (o < z - 1))(lambda: cross_copy(g, h, p, o).wait_recv())
        pl.when(z > 0)(lambda: pass_copy(g, h, p, 1).wait_recv())
        pl.when(z < outer - 1)(lambda: pass_copy(g, h, p, 0).wait_recv())

    def part_copy(h, p, up, to):
        buf = (downs, ups)[up]
        first, count = (to * 2 + x, 1) if side_first[h][p] else (to * 2, 2)
        return pltpu.make_async_remote_copy(
            src_ref=own.at[h, pl.ds(first, count), :, lanes(p)], dst_ref=buf.at[h, to, pl.ds(0, count), :, lanes(p)],
            send_sem=part_send.at[h * parts + p, up, to], recv_sem=part_recv.at[h * parts + p, up, to],
            device_id={"ctx": me + (2 if up else -2)},
        )

    def add_part(h, p, up, to):
        buf = (downs, ups)[up]
        part_copy(h, p, up, to).wait_recv()
        for c in range(1 if side_first[h][p] else 2):
            block = to * 2 + (x if side_first[h][p] else c)
            total = own[h, block, :, lanes(p)].astype(f32) + buf[h, to, c, :, lanes(p)].astype(f32)
            own[h, block, :, lanes(p)] = total.astype(b16)

    def far_part(h, p, to, slot):
        return pltpu.make_async_remote_copy(
            src_ref=own.at[h, to * 2 + x, :, lanes(p)], dst_ref=ups.at[h, slot, 0, :, lanes(p)],
            send_sem=part_send.at[h * parts + p, 0, to], recv_sem=part_recv.at[h * parts + p, 1, slot],
            device_id={"ctx": to * 2 + x},
        )

    def side_copy(h, p, to):
        return pltpu.make_async_remote_copy(
            src_ref=own.at[h, to * 2 + 1 - x, :, lanes(p)], dst_ref=side.at[h, to if side_first[h][p] else 0, :, lanes(p)],
            send_sem=side_send.at[h * parts + p, to], recv_sem=side_recv.at[h * parts + p, to],
            device_id={"ctx": other},
        )

    def reduce_start(h, p):
        if side_first[h][p]:
            for i in range(outer):
                send(None, functools.partial(side_copy, h, p, i // 2 if i % 2 else outer - 1 - i // 2))
            return
        for to in range(outer - 1, 0, -1):
            send(lambda: z == 0, functools.partial(part_copy, h, p, 1, to))
            send(lambda: z == outer - 1, functools.partial(part_copy, h, p, 0, outer - 1 - to))

    def reduce_beside(h, p, to):
        side_copy(h, p, to).wait_recv()
        total = own[h, to * 2 + x, :, lanes(p)].astype(f32) + side[h, to, :, lanes(p)].astype(f32)
        own[h, to * 2 + x, :, lanes(p)] = total.astype(b16)
        if side_first[h][p] > 1:
            send(lambda: z != to, lambda: far_part(h, p, to, z))
            return
        if to > 0:
            send(lambda: z == 0, lambda: part_copy(h, p, 1, to))
        if to < outer - 1:
            send(lambda: z == outer - 1, lambda: part_copy(h, p, 0, to))

    def reduce_relay(h, p, to, d):
        back = outer - 1 - to

        @pl.when(z == d)
        def _():
            add_part(h, p, 1, to)

        send(lambda: z == d, lambda: part_copy(h, p, 1, to))

        @pl.when(z == outer - 1 - d)
        def _():
            add_part(h, p, 0, back)

        send(lambda: z == outer - 1 - d, lambda: part_copy(h, p, 0, back))

    def reduce_end(h, p):
        if side_first[h][p] > 1:
            total = own[h, me, :, lanes(p)].astype(f32)
            for d in range(1, outer):
                source = lax.rem(z + d, outer)
                far_part(h, p, source, source).wait_recv()
                total = total + ups[h, source, 0, :, lanes(p)].astype(f32)
            updated[h, :, lanes(p)] = total
            return

        @pl.when(z > 0)
        def _():
            add_part(h, p, 1, z)

        @pl.when(z < outer - 1)
        def _():
            add_part(h, p, 0, z)

        if not side_first[h][p]:
            send(None, lambda: side_copy(h, p, z))

    def renew(h, p):
        if side_first[h][p] > 1:
            total = updated[h, :, lanes(p)]
        else:
            total = own[h, me, :, lanes(p)].astype(f32)
        total = total + old[h, me, :, lanes(p)].astype(f32)
        if not side_first[h][p]:
            side_copy(h, p, z).wait_recv()
            total = total + side[h, 0, :, lanes(p)].astype(f32)
        updated[h, :, lanes(p)] = total
        new[h, me, :, lanes(p)] = total.astype(b16)
        issue(1, h, p)

    def pieces(g, h, j):
        buf = (old, new)[g]
        start, shift = plan.starts[j], plan.shifts[j]
        for b in range(n):
            piece = buf[h, b, :, start : start + window].astype(f32)
            yield b, plan.move(piece, shift, 64 * (h % 2))

    def prepare_old(h):
        for j in range(3):
            total = jnp.zeros((1, window), f32)
            for b, piece in pieces(0, h, j):
                weights[j, b * units : (b + 1) * units] = piece.astype(b16)
                total = total + jnp.sum(piece * piece, axis=0, keepdims=True)
            squares_old[3 * h + j : 3 * h + j + 1, :] = total

    def prepare_new(h):
        for j in range(3):
            total = jnp.zeros((1, window), f32)
            for b, piece in pieces(1, h, j):
                total = total + jnp.sum(piece * piece, axis=0, keepdims=True)
            scale = jnp.sqrt(squares_old[3 * h + j : 3 * h + j + 1, :]) * lax.rsqrt(total + EPS)
            for b, piece in pieces(1, h, j):
                weights[j, b * units : (b + 1) * units] = (piece * scale).astype(b16)
            start, shift = plan.starts[j], plan.shifts[j]
            exact = plan.move(updated[h, :, start : start + window], shift, 64 * (h % 2)) * scale
            fresh_ref[j, h] = plan.move(exact, 64 * (h % 2), 0)[:, :width].astype(b16)

    def at_steps(i, slots):
        for k, events in sorted(slots.items()):
            @pl.when(i == k)
            def _():
                for event in events:
                    event()

    def grads(h, slots):
        for j in range(3):
            acc[j] = jnp.zeros(acc.shape[1:], f32)
        cut = plan.columns(h)

        def body(i, _):
            at_steps(i, slots)
            span = pl.ds(pl.multiple_of(i * step, step), step)
            key = keys[span, cut]
            scaled = (values[span, cut].astype(f32) * rate[span, h : h + 1]).astype(b16)
            gpre = dot(weights[0], key, 1, 1)
            upre = dot(weights[1], key, 1, 1)
            back = dot(weights[2], scaled, 1, 1)
            sig = jax.nn.sigmoid(gpre)
            act = gpre * sig
            slope = sig * (1.0 + gpre * (1.0 - sig))
            acc[0] += dot((back * upre * slope).astype(b16), key, 1, 0)
            acc[1] += dot((back * act).astype(b16), key, 1, 0)
            acc[2] += dot((act * upre).astype(b16), scaled, 1, 0)
            return 0

        lax.fori_loop(0, tokens // step, body, 0)

    def start(h):
        if h % 2:
            load(2, h // 2).start()
        shift = 64 * (h % 2)
        for b in range(n):
            pieces_of = [
                plan.move(acc[j, b * units : (b + 1) * units], shift, plan.shifts[j]) for j in range(3)
            ]
            own[h, b] = plan.pack(*pieces_of).astype(b16)
        for p in range(parts):
            reduce_start(h, p)

    def apply_head(h, slots):
        cut = plan.columns(h)

        def body(i, _):
            at_steps(i, slots)
            span = pl.ds(pl.multiple_of(i * long, long), long)
            query = keys[span, cut]
            gate = dot(weights[0], query, 1, 1)
            up = dot(weights[1], query, 1, 1)
            mixed = (jax.nn.silu(gate) * up).astype(b16)
            out = dot(mixed, weights[2], 0, 0)
            if h % 2:
                shared = slice(cut.start, cut.start + 128)
                outs[span, shared] = outs[span, shared] + out[:, :128]
                outs[span, cut.start + 128 : cut.stop] = out[:, 128:]
            else:
                outs[span, cut] = out
            part = out * out
            total = part[:, :128]
            for c in range(128, window, 128):
                total = total + part[:, c : c + 128]
            if h > 0:
                total = squares[span, :] + total
            if h < heads - 1:
                squares[span, :] = total
            else:
                row[:, span] = jnp.sum(total.T, axis=0, keepdims=True)
            return 0

        lax.fori_loop(0, tokens // long, body, 0)

    def ready(g, h):
        if h % 2 == 0:
            for i in (2,) if g else (0, 1):
                load(i, h // 2).wait()
        for p in range(parts):
            arrived(g, h, p)
        (prepare_new if g else prepare_old)(h)

    handlers = {
        ISSUE: issue, RELAY: relay, CROSS: cross, READY: ready, START: start, SIDE: reduce_beside,
        PART: reduce_relay, END: reduce_end, FINISH: renew,
    }
    def turn_rates():
        turned = rate_ref[...]
        if heads < 8:
            turned = jnp.concatenate([turned, jnp.zeros((8 - heads, tokens), f32)], axis=0)
        rate[...] = turned.T

    order = list(order)
    while order:
        event = order.pop(0)
        if event == (RELAY, 0, 0, 0, 1):
            turn_rates()
        if event[0] != READY:
            handlers[event[0]](*event[1:])
            continue
        ready(*event[1:])
        slots = {}
        for k in range(tokens // (long if event[1] else step)):
            while order[0][0] != STEP:
                kind, *rest = order.pop(0)
                slots.setdefault(k, []).append(functools.partial(handlers[kind], *rest))
            order.pop(0)
        (apply_head if event[1] else grads)(event[2], slots)

    def row_copy(t):
        return pltpu.make_async_remote_copy(
            src_ref=row, dst_ref=rows_in.at[t - 1],
            send_sem=row_send.at[t - 1], recv_sem=row_recv.at[t - 1],
            device_id={"head": lax.rem(mine + t, plan.peers)},
        )

    for t in range(1, plan.peers):
        send(None, functools.partial(row_copy, t))
    total = row[...]
    for t in range(1, plan.peers):
        row_copy(t).wait_recv()
        total = total + rows_in[t - 1]
    row_out[...] = lax.rsqrt(total / plan.width_all + EPS)
    for done in sends:
        done()


def finish_kernel(step, outs_ref, row_ref, gain_ref, fresh_ref, out_hbm, *rest):
    weights, laid, staged, sem, weight_sem = rest[:3], rest[3], rest[4], rest[5], rest[6]
    tokens, width = outs_ref.shape

    def store(i):
        span = pl.ds(i * step, step)
        return pltpu.make_async_copy(staged.at[span], out_hbm.at[span], sem.at[i])

    def lay(j):
        return pltpu.make_async_copy(laid.at[j], weights[j], weight_sem.at[j])

    for i in range(tokens // step):
        span = slice(i * step, (i + 1) * step)
        scale = jnp.broadcast_to(row_ref[:, span], (128, step)).T
        for c in range(0, width, 128):
            cut = slice(c, c + 128)
            staged[span, cut] = (outs_ref[span, cut] * scale * gain_ref[cut][None]).astype(staged.dtype)
        store(i).start()
        if i < len(weights):
            heads = [fresh_ref[i, h].astype(jnp.float32) for h in range(fresh_ref.shape[1])]
            laid[i] = jnp.stack(heads, axis=1).astype(laid.dtype)
            lay(i).start()
    for i in range(tokens // step):
        store(i).wait()
    for j in range(len(weights)):
        lay(j).wait()


def finish(outs, row, gain, fresh):
    rows, width = outs.shape
    units, heads = fresh.shape[2], fresh.shape[1]
    weight = jax.ShapeDtypeStruct((units, heads, fresh.shape[3]), fresh.dtype)
    step = math.gcd(rows, 128)
    return pl.pallas_call(
        functools.partial(finish_kernel, step),
        out_shape=(jax.ShapeDtypeStruct(outs.shape, jnp.bfloat16),) + (weight,) * 3,
        in_specs=vmem(4),
        out_specs=(pl.BlockSpec(memory_space=pl.ANY),) * 4,
        scratch_shapes=[
            pltpu.VMEM((3,) + weight.shape, weight.dtype),
            pltpu.VMEM(outs.shape, jnp.bfloat16),
            pltpu.SemaphoreType.DMA((rows // step,)),
            pltpu.SemaphoreType.DMA((3,)),
        ],
        compiler_params=pltpu.CompilerParams(vmem_limit_bytes=32 * 1024 * 1024),
        name="finish_rows",
    )(outs, row, gain, fresh)


def fused(n, peers, width_all, keys, values, queries, rates, w_gate, w_up, w_down):
    rows = keys.shape[0]
    units, heads, width = w_gate.shape
    plan = Plan(n, peers, rows, units, heads, width, width_all)
    f32, b16 = jnp.float32, jnp.bfloat16
    outer = plan.outer
    hbm = pl.BlockSpec(memory_space=pl.ANY)
    block = (units, plan.packed)
    dma = pltpu.SemaphoreType.DMA
    copies = 2 * heads
    return pl.pallas_call(
        functools.partial(fused_kernel, plan),
        out_shape=(
            pltpu.VMEM(keys.shape, f32),
            pltpu.VMEM((1, rows), f32),
            pltpu.VMEM((3, heads, units, width), b16),
        ),
        in_specs=[hbm] * 3 + vmem(4),
        out_specs=tuple(vmem(3)),
        scratch_shapes=[
            pltpu.VMEM(keys.shape, b16),
            pltpu.VMEM(keys.shape, b16),
            pltpu.VMEM((rows, 8), f32),
            pltpu.VMEM((heads, n) + block, b16),
            pltpu.VMEM((heads, n) + block, b16),
            pltpu.VMEM((heads, n) + block, b16),
            pltpu.VMEM((heads, outer, 2) + block, b16),
            pltpu.VMEM((heads, outer, 2) + block, b16),
            pltpu.VMEM((heads, outer) + block, b16),
            pltpu.VMEM((heads,) + block, f32),
            pltpu.VMEM((3, n * units, plan.window), b16),
            pltpu.VMEM((3, n * units, plan.window), f32),
            pltpu.VMEM((3 * heads, plan.window), f32),
            pltpu.VMEM((rows, 128), f32),
            pltpu.VMEM((1, rows), f32),
            pltpu.VMEM((peers - 1, 1, rows), f32),
            dma((3, heads // 2)),
            dma((2, copies, 2, outer)),
            dma((2, copies, outer)),
            dma((2, copies, outer)),
            dma((2, copies, outer)),
            dma((2, copies, 2)),
            dma((2, copies, 2)),
            dma((copies, 2, outer)),
            dma((copies, 2, outer)),
            dma((copies, outer)),
            dma((copies, outer)),
            dma((peers - 1,)),
            dma((peers - 1,)),
        ],
        compiler_params=pltpu.CompilerParams(
            collective_id=2, has_side_effects=True, vmem_limit_bytes=VMEM_LIMIT
        ),
        name="fused_layer",
    )(keys, values, queries, rates.T, w_gate, w_up, w_down)


def per_device(n, peers, width_all, keys, values, queries, rates, w_gate, w_up, w_down, gain):
    rows = keys.shape[0]
    units, heads, width = w_gate.shape
    f32 = jnp.float32
    if fits(n, rows, units, heads, width):
        outs, row, fresh = fused(
            n, peers, width_all, keys, values, queries, rates, w_gate, w_up, w_down
        )
        return finish(outs, row, gain, fresh)
    own = jnp.stack([w_gate, w_up, w_down]).transpose(0, 2, 1, 3)
    own = own.reshape(3 * heads, units, width)
    full = gather(own, n).transpose(1, 3, 0, 2)
    full = full.reshape(3, heads, width, n * units)
    grads = token_grads(keys, values, rates, full)
    block = (n, 3 * heads * width // n, n * units)
    old = lax.dynamic_index_in_dim(full.reshape(block), lax.axis_index("ctx"), 0, keepdims=False)
    fresh = update(grads.reshape(block), old, n).reshape(full.shape)
    mine = lax.dynamic_slice_in_dim(fresh, lax.axis_index("ctx") * units, units, 3)
    mine = mine.transpose(0, 3, 1, 2)
    outs, squares = apply(queries, fresh)
    squares = lax.psum(squares.reshape(rows), "head")
    scale = lax.rsqrt(squares / width_all + EPS)
    output = (outs.astype(f32) * scale[:, None] * gain[None]).astype(jnp.bfloat16)
    return (output, mine[0], mine[1], mine[2])


def solution(mesh):
    weight = P("ctx", "head", None)
    token = P("ctx", "head")

    def whole(keys, *rest):
        body = functools.partial(
            per_device, mesh.shape["ctx"], mesh.shape["head"], keys.shape[1]
        )
        return jax.shard_map(
            body,
            mesh=mesh,
            in_specs=(token,) * 4 + (weight,) * 3 + (P("head"),),
            out_specs=(token, weight, weight, weight),
            check_vma=False,
        )(keys, *rest)

    return whole
```
